128 devices in a mesh: dp: 32 (over y_lo, z, x), tensor: 4 (over y_hi, core).
Axes of the slice: x: 4, y: 4 (y_hi: 2, y_lo: 2; y = y_hi * 2 + y_lo), z: 4, core: 2. Of those that a mesh axis runs over, the one named last changes fastest.
Arguments:
- tokens_in: bfloat16 [16384, 2048], P(('dp', 'tensor')), may hold values from -6 to 6
- cotangent: bfloat16 [16384, 2048], P(('dp', 'tensor')), may hold values from -6 to 6
- seq_ids: int32 [16384], P('dp'), may hold values from 0 to 1, as said below
- block_ids: int32 [16384], P('dp'), may hold values from 0 to 1, as said below
- positions: int32 [16384], P('dp'), may hold values from 0 to 383, as said below
- attn_gain: bfloat16 [2048], P('dp'), may hold values from 0.5 to 1.5
- ffn_gain: bfloat16 [2048], P('dp'), may hold values from 0.5 to 1.5
- w_query: bfloat16 [2048, 2048], P('dp', 'tensor'), may hold values from -0.125 to 0.125
- w_key: bfloat16 [2048, 256], P('dp', 'tensor'), may hold values from -0.125 to 0.125
- w_value: bfloat16 [2048, 256], P('dp', 'tensor'), may hold values from -0.125 to 0.125
- w_out: bfloat16 [2048, 2048], P('tensor', 'dp'), may hold values from -1 to 1
- w_gate: bfloat16 [2048, 5632], P('dp', 'tensor'), may hold values from -0.125 to 0.125
- w_up: bfloat16 [2048, 5632], P('dp', 'tensor'), may hold values from -0.125 to 0.125
- w_down: bfloat16 [5632, 2048], P('tensor', 'dp'), may hold values from -0.15625 to 0.15625
Outputs:
- result: bfloat16 [16384, 2048], P(('dp', 'tensor'))
- grad_tokens: bfloat16 [16384, 2048], P(('dp', 'tensor'))
- grad_attn_gain: float32 [2048], P('dp')
- grad_ffn_gain: float32 [2048], P('dp')
- grad_w_query: float32 [2048, 2048], P('dp', 'tensor')
- grad_w_key: float32 [2048, 256], P('dp', 'tensor')
- grad_w_value: float32 [2048, 256], P('dp', 'tensor')
- grad_w_out: float32 [2048, 2048], P('tensor', 'dp')
- grad_w_gate: float32 [2048, 5632], P('dp', 'tensor')
- grad_w_up: float32 [2048, 5632], P('dp', 'tensor')
- grad_w_down: float32 [5632, 2048], P('tensor', 'dp')
The draws below stay inside these ranges and needn't reach their ends.
Inputs may be any that keep to these rules, and one draw needn't show every extreme that they name: `seq_ids`: each run of 512 tokens holds two documents, 0 then 1, each of 128 to 384 tokens; never falls within a run. `positions`: counted from 0 at the start of each document; some document has 384 tokens. `block_ids`: the attention block of the token's place in its document, of 256 places each; some document has 384 tokens.
All inputs are finite; a program needn't handle non-finite values.
Results may differ from the reference program's by a relative error of at most 0.03.
Values may be sent and summed in bfloat16 or wider, within the bound.
A program may use at most 128 MiB of HBM per device.

```python
import math
import jax
import jax.numpy as jnp
from jax import lax

D = 2048
H = 32
KV = 4
HD = 64
FF = 5632
GROUP_TOK = 512
BLOCK = 256
TOKENS = 16384


def documents(key):
    groups = TOKENS // GROUP_TOK
    boundary = jax.random.randint(jax.random.fold_in(key, 11), (groups, 1), GROUP_TOK // 4, 3 * GROUP_TOK // 4 + 1)
    first_row = jnp.arange(groups, dtype=jnp.int32)[:, None] == 0
    boundary = jnp.where(first_row, GROUP_TOK // 4, boundary).astype(jnp.int32)
    column = jnp.arange(GROUP_TOK, dtype=jnp.int32)[None, :]
    second = (column >= boundary).astype(jnp.int32)
    within = column - second * boundary
    return (second.reshape(-1).astype(jnp.int32), within.reshape(-1).astype(jnp.int32))


def draw_seq_ids(key, part):
    return documents(key)[0]


def draw_positions(key, part):
    return documents(key)[1]


def draw_block_ids(key, part):
    return documents(key)[1] // BLOCK


def level_of(rng, extent, split, least, high):
    level, own = 1.0, jax.random.fold_in(rng, 6)
    for dim, blocks in split:
        draws = jnp.exp(jax.random.uniform(jax.random.fold_in(own, dim), (blocks,), jnp.float32, least / len(split), high / len(split)))
        level = level * jnp.repeat(draws, extent[dim] // blocks).reshape([-1 if axis == dim else 1 for axis in range(len(extent))])
    return level


def normal_values(stream_key, extent, width, reach, cuts=(), held_as=jnp.bfloat16):
    gain = level_of(stream_key, extent, cuts, -0.22, 0.18) if cuts else 1.0
    entries = jax.random.normal(stream_key, extent, jnp.float32) * width * gain
    return jnp.minimum(jnp.maximum(entries, -reach), reach).astype(held_as)


def setup_inputs(seed: int = 0) -> dict:
    splits = jax.random.split(jax.random.key(seed), 15)
    return {
        "tokens_in": normal_values(splits[0], (TOKENS, D), 1.0, 6.0, ((0, 128),)),
        "cotangent": normal_values(splits[1], (TOKENS, D), 1.0, 6.0, ((0, 128),)),
        "seq_ids": draw_seq_ids(jax.random.fold_in(splits[14], 71), 0),
        "block_ids": draw_block_ids(jax.random.fold_in(splits[14], 71), 0),
        "positions": draw_positions(jax.random.fold_in(splits[14], 71), 0),
        "attn_gain": jnp.clip(1.0 + 0.1 * jax.random.normal(splits[5], (D,), jnp.float32), 0.5, 1.5).astype(jnp.bfloat16),
        "ffn_gain": jnp.clip(1.0 + 0.1 * jax.random.normal(splits[6], (D,), jnp.float32), 0.5, 1.5).astype(jnp.bfloat16),
        "w_query": normal_values(splits[7], (D, H * HD), D ** -0.5, 0.125, ((0, 32), (1, 4))),
        "w_key": normal_values(splits[8], (D, KV * HD), D ** -0.5, 0.125, ((0, 32), (1, 4))),
        "w_value": normal_values(splits[9], (D, KV * HD), D ** -0.5, 0.125, ((0, 32), (1, 4))),
        "w_out": normal_values(splits[10], (H * HD, D), (HD // 2) ** -0.5, 1.0, ((0, 4), (1, 32))),
        "w_gate": normal_values(splits[11], (D, FF), D ** -0.5, 0.125, ((0, 32), (1, 4))),
        "w_up": normal_values(splits[12], (D, FF), D ** -0.5, 0.125, ((0, 32), (1, 4))),
        "w_down": normal_values(splits[13], (FF, D), (FF // 4) ** -0.5, 0.15625, ((0, 4), (1, 32))),
    }


EPSILON = 1e-05
ROPE_BASE = 10000.0
HIGHEST_PREC = lax.Precision.HIGHEST

@jax.custom_vjp
def low(v):
    return lax.optimization_barrier(v.astype(jnp.bfloat16)).astype(jnp.float32)

@jax.custom_vjp
def low_back(v):
    return v

def low_keep(v):
    return (low(v), None)

def low_pass(kept, grad):
    return (grad,)

def back_keep(v):
    return (v, None)

def back_low(kept, grad):
    return (low(grad),)
low.defvjp(low_keep, low_pass)
low_back.defvjp(back_keep, back_low)

def product(left_op, right_op):
    return jnp.dot(left_op, right_op, precision=HIGHEST_PREC, preferred_element_type=jnp.float32)

def rms_scaled(values, gain_row):
    return values * lax.rsqrt(lax.optimization_barrier(jnp.mean(values * values, -1, keepdims=True)) + EPSILON) * gain_row

def rope_tables(places, head_width):
    half_width = head_width // 2
    inv_freq = 1.0 / ROPE_BASE ** (jnp.arange(half_width, dtype=jnp.float32) * 2.0 / head_width)
    angles = places.astype(jnp.float32)[:, None] * inv_freq[None, :]
    angles = jnp.concatenate([angles, angles], -1)
    return (jnp.cos(angles), jnp.sin(angles))

def rotate(values, cosine, sine_rows):
    half_width = values.shape[-1] // 2
    turned = jnp.concatenate([-values[..., half_width:], values[..., :half_width]], -1)
    return values * cosine[:, None, :] + turned * sine_rows[:, None, :]

def attend_group(package):
    queries, key_rows, value_rows, seq_group, block_group = package
    score_scale = 1.0 / math.sqrt(HD)
    raw_scores = jnp.einsum('tkhd,skd->khts', queries, key_rows, precision=HIGHEST_PREC)
    scores = score_scale * low_back(raw_scores)
    allowed = (seq_group[:, None] == seq_group[None, :]) & (block_group[None, :] <= block_group[:, None])
    masked = jnp.where(allowed, scores, -1e+30)
    row_max = lax.optimization_barrier(jnp.max(masked, -1, keepdims=True))
    exp_terms = jnp.exp(masked - row_max)
    prob_rows = exp_terms / lax.optimization_barrier(jnp.sum(exp_terms, -1, keepdims=True))
    return jnp.einsum('khts,skd->tkhd', low(prob_rows), value_rows, precision=HIGHEST_PREC)

def forward(tokens, attn_gain, ffn_gain, w_query, w_key, w_value, w_out, w_gate, w_up, w_down, seq_ids, block_ids, positions):
    groups = tokens.shape[0] // GROUP_TOK
    attn_normed = low(rms_scaled(tokens, attn_gain))
    cosine, sine_rows = rope_tables(positions, HD)
    queries = low(rotate(low_back(product(attn_normed, w_query)).reshape(-1, H, HD), cosine, sine_rows))
    key_rows = low(rotate(low_back(product(attn_normed, w_key)).reshape(-1, KV, HD), cosine, sine_rows))
    value_rows = low(low_back(product(attn_normed, w_value)))
    package = (queries.reshape(groups, GROUP_TOK, KV, H // KV, HD), key_rows.reshape(groups, GROUP_TOK, KV, HD), value_rows.reshape(groups, GROUP_TOK, KV, HD), seq_ids.reshape(groups, GROUP_TOK), block_ids.reshape(groups, GROUP_TOK))
    mixed_rows = lax.map(jax.checkpoint(attend_group), package)
    attended = low_back(low(mixed_rows.reshape(-1, H * HD)))
    middle = tokens + low_back(product(attended, w_out))
    ffn_normed = low(rms_scaled(middle, ffn_gain))
    gate_pre = low_back(product(ffn_normed, w_gate))
    up_rows = low_back(product(ffn_normed, w_up))
    hidden = low(jax.nn.silu(gate_pre) * up_rows)
    return middle + low_back(product(hidden, w_down))

def reference(tokens_in, cotangent, seq_ids, block_ids, positions, attn_gain, ffn_gain, w_query, w_key, w_value, w_out, w_gate, w_up, w_down):
    floats = tuple((member.astype(jnp.float32) for member in (tokens_in, attn_gain, ffn_gain, w_query, w_key, w_value, w_out, w_gate, w_up, w_down)))

    def closed(*members):
        return forward(*members, seq_ids, block_ids, positions)
    result, pullback = jax.vjp(closed, *floats)
    gradients = pullback(cotangent.astype(jnp.float32))
    return (result.astype(jnp.bfloat16), gradients[0].astype(jnp.bfloat16), gradients[1], gradients[2], gradients[3], gradients[4], gradients[5], gradients[6], gradients[7], gradients[8], gradients[9])
```

```python
import functools
import math

import jax
import jax.numpy as jnp
from jax import lax
from jax.experimental import pallas as pl
from jax.experimental.pallas import tpu as pltpu
from jax.sharding import PartitionSpec as P

HD = 64
EPSILON = 1e-05
ROPE_BASE = 10000.0
MESH = pl.DeviceIdType.MESH
BF = jnp.bfloat16
F32 = jnp.float32
ANY = pl.BlockSpec(memory_space=pl.ANY)
VM = pl.BlockSpec(memory_space=pltpu.VMEM)
FH = 768


class Net:
    def __init__(self, send, recv, loc):
        self.send, self.recv, self.loc = send, recv, loc
        self.n = self.m = 0
        dp, t = lax.axis_index("dp"), lax.axis_index("tensor")
        self.a = lax.div(dp, 16)
        self.z = lax.rem(lax.div(dp, 4), 4)
        self.x = lax.rem(dp, 4)
        self.hi = lax.div(t, 2)
        self.c = lax.rem(t, 2)
        self.t = t
        self.sends = []

    def dev(self, a=None, z=None, x=None, hi=None, c=None):
        a = self.a if a is None else a
        z = self.z if z is None else z
        x = self.x if x is None else x
        hi = self.hi if hi is None else hi
        c = self.c if c is None else c
        return (a * 16 + z * 4 + x, hi * 2 + c)

    def xp(self, s):
        return self.dev(x=lax.rem(self.x + s, 4))

    def zp(self, s):
        return self.dev(z=lax.rem(self.z + s, 4))

    def first(self, s, own):
        k = self.a if own else 1 - self.a
        return self.dev(z=lax.rem(self.z + s * k, 4), x=lax.rem(self.x + s * (1 - k), 4))

    def flip(self, da, dh):
        return self.dev(a=1 - self.a if da else None, hi=1 - self.hi if dh else None)

    def sib(self):
        return self.dev(c=1 - self.c)

    def greet(self, peers):
        bar = pltpu.get_barrier_semaphore()
        for p in peers:
            pl.semaphore_signal(bar, inc=1, device_id=p, device_id_type=MESH)
        pl.semaphore_wait(bar, len(peers))

    def put(self, src, dst, dev):
        i = self.n
        self.n += 1
        cp = pltpu.make_async_remote_copy(
            src_ref=src, dst_ref=dst, send_sem=self.send.at[i], recv_sem=self.recv.at[i],
            device_id=dev, device_id_type=MESH,
        )
        cp.start()
        self.sends.append(cp)
        return cp

    def copy(self, src, dst):
        i = self.m
        self.m += 1
        cp = pltpu.make_async_copy(src, dst, self.loc.at[i])
        cp.start()
        return cp

    def finish(self):
        for cp in self.sends:
            cp.wait_send()


FLIP4 = ((0, 1),)
FLIP8 = ((1, 0), (1, 1), (0, 1))
ORDER = (1, 3, 2)


def sems(n, m):
    return [pltpu.SemaphoreType.DMA((n,)), pltpu.SemaphoreType.DMA((n,)), pltpu.SemaphoreType.DMA((m,))]


def all_peers(net):
    return (
        [net.xp(s) for s in ORDER]
        + [net.zp(s) for s in ORDER]
        + [net.sib()]
        + [net.flip(*f) for f in FLIP8]
    )


def k1_body(tok, cot, wq, wo, wg, wu, wd, gn, tok_all, cot_all, aq, ao, ag, au, ad, an, send, recv, loc):
    net = Net(send, recv, loc)
    a, z, x, t, hi, c = net.a, net.z, net.x, net.t, net.hi, net.c
    net.greet(all_peers(net))
    items = [(gn, an, False), (wq, aq, False), (wo, ao, False), (wg, ag, True), (wu, au, True), (wd, ad, True)]
    state = []
    waits = [net.copy(tok, tok_all.at[t]), net.copy(cot, cot_all.at[a, t])]
    got_t = [net.put(tok, tok_all.at[t], net.flip(0, 1))]
    got_c = []
    tail = [net.put(tok, tok_all.at[t], net.sib()), net.put(cot, cot_all.at[a, t], net.sib())]
    for src, dst, half in items:
        own = src.at[a] if half else src
        other = src.at[1 - a] if half else src
        here = dst.at[a, z, x]
        lc = net.copy(own, here)
        yc = net.put(other, here, net.flip(1, 0))
        st = [net.put(own, here, net.first(s, True)) for s in ORDER]
        state.append((dst, lc, yc, st))
    for f in FLIP8:
        got_c.append(net.put(cot, cot_all.at[a, t], net.flip(*f)))
    more = []
    for dst, lc, yc, st in state:
        yc.wait_recv()
        there = dst.at[1 - a, z, x]
        more.append([net.put(there, there, net.first(s, False)) for s in ORDER])
    for (dst, lc, yc, st), so in zip(state, more):
        lc.wait()
        for cp in st + so:
            cp.wait_recv()
        for s in ORDER:
            tail.append(net.put(dst.at[0, z], dst.at[0, z], net.zp(s)))
            tail.append(net.put(dst.at[1, :, x], dst.at[1, :, x], net.xp(s)))
    got_t[0].wait_recv()
    th = (1 - hi) * 2 + c
    tail.append(net.put(tok_all.at[th], tok_all.at[th], net.sib()))
    for (da, dh), cp in zip(FLIP8, got_c):
        cp.wait_recv()
        at = 1 - a if da else a
        tt = th if dh else t
        tail.append(net.put(cot_all.at[at, tt], cot_all.at[at, tt], net.sib()))
    for w in waits:
        w.wait()
    for cp in tail:
        cp.wait_recv()
    net.finish()


def k1(tok, cot, wq, wo, wg, wu, wd, gn):
    def full(w, half):
        return jax.ShapeDtypeStruct((2, 4, 4) + (w.shape[1:] if half else w.shape), BF)

    rows, d = tok.shape
    return pl.pallas_call(
        k1_body,
        out_shape=[
            jax.ShapeDtypeStruct((4, rows, d), BF),
            jax.ShapeDtypeStruct((2, 4, rows, d), BF),
            full(wq, False), full(wo, False), full(wg, True), full(wu, True), full(wd, True), full(gn, False),
        ],
        in_specs=[ANY] * 8,
        out_specs=[ANY] * 8,
        scratch_shapes=sems(96, 10),
        compiler_params=pltpu.CompilerParams(collective_id=1, has_side_effects=True),
        name="gather_all",
    )(tok, cot, wq, wo, wg, wu, wd, gn)


def rms_unit(u):
    return lax.rsqrt(jnp.mean(u * u, -1, keepdims=True) + EPSILON)


def add_to(dst, terms, rows, step=32):
    @pl.loop(0, rows // step)
    def _(i):
        sl = pl.ds(pl.multiple_of(i * step, step), step)
        total = terms[0][sl, :].astype(F32)
        for ref in terms[1:]:
            total += ref[sl, :].astype(F32)
        dst[sl, :] = total.astype(dst.dtype)


def k2_body(part, tok, gain, out, mid, ploc, rc, rh, send, recv, loc):
    net = Net(send, recv, loc)
    a, t, hi, c = net.a, net.t, net.hi, net.c
    net.greet([net.sib()] + [net.flip(*f) for f in FLIP8])
    rows = tok.shape[0]
    far, near = 1 - hi, hi
    cc = [net.put(part.at[h * 2 + (1 - c)], rc.at[i], net.sib()) for i, h in enumerate((far, near))]
    lc = [net.copy(part.at[h * 2 + c], ploc.at[i]) for i, h in enumerate((far, near))]
    lc[0].wait()
    cc[0].wait_recv()
    add_to(ploc.at[0], [ploc.at[0], rc.at[0]], rows)
    ch = net.put(ploc.at[0], rh, net.flip(0, 1))
    lc[1].wait()
    cc[1].wait_recv()
    ch.wait_recv()
    step = 32

    @pl.loop(0, rows // step)
    def _(i):
        sl = pl.ds(pl.multiple_of(i * step, step), step)
        m = (
            tok[sl, :].astype(F32)
            + (ploc[1, sl, :].astype(F32) + rc[1, sl, :].astype(F32))
            + rh[sl, :].astype(F32)
        )
        mid[sl, :] = m
        out[a, t, sl, :] = (m * rms_unit(m) * gain[...]).astype(BF)

    mine = out.at[a, t]
    got = [net.put(mine, mine, net.flip(*f)) for f in FLIP8]
    tail = [net.put(mine, mine, net.sib())]
    th = far * 2 + c
    for (da, dh), cp in zip(FLIP8, got):
        cp.wait_recv()
        blk = out.at[1 - a if da else a, th if dh else t]
        tail.append(net.put(blk, blk, net.sib()))
    for cp in tail:
        cp.wait_recv()
    net.finish()


def k2(part, tok, gain):
    rows, d = tok.shape
    return pl.pallas_call(
        k2_body,
        out_shape=[jax.ShapeDtypeStruct((2, 4, rows, d), BF), jax.ShapeDtypeStruct((rows, d), F32)],
        in_specs=[ANY, VM, VM],
        out_specs=[VM, VM],
        scratch_shapes=[
            pltpu.VMEM((2, rows, d), BF), pltpu.VMEM((2, rows, d), BF), pltpu.VMEM((rows, d), BF),
        ] + sems(12, 2),
        compiler_params=pltpu.CompilerParams(collective_id=2, has_side_effects=True, vmem_limit_bytes=40 << 20),
        name="sum_norm_gather",
    )(part, tok, gain)


def scatter8_start(net, part, ploc, rc):
    a, hi, c = net.a, net.hi, net.c
    chips = [(1 - a if da else a, 1 - hi if dh else hi) for da, dh in FLIP8 + ((0, 0),)]
    cc = [net.put(part.at[b, h * 2 + (1 - c)], rc.at[i], net.sib()) for i, (b, h) in enumerate(chips)]
    lc = [net.copy(part.at[b, h * 2 + c], ploc.at[i]) for i, (b, h) in enumerate(chips)]
    return cc, lc


def scatter8_send(net, cc, lc, ploc, rc, ry, rows):
    out = []
    for i, f in enumerate(FLIP8):
        lc[i].wait()
        cc[i].wait_recv()
        add_to(ploc.at[i], [ploc.at[i], rc.at[i]], rows)
        out.append(net.put(ploc.at[i], ry.at[i], net.flip(*f)))
    lc[3].wait()
    cc[3].wait_recv()
    return out


def norm_back(u, g, gain):
    r = rms_unit(u)
    unit = u * r
    gvec = g * gain
    return r * (gvec - unit * jnp.mean(gvec * unit, -1, keepdims=True))


def k3_body(part, mid, cot, gain, out, gmid, ploc, rc, ry, send, recv, loc):
    net = Net(send, recv, loc)
    t, hi, c = net.t, net.hi, net.c
    net.greet([net.sib()] + [net.flip(*f) for f in FLIP8])
    rows = cot.shape[0]
    cc, lc = scatter8_start(net, part, ploc, rc)
    for cp in scatter8_send(net, cc, lc, ploc, rc, ry, rows):
        cp.wait_recv()
    step = 32

    @pl.loop(0, rows // step)
    def _(i):
        sl = pl.ds(pl.multiple_of(i * step, step), step)
        g = ploc[3, sl, :].astype(F32) + rc[3, sl, :].astype(F32)
        for j in range(3):
            g += ry[j, sl, :].astype(F32)
        gm = cot[sl, :].astype(F32) + norm_back(mid[sl, :], g, gain[...])
        gmid[sl, :] = gm
        out[t, sl, :] = gm.astype(BF)

    mine = out.at[t]
    got = net.put(mine, mine, net.flip(0, 1))
    tail = [net.put(mine, mine, net.sib())]
    got.wait_recv()
    blk = out.at[(1 - hi) * 2 + c]
    tail.append(net.put(blk, blk, net.sib()))
    for cp in tail:
        cp.wait_recv()
    net.finish()


def k3(part, mid, cot, gain):
    rows, d = cot.shape
    return pl.pallas_call(
        k3_body,
        out_shape=[jax.ShapeDtypeStruct((4, rows, d), BF), jax.ShapeDtypeStruct((rows, d), F32)],
        in_specs=[ANY, VM, VM, VM],
        out_specs=[VM, VM],
        scratch_shapes=[
            pltpu.VMEM((4, rows, d), BF), pltpu.VMEM((4, rows, d), BF), pltpu.VMEM((3, rows, d), BF),
        ] + sems(12, 4),
        compiler_params=pltpu.CompilerParams(collective_id=3, has_side_effects=True, vmem_limit_bytes=40 << 20),
        name="sum_normback_gather",
    )(part, mid, cot, gain)


def k4_body(
    pg, pu, pd, po, pq, fpart, apart, mid, tok, gmid, gain,
    og, ou, od, oo, oq, res, gtok,
    lg, lu, ld, lo, lq, r1g, r1u, r1d, r1o, r1q, r2g, r2u, r2d, r2o, r2q, ryo, ryq,
    ploc, rc, ry, aloc, arc, arh, send, recv, loc,
):
    net = Net(send, recv, loc)
    a, z, x, hi, c = net.a, net.z, net.x, net.hi, net.c
    net.greet(all_peers(net))
    rows = tok.shape[0]
    items = [
        (pg, og, lg, r1g, r2g, None), (pu, ou, lu, r1u, r2u, None), (pd, od, ld, r1d, r2d, None),
        (po, oo, lo, r1o, r2o, ryo), (pq, oq, lq, r1q, r2q, ryq),
    ]
    far, near = 1 - hi, hi
    acc = [net.put(apart.at[h * 2 + (1 - c)], arc.at[i], net.sib()) for i, h in enumerate((far, near))]
    alc = [net.copy(apart.at[h * 2 + c], aloc.at[i]) for i, h in enumerate((far, near))]
    st1 = []
    for p, o, l, r1, r2, _ in items:
        lc = [net.copy(p.at[0, z], l.at[0]), net.copy(p.at[1, :, x], l.at[1])]
        got = [[], []]
        for k, s in enumerate(ORDER):
            zz, xx = lax.rem(z + s, 4), lax.rem(x + s, 4)
            got[0].append(net.put(p.at[0, zz], r1.at[0, k], net.zp(s)))
            got[1].append(net.put(p.at[1, :, xx], r1.at[1, k], net.xp(s)))
        st1.append((lc, got))
    fcc, flc = scatter8_start(net, fpart, ploc, rc)
    alc[0].wait()
    acc[0].wait_recv()
    add_to(aloc.at[0], [aloc.at[0], arc.at[0]], rows)
    ach = net.put(aloc.at[0], arh, net.flip(0, 1))
    fgot = scatter8_send(net, fcc, flc, ploc, rc, ry, rows)
    alc[1].wait()
    acc[1].wait_recv()
    ach.wait_recv()
    step = 32

    @pl.loop(0, rows // step)
    def _(i):
        sl = pl.ds(pl.multiple_of(i * step, step), step)
        g = aloc[1, sl, :].astype(F32) + arc[1, sl, :].astype(F32) + arh[sl, :].astype(F32)
        gtok[sl, :] = (gmid[sl, :] + norm_back(tok[sl, :].astype(F32), g, gain[...])).astype(BF)

    for cp in fgot:
        cp.wait_recv()

    @pl.loop(0, rows // step)
    def _(i):
        sl = pl.ds(pl.multiple_of(i * step, step), step)
        g = ploc[3, sl, :].astype(F32) + rc[3, sl, :].astype(F32)
        for j in range(3):
            g += ry[j, sl, :].astype(F32)
        res[sl, :] = (mid[sl, :] + g).astype(BF)

    st2 = []
    for (p, o, l, r1, r2, _), (lc, got) in zip(items, st1):
        nxt = []
        for h in range(2):
            lc[h].wait()
            for cp in got[h]:
                cp.wait_recv()
            for b in range(4):
                add_to(l.at[h, b], [l.at[h, b]] + [r1.at[h, k, b] for k in range(3)], 64)
            me = x if h == 0 else z
            nxt.append([
                net.put(l.at[h, lax.rem(me + s, 4)], r2.at[h, k], net.xp(s) if h == 0 else net.zp(s))
                for k, s in enumerate(ORDER)
            ])
        st2.append(nxt)
    st3 = []
    for (p, o, l, r1, r2, r3), nxt in zip(items, st2):
        for h in range(2):
            for cp in nxt[h]:
                cp.wait_recv()
            me = x if h == 0 else z
            add_to(r2.at[h, 0], [l.at[h, me]] + [r2.at[h, k] for k in range(3)], 64)
        if r3 is None:
            st3.append(net.put(r2.at[1 - a, 0], o.at[a], net.flip(1, 0)))
            o[a, :, :] = r2[a, 0]
        else:
            st3.append(net.put(r2.at[1 - a, 0], r3, net.flip(1, 0)))
    for (p, o, l, r1, r2, r3), cp in zip(items, st3):
        cp.wait_recv()
        if r3 is not None:
            add_to(o, [r2.at[a, 0], r3], 64)
    net.finish()


def k4(grads, fpart, apart, mid, tok, gmid, gain):
    rows, d = tok.shape
    widths = [g.shape[-1] for g in grads]
    outs = [jax.ShapeDtypeStruct((2, 64, w), BF) for w in widths[:3]]
    outs += [jax.ShapeDtypeStruct((64, w), F32) for w in widths[3:]]
    outs += [jax.ShapeDtypeStruct((rows, d), BF)] * 2
    scratch = [pltpu.VMEM((2, 4, 64, w), BF) for w in widths]
    scratch += [pltpu.VMEM((2, 3, 4, 64, w), BF) for w in widths]
    scratch += [pltpu.VMEM((2, 3, 64, w), BF) for w in widths]
    scratch += [pltpu.VMEM((64, w), BF) for w in widths[3:]]
    scratch += [
        pltpu.VMEM((4, rows, d), BF), pltpu.VMEM((4, rows, d), BF), pltpu.VMEM((3, rows, d), BF),
        pltpu.VMEM((2, rows, d), BF), pltpu.VMEM((2, rows, d), BF), pltpu.VMEM((rows, d), BF),
    ]
    return pl.pallas_call(
        k4_body,
        out_shape=outs,
        in_specs=[ANY] * 7 + [VM] * 4,
        out_specs=[VM] * 7,
        scratch_shapes=scratch + sems(96, 24),
        compiler_params=pltpu.CompilerParams(collective_id=4, has_side_effects=True, vmem_limit_bytes=56 << 20),
        name="scatter_all",
    )(*grads, fpart, apart, mid, tok, gmid, gain)


def rope_tables(places, head_width):
    half_width = head_width // 2
    inv_freq = 1.0 / ROPE_BASE ** (jnp.arange(half_width, dtype=F32) * 2.0 / head_width)
    angles = places.astype(F32)[:, None] * inv_freq[None, :]
    angles = jnp.concatenate([angles, angles], -1)
    return (jnp.cos(angles), jnp.sin(angles))


def rotate(values, cosine, sine_rows):
    half_width = values.shape[-1] // 2
    turned = jnp.concatenate([-values[..., half_width:], values[..., :half_width]], -1)
    return values * cosine[:, None, :] + turned * sine_rows[:, None, :]


def rotate_back(grad_rows, cosine, sine_rows):
    half_width = grad_rows.shape[-1] // 2
    scaled = grad_rows * sine_rows[:, None, :]
    turned = jnp.concatenate([scaled[..., half_width:], -scaled[..., :half_width]], -1)
    return grad_rows * cosine[:, None, :] + turned


def mm(l, r, dims=((1,), (0,))):
    return lax.dot_general(l, r, (dims, ((), ())), preferred_element_type=F32)


NT = ((1,), (1,))
TN = ((0,), (0,))


def ein(eq, l, r):
    return jnp.einsum(eq, l, r, preferred_element_type=F32)


def halves(w):
    w = jnp.pad(w, ((0, 0), (0, 2 * FH - w.shape[1])))
    return jnp.stack([w[:, :FH], w[:, FH:]])


def per_device(
    tokens_in, cotangent, seq_ids, block_ids, positions, attn_gain, ffn_gain,
    w_query, w_key, w_value, w_out, w_gate, w_up, w_down,
):
    rows, d = tokens_in.shape
    n = seq_ids.shape[0]
    ff = w_gate.shape[1]
    hq = w_query.shape[1] // HD
    scale = 1.0 / math.sqrt(HD)
    wq = jnp.concatenate([w_query, w_key, w_value], 1)
    wo = w_out.T
    gn = jnp.pad(jnp.stack([attn_gain, ffn_gain]), ((0, 14), (0, 64)))
    tok, cot, wqkv, wot, wg, wu, wdt, gains = k1(
        tokens_in, cotangent, wq, wo, halves(w_gate), halves(w_up), halves(w_down.T), gn
    )
    tok = tok.reshape(n, d)
    cot = cot.reshape(2 * n, d)
    wqkv = wqkv.reshape(d, -1)
    wot = wot.reshape(d, -1)
    wg, wu, wdt = (w.reshape(d, FH) for w in (wg, wu, wdt))
    gains = gains[..., :2, :64].astype(F32)
    g1 = gains[..., 0, :].reshape(1, d)
    g2 = gains[..., 1, :].reshape(1, d)

    inputs = tok.astype(F32)
    xn = (inputs * rms_unit(inputs) * g1).astype(BF)
    qkv = mm(xn, wqkv)
    cosine, sine = rope_tables(positions, HD)
    q = rotate(qkv[:, : hq * HD].reshape(n, hq, HD), cosine, sine).astype(BF)
    k = rotate(qkv[:, hq * HD : hq * HD + HD].reshape(n, 1, HD), cosine, sine).astype(BF)[:, 0]
    v = qkv[:, hq * HD + HD :].astype(BF)
    allowed = (seq_ids[:, None] == seq_ids[None, :]) & (block_ids[None, :] <= block_ids[:, None])
    s = jnp.where(allowed[None], ein("thd,sd->hts", q, k) * scale, -1e30)
    top = jnp.max(s, -1, keepdims=True)
    e = jnp.exp(s - top)
    total = jnp.sum(e, -1, keepdims=True)
    p = e / total
    plow = p.astype(BF)
    att = ein("hts,sd->thd", plow, v).astype(BF).reshape(n, hq * HD)
    part = mm(att, wot, NT).astype(BF).reshape(4, rows, d)
    xf, mid = k2(part, tokens_in, g2)
    xf = xf.reshape(2 * n, d)
    gate = mm(xf, wg)
    up = mm(xf, wu)
    sig = jax.nn.sigmoid(gate)
    silu = gate * sig
    hid = (silu * up).astype(BF)
    gh = mm(cot, wdt)
    dgate = (gh * up * (sig * (1.0 + gate * (1.0 - sig)))).astype(BF)
    dup = (gh * silu).astype(BF)
    fback = (mm(dgate, wg, NT) + mm(dup, wu, NT)).astype(BF)
    gm_all, gmid = k3(fback.reshape(2, 4, rows, d), mid, cotangent, g2)
    gm_all = gm_all.reshape(n, d)
    fout = mm(hid, wdt, NT).astype(BF)
    pd = mm(cot, hid, TN).astype(BF)
    pg = mm(xf, dgate, TN).astype(BF)
    pu = mm(xf, dup, TN).astype(BF)

    gatt = mm(gm_all, wot).astype(BF)
    po = mm(gm_all, att, TN).astype(BF)
    gatt3 = gatt.reshape(n, hq, HD)
    gp = ein("thd,sd->hts", gatt3, v)
    gv = ein("hts,thd->sd", plow, gatt3).astype(BF)
    inner = jnp.sum(p * gp, -1, keepdims=True)
    graw = (p * (gp - inner) * scale).astype(BF)
    gq = ein("hts,sd->thd", graw, k)
    gk = ein("hts,thd->sd", graw, q)
    dq = rotate_back(gq, cosine, sine).reshape(n, hq * HD).astype(BF)
    dk = rotate_back(gk[:, None], cosine, sine)[:, 0].astype(BF)
    dqkv = jnp.concatenate([dq, dk, gv], 1)
    aback = mm(dqkv, wqkv, NT).astype(BF)
    pq = mm(xn, dqkv, TN).astype(BF)

    grads = [w.reshape(2, 4, 4, 64, w.shape[1]) for w in (pg, pu, pd, po, pq)]
    og, ou, od, oo, oq, res, gtok = k4(
        grads, fout.reshape(2, 4, rows, d), aback.reshape(4, rows, d), mid, tokens_in, gmid, g1
    )

    def join(o):
        return jnp.concatenate([o[0], o[1]], 1)[:, :ff].astype(F32)

    og, ou, od = join(og), join(ou), join(od)
    dg1 = jnp.sum(oq * wq.astype(F32), 1) / attn_gain.astype(F32)
    dg2 = jnp.sum(og * w_gate.astype(F32) + ou * w_up.astype(F32), 1) / ffn_gain.astype(F32)
    dg1, dg2 = lax.psum((dg1, dg2), "tensor")
    nq = hq * HD
    return (
        res, gtok, dg1, dg2, oq[:, :nq], oq[:, nq : nq + HD], oq[:, nq + HD :], oo.T, og, ou, od.T,
    )


def solution(mesh):
    both, dp, cols, rows = P(("dp", "tensor"), None), P("dp"), P("dp", "tensor"), P("tensor", "dp")
    return jax.shard_map(
        per_device,
        mesh=mesh,
        in_specs=(both, both, dp, dp, dp, dp, dp, cols, cols, cols, rows, cols, cols, rows),
        out_specs=(both, both, dp, dp, cols, cols, cols, rows, cols, cols, rows),
        check_vma=False,
    )
```

```python
import functools
import math

import jax
import jax.numpy as jnp
from jax import lax
from jax.experimental import pallas as pl
from jax.experimental.pallas import tpu as pltpu
from jax.sharding import PartitionSpec as P

HD = 64
EPSILON = 1e-05
ROPE_BASE = 10000.0
MESH = pl.DeviceIdType.MESH
BF = jnp.bfloat16
F32 = jnp.float32
ANY = pl.BlockSpec(memory_space=pl.ANY)
VM = pl.BlockSpec(memory_space=pltpu.VMEM)
FH = 768


class Net:
    def __init__(self, send, recv, loc):
        self.send, self.recv, self.loc = send, recv, loc
        self.n = self.m = 0
        dp, t = lax.axis_index("dp"), lax.axis_index("tensor")
        self.a = lax.div(dp, 16)
        self.z = lax.rem(lax.div(dp, 4), 4)
        self.x = lax.rem(dp, 4)
        self.hi = lax.div(t, 2)
        self.c = lax.rem(t, 2)
        self.t = t
        self.sends = []

    def dev(self, a=None, z=None, x=None, hi=None, c=None):
        a = self.a if a is None else a
        z = self.z if z is None else z
        x = self.x if x is None else x
        hi = self.hi if hi is None else hi
        c = self.c if c is None else c
        return (a * 16 + z * 4 + x, hi * 2 + c)

    def xp(self, s):
        return self.dev(x=lax.rem(self.x + s, 4))

    def zp(self, s):
        return self.dev(z=lax.rem(self.z + s, 4))

    def first(self, s, own):
        k = self.a if own else 1 - self.a
        return self.dev(z=lax.rem(self.z + s * k, 4), x=lax.rem(self.x + s * (1 - k), 4))

    def flip(self, da, dh):
        return self.dev(a=1 - self.a if da else None, hi=1 - self.hi if dh else None)

    def sib(self):
        return self.dev(c=1 - self.c)

    def greet(self, peers):
        bar = pltpu.get_barrier_semaphore()
        for p in peers:
            pl.semaphore_signal(bar, inc=1, device_id=p, device_id_type=MESH)
        pl.semaphore_wait(bar, len(peers))

    def put(self, src, dst, dev):
        i = self.n
        self.n += 1
        cp = pltpu.make_async_remote_copy(
            src_ref=src, dst_ref=dst, send_sem=self.send.at[i], recv_sem=self.recv.at[i],
            device_id=dev, device_id_type=MESH,
        )
        cp.start()
        self.sends.append(cp)
        return cp

    def copy(self, src, dst):
        i = self.m
        self.m += 1
        cp = pltpu.make_async_copy(src, dst, self.loc.at[i])
        cp.start()
        return cp

    def finish(self):
        for cp in self.sends:
            cp.wait_send()


FLIP4 = ((0, 1),)
FLIP8 = ((1, 0), (1, 1), (0, 1))
ORDER = (1, 3, 2)


def sems(n, m):
    return [pltpu.SemaphoreType.DMA((n,)), pltpu.SemaphoreType.DMA((n,)), pltpu.SemaphoreType.DMA((m,))]


def all_peers(net):
    return (
        [net.xp(s) for s in ORDER]
        + [net.zp(s) for s in ORDER]
        + [net.sib()]
        + [net.flip(*f) for f in FLIP8]
    )


def rms_unit(u):
    return lax.rsqrt(jnp.mean(u * u, -1, keepdims=True) + EPSILON)


def add_to(dst, terms, rows, step=32):
    @pl.loop(0, rows // step)
    def _(i):
        sl = pl.ds(pl.multiple_of(i * step, step), step)
        total = terms[0][sl, :].astype(F32)
        for ref in terms[1:]:
            total += ref[sl, :].astype(F32)
        dst[sl, :] = total.astype(dst.dtype)


def dot(l, r, dims=((1,), (0,))):
    return lax.dot_general(l, r, (dims, ((), ())), preferred_element_type=F32)


NT = ((1,), (1,))
TN = ((0,), (0,))


def low_half(shape):
    return lax.broadcasted_iota(jnp.int32, shape, 1) < HD


def first_quarter(shape):
    lane = lax.broadcasted_iota(jnp.int32, shape, 1)
    return lax.rem(lane, HD) < HD // 2


def rot(u, cos, sin):
    near = jnp.where(first_quarter(u.shape), pltpu.roll(u, 96, 1), pltpu.roll(u, 32, 1))
    return u * cos + near * sin


def rot_back(w, cos, sin):
    y = w * sin
    near = jnp.where(first_quarter(w.shape), pltpu.roll(y, 96, 1), pltpu.roll(y, 32, 1))
    return w * cos + near


class Gather:
    def __init__(self, net, src, dst, half):
        self.net, self.dst = net, dst
        self.own = src.at[net.a] if half else src
        self.other = src.at[1 - net.a] if half else src
        self.here = dst.at[net.a, net.z, net.x]

    def local(self):
        self.lc = self.net.copy(self.own, self.here)

    def over_y(self):
        self.yc = self.net.put(self.other, self.here, self.net.flip(1, 0))

    def stage_own(self):
        self.st = [self.net.put(self.own, self.here, self.net.first(s, True)) for s in ORDER]

    def stage_other(self):
        net = self.net
        self.yc.wait_recv()
        there = self.dst.at[1 - net.a, net.z, net.x]
        self.st += [net.put(there, there, net.first(s, False)) for s in ORDER]

    def stage_two(self):
        net, dst = self.net, self.dst
        self.lc.wait()
        for cp in self.st:
            cp.wait_recv()
        z, x = net.z, net.x
        self.last = []
        for s in ORDER:
            self.last.append(net.put(dst.at[0, z], dst.at[0, z], net.zp(s)))
            self.last.append(net.put(dst.at[1, :, x], dst.at[1, :, x], net.xp(s)))

    def done(self):
        for cp in self.last:
            cp.wait_recv()


def m1_body(
    tok, cot, wq, wo, wg, wu, wd, gn, cos, sin, seqr, seqc, blkr, blkc,
    xf, mid, xn, q, kv4, att, gains, aq, ao, cot_all, ag, au, ad,
    tall, an, bias, ones2, kvf, part, rc, rh, send, recv, loc,
):
    net = Net(send, recv, loc)
    a, z, x, t, hi, c = net.a, net.z, net.x, net.t, net.hi, net.c
    rows, d = tok.shape
    n = 4 * rows
    net.greet(all_peers(net))
    far, near = 1 - hi, hi
    tt = far * 2 + c
    sib, chip = net.sib(), net.flip(0, 1)
    tl = net.copy(tok, tall.at[t])
    tf = net.put(tok, tall.at[t], chip)
    ts = [net.put(tok, tall.at[t], sib)]
    gg, gq, go = Gather(net, gn, an, False), Gather(net, wq, aq, False), Gather(net, wo, ao, False)
    ffn = [Gather(net, w, o, True) for w, o in ((wg, ag), (wu, au), (wd, ad))]
    for g in (gg, gq, go):
        g.over_y()
        g.local()
        g.stage_own()
    for g in ffn:
        g.local()
    cl = net.copy(cot, cot_all.at[a, t])
    bias[...] = jnp.where(
        (seqc[...] == seqr[...]) & (blkr[...] <= blkc[...]), jnp.float32(0.0), jnp.float32(-1e30)
    )
    for g in (gg, gq, go):
        g.stage_other()
    for g in (gg, gq, go):
        g.stage_two()
    tf.wait_recv()
    ts.append(net.put(tall.at[tt], tall.at[tt], sib))
    cf = [net.put(cot, cot_all.at[a, t], net.flip(*f)) for f in FLIP8]
    cs = [net.put(cot, cot_all.at[a, t], sib)]
    for g in ffn:
        g.over_y()
    tl.wait()
    for cp in ts:
        cp.wait_recv()
    gg.done()
    for i in range(16):
        k = 2 * i
        pair = an[k // 16, k // 4 % 4, k % 4] + an[k // 16, k // 4 % 4, k % 4 + 1]
        gains[:, 128 * i : 128 * i + 128] = pair
    step = 32

    @pl.loop(0, n // step)
    def _(i):
        b = lax.div(i, rows // step)
        u = tall[b, pl.ds(pl.multiple_of(lax.rem(i, rows // step) * step, step), step), :].astype(F32)
        xn[pl.ds(pl.multiple_of(i * step, step), step), :] = (u * rms_unit(u) * gains[0:1, :]).astype(BF)

    gq.done()
    for g in ffn:
        g.stage_own()
    scale = 1.0 / math.sqrt(HD)
    for lo, width in ((0, 256), (256, 256), (512, 128)):
        w = aq[:, :, :, :, lo : lo + width].reshape(d, width)
        val = dot(xn[...], w)
        if lo < 512:
            for i in range(2):
                at = lo + 128 * i
                q[:, at : at + 128] = (rot(val[:, 128 * i : 128 * i + 128], cos[...], sin[...]) * scale).astype(BF)
        else:
            low = low_half(val.shape)
            ke = jnp.where(low, rot(val, cos[...], sin[...]), 0.0)
            vo = jnp.where(low, 0.0, val)
            ve = pltpu.roll(vo, 64, 1)
            kv4[0] = ke.astype(BF)
            kv4[1] = pltpu.roll(ke, 64, 1).astype(BF)
            kv4[2] = ve.astype(BF)
            kv4[3] = vo.astype(BF)
            ones2[0] = jnp.where(low, ve, 1.0).astype(BF)
            ones2[1] = jnp.where(low, 1.0, vo).astype(BF)
    for g in ffn:
        g.stage_other()

    @pl.loop(0, 4)
    def _(j):
        ln = pl.ds(pl.multiple_of(j * 128, 128), 128)
        qp = q[:, ln]
        low = low_half((n, 128))
        o = []
        for h in range(2):
            s = dot(qp, kv4[h], NT) + bias[...]
            e = jnp.exp(s - jnp.max(s, -1, keepdims=True)).astype(BF)
            o.append(dot(e, ones2[h]))
        total = jnp.where(low, pltpu.roll(o[0], 64, 1), pltpu.roll(o[1], 64, 1))
        att[:, ln] = (jnp.where(low, o[0], o[1]) / total).astype(BF)

    go.done()
    for i in range(4):
        w = ao[i // 2, 2 * (i % 2) : 2 * (i % 2) + 2].reshape(512, 512)
        part[:, :, 512 * i : 512 * i + 512] = dot(att[...], w, NT).reshape(4, rows, 512).astype(BF)
    cc = [net.put(part.at[h * 2 + (1 - c)], rc.at[i], sib) for i, h in enumerate((far, near))]
    for g in ffn:
        g.stage_two()
    cc[0].wait_recv()
    pf = part.at[far * 2 + c]
    add_to(pf, [pf, rc.at[0]], rows)
    ch = net.put(pf, rh, chip)
    for (da, dh), cp in zip(FLIP8, cf):
        cp.wait_recv()
        blk = cot_all.at[1 - a if da else a, tt if dh else t]
        cs.append(net.put(blk, blk, sib))
    cc[1].wait_recv()
    ch.wait_recv()
    mine_part = part.at[near * 2 + c]

    @pl.loop(0, rows // step)
    def _(i):
        sl = pl.ds(pl.multiple_of(i * step, step), step)
        m = (
            tall[t, sl, :].astype(F32)
            + (mine_part[sl, :].astype(F32) + rc[1, sl, :].astype(F32))
            + rh[sl, :].astype(F32)
        )
        mid[sl, :] = m
        xf[a, t, sl, :] = (m * rms_unit(m) * gains[1:2, :]).astype(BF)

    mine = xf.at[a, t]
    got = [net.put(mine, mine, net.flip(*f)) for f in FLIP8]
    tail = [net.put(mine, mine, sib)]
    for (da, dh), cp in zip(FLIP8, got):
        cp.wait_recv()
        blk = xf.at[1 - a if da else a, tt if dh else t]
        tail.append(net.put(blk, blk, sib))
    cl.wait()
    for g in ffn:
        g.done()
    for cp in tail + cs:
        cp.wait_recv()
    net.finish()


def m1(tok, cot, wq, wo, wg, wu, wd, gn, cos, sin, seq, blk):
    rows, d = tok.shape
    n = 4 * rows
    sd = jax.ShapeDtypeStruct
    col = lambda v: v.reshape(n, 1)
    row = lambda v: v.reshape(1, n)
    return pl.pallas_call(
        m1_body,
        out_shape=[
            sd((2, 4, rows, d), BF), sd((rows, d), F32), sd((n, d), BF), sd((n, 512), BF), sd((4, n, 128), BF),
            sd((n, 512), BF), sd((8, d), F32), sd((2, 4, 4) + wq.shape, BF), sd((2, 4, 4) + wo.shape, BF),
            sd((2, 4, rows, d), BF),
        ] + [sd((2, 4, 4) + w.shape[1:], BF) for w in (wg, wu, wd)],
        in_specs=[ANY] * 8 + [VM] * 6,
        out_specs=[VM] * 9 + [ANY] * 4,
        scratch_shapes=[
            pltpu.VMEM((4, rows, d), BF), pltpu.VMEM((2, 4, 4, 8, 128), F32), pltpu.VMEM((n, n), F32),
            pltpu.VMEM((2, n, 128), BF), pltpu.VMEM((n, 128), F32), pltpu.VMEM((4, rows, d), BF),
            pltpu.VMEM((2, rows, d), BF), pltpu.VMEM((rows, d), BF),
        ] + sems(110, 12),
        compiler_params=pltpu.CompilerParams(collective_id=1, has_side_effects=True, vmem_limit_bytes=56 << 20),
        name="attention_forward",
    )(tok, cot, wq, wo, wg, wu, wd, gn, cos, sin, row(seq), col(seq), row(blk), col(blk))


def scatter8_start(net, part, ploc, rc):
    a, hi, c = net.a, net.hi, net.c
    chips = [(1 - a if da else a, 1 - hi if dh else hi) for da, dh in FLIP8 + ((0, 0),)]
    cc = [net.put(part.at[b, h * 2 + (1 - c)], rc.at[i], net.sib()) for i, (b, h) in enumerate(chips)]
    lc = [net.copy(part.at[b, h * 2 + c], ploc.at[i]) for i, (b, h) in enumerate(chips)]
    return cc, lc


def scatter8_send(net, cc, lc, ploc, rc, ry, rows):
    out = []
    for i, f in enumerate(FLIP8):
        lc[i].wait()
        cc[i].wait_recv()
        add_to(ploc.at[i], [ploc.at[i], rc.at[i]], rows)
        out.append(net.put(ploc.at[i], ry.at[i], net.flip(*f)))
    lc[3].wait()
    cc[3].wait_recv()
    return out


def norm_back(u, g, gain):
    r = rms_unit(u)
    unit = u * r
    gvec = g * gain
    return r * (gvec - unit * jnp.mean(gvec * unit, -1, keepdims=True))


def k3_body(part, mid, cot, gain, out, gmid, ploc, rc, ry, send, recv, loc):
    net = Net(send, recv, loc)
    t, hi, c = net.t, net.hi, net.c
    net.greet([net.sib()] + [net.flip(*f) for f in FLIP8])
    rows = cot.shape[0]
    cc, lc = scatter8_start(net, part, ploc, rc)
    for cp in scatter8_send(net, cc, lc, ploc, rc, ry, rows):
        cp.wait_recv()
    step = 32

    @pl.loop(0, rows // step)
    def _(i):
        sl = pl.ds(pl.multiple_of(i * step, step), step)
        g = ploc[3, sl, :].astype(F32) + rc[3, sl, :].astype(F32)
        for j in range(3):
            g += ry[j, sl, :].astype(F32)
        gm = cot[sl, :].astype(F32) + norm_back(mid[sl, :], g, gain[...])
        gmid[sl, :] = gm
        out[t, sl, :] = gm.astype(BF)

    mine = out.at[t]
    got = net.put(mine, mine, net.flip(0, 1))
    tail = [net.put(mine, mine, net.sib())]
    got.wait_recv()
    blk = out.at[(1 - hi) * 2 + c]
    tail.append(net.put(blk, blk, net.sib()))
    for cp in tail:
        cp.wait_recv()
    net.finish()


def k3(part, mid, cot, gain):
    rows, d = cot.shape
    return pl.pallas_call(
        k3_body,
        out_shape=[jax.ShapeDtypeStruct((4, rows, d), BF), jax.ShapeDtypeStruct((rows, d), F32)],
        in_specs=[ANY, VM, VM, VM],
        out_specs=[VM, VM],
        scratch_shapes=[
            pltpu.VMEM((4, rows, d), BF), pltpu.VMEM((4, rows, d), BF), pltpu.VMEM((3, rows, d), BF),
        ] + sems(12, 4),
        compiler_params=pltpu.CompilerParams(collective_id=3, has_side_effects=True, vmem_limit_bytes=40 << 20),
        name="sum_normback_gather",
    )(part, mid, cot, gain)


def k4_body(
    pg, pu, pd, po, pq, fpart, apart, mid, tok, gmid, gain,
    og, ou, od, oo, oq, res, gtok,
    lg, lu, ld, lo, lq, r1g, r1u, r1d, r1o, r1q, r2g, r2u, r2d, r2o, r2q, ryo, ryq,
    ploc, rc, ry, aloc, arc, arh, send, recv, loc,
):
    net = Net(send, recv, loc)
    a, z, x, hi, c = net.a, net.z, net.x, net.hi, net.c
    net.greet(all_peers(net))
    rows = tok.shape[0]
    items = [
        (pg, og, lg, r1g, r2g, None), (pu, ou, lu, r1u, r2u, None), (pd, od, ld, r1d, r2d, None),
        (po, oo, lo, r1o, r2o, ryo), (pq, oq, lq, r1q, r2q, ryq),
    ]
    far, near = 1 - hi, hi
    acc = [net.put(apart.at[h * 2 + (1 - c)], arc.at[i], net.sib()) for i, h in enumerate((far, near))]
    alc = [net.copy(apart.at[h * 2 + c], aloc.at[i]) for i, h in enumerate((far, near))]
    st1 = []
    for p, o, l, r1, r2, _ in items:
        lc = [net.copy(p.at[0, z], l.at[0]), net.copy(p.at[1, :, x], l.at[1])]
        got = [[], []]
        for k, s in enumerate(ORDER):
            zz, xx = lax.rem(z + s, 4), lax.rem(x + s, 4)
            got[0].append(net.put(p.at[0, zz], r1.at[0, k], net.zp(s)))
            got[1].append(net.put(p.at[1, :, xx], r1.at[1, k], net.xp(s)))
        st1.append((lc, got))
    fcc, flc = scatter8_start(net, fpart, ploc, rc)
    alc[0].wait()
    acc[0].wait_recv()
    add_to(aloc.at[0], [aloc.at[0], arc.at[0]], rows)
    ach = net.put(aloc.at[0], arh, net.flip(0, 1))
    fgot = scatter8_send(net, fcc, flc, ploc, rc, ry, rows)
    alc[1].wait()
    acc[1].wait_recv()
    ach.wait_recv()
    step = 32

    @pl.loop(0, rows // step)
    def _(i):
        sl = pl.ds(pl.multiple_of(i * step, step), step)
        g = aloc[1, sl, :].astype(F32) + arc[1, sl, :].astype(F32) + arh[sl, :].astype(F32)
        gtok[sl, :] = (gmid[sl, :] + norm_back(tok[sl, :].astype(F32), g, gain[...])).astype(BF)

    for cp in fgot:
        cp.wait_recv()

    @pl.loop(0, rows // step)
    def _(i):
        sl = pl.ds(pl.multiple_of(i * step, step), step)
        g = ploc[3, sl, :].astype(F32) + rc[3, sl, :].astype(F32)
        for j in range(3):
            g += ry[j, sl, :].astype(F32)
        res[sl, :] = (mid[sl, :] + g).astype(BF)

    st2 = []
    for (p, o, l, r1, r2, _), (lc, got) in zip(items, st1):
        nxt = []
        for h in range(2):
            lc[h].wait()
            for cp in got[h]:
                cp.wait_recv()
            for b in range(4):
                add_to(l.at[h, b], [l.at[h, b]] + [r1.at[h, k, b] for k in range(3)], 64)
            me = x if h == 0 else z
            nxt.append([
                net.put(l.at[h, lax.rem(me + s, 4)], r2.at[h, k], net.xp(s) if h == 0 else net.zp(s))
                for k, s in enumerate(ORDER)
            ])
        st2.append(nxt)
    st3 = []
    for (p, o, l, r1, r2, r3), nxt in zip(items, st2):
        for h in range(2):
            for cp in nxt[h]:
                cp.wait_recv()
            me = x if h == 0 else z
            add_to(r2.at[h, 0], [l.at[h, me]] + [r2.at[h, k] for k in range(3)], 64)
        if r3 is None:
            st3.append(net.put(r2.at[1 - a, 0], o.at[a], net.flip(1, 0)))
            o[a, :, :] = r2[a, 0]
        else:
            st3.append(net.put(r2.at[1 - a, 0], r3, net.flip(1, 0)))
    for (p, o, l, r1, r2, r3), cp in zip(items, st3):
        cp.wait_recv()
        if r3 is not None:
            add_to(o, [r2.at[a, 0], r3], 64)
    net.finish()


def k4(grads, fpart, apart, mid, tok, gmid, gain):
    rows, d = tok.shape
    widths = [g.shape[-1] for g in grads]
    outs = [jax.ShapeDtypeStruct((2, 64, w), BF) for w in widths[:3]]
    outs += [jax.ShapeDtypeStruct((64, w), F32) for w in widths[3:]]
    outs += [jax.ShapeDtypeStruct((rows, d), BF)] * 2
    scratch = [pltpu.VMEM((2, 4, 64, w), BF) for w in widths]
    scratch += [pltpu.VMEM((2, 3, 4, 64, w), BF) for w in widths]
    scratch += [pltpu.VMEM((2, 3, 64, w), BF) for w in widths]
    scratch += [pltpu.VMEM((64, w), BF) for w in widths[3:]]
    scratch += [
        pltpu.VMEM((4, rows, d), BF), pltpu.VMEM((4, rows, d), BF), pltpu.VMEM((3, rows, d), BF),
        pltpu.VMEM((2, rows, d), BF), pltpu.VMEM((2, rows, d), BF), pltpu.VMEM((rows, d), BF),
    ]
    return pl.pallas_call(
        k4_body,
        out_shape=outs,
        in_specs=[ANY] * 7 + [VM] * 4,
        out_specs=[VM] * 7,
        scratch_shapes=scratch + sems(96, 24),
        compiler_params=pltpu.CompilerParams(collective_id=4, has_side_effects=True, vmem_limit_bytes=56 << 20),
        name="scatter_all",
    )(*grads, fpart, apart, mid, tok, gmid, gain)


def rope_tables(places, head_width):
    half_width = head_width // 2
    inv_freq = 1.0 / ROPE_BASE ** (jnp.arange(half_width, dtype=F32) * 2.0 / head_width)
    angles = places.astype(F32)[:, None] * inv_freq[None, :]
    angles = jnp.concatenate([angles, angles], -1)
    return (jnp.cos(angles), jnp.sin(angles))


def rotate(values, cosine, sine_rows):
    half_width = values.shape[-1] // 2
    turned = jnp.concatenate([-values[..., half_width:], values[..., :half_width]], -1)
    return values * cosine[:, None, :] + turned * sine_rows[:, None, :]


def rotate_back(grad_rows, cosine, sine_rows):
    half_width = grad_rows.shape[-1] // 2
    scaled = grad_rows * sine_rows[:, None, :]
    turned = jnp.concatenate([scaled[..., half_width:], -scaled[..., :half_width]], -1)
    return grad_rows * cosine[:, None, :] + turned


def mm(l, r, dims=((1,), (0,))):
    return lax.dot_general(l, r, (dims, ((), ())), preferred_element_type=F32)


def ein(eq, l, r):
    return jnp.einsum(eq, l, r, preferred_element_type=F32)


def halves(w):
    w = jnp.pad(w, ((0, 0), (0, 2 * FH - w.shape[1])))
    return jnp.stack([w[:, :FH], w[:, FH:]])


def per_device(
    tokens_in, cotangent, seq_ids, block_ids, positions, attn_gain, ffn_gain,
    w_query, w_key, w_value, w_out, w_gate, w_up, w_down,
):
    rows, d = tokens_in.shape
    n = seq_ids.shape[0]
    ff = w_gate.shape[1]
    hq = w_query.shape[1] // HD
    scale = 1.0 / math.sqrt(HD)
    wq = jnp.concatenate([w_query, w_key, w_value], 1)
    wo = w_out.T
    gn = jnp.pad(jnp.stack([attn_gain, ffn_gain]).astype(F32), ((0, 6), (0, 64)))
    gn = jnp.where(lax.rem(lax.axis_index("dp"), 2) == 0, gn, jnp.roll(gn, 64, 1))
    cosine, sine = rope_tables(positions, HD)
    half = HD // 2
    signed = jnp.concatenate([-sine[:, :half], sine[:, half:]], -1)
    cos2, sin2 = jnp.concatenate([cosine] * 2, -1), jnp.concatenate([signed] * 2, -1)
    xf, mid, xn, q, kv4, att, gains, wqkv, wot, cot, wg, wu, wdt = m1(
        tokens_in, cotangent, wq, wo, halves(w_gate), halves(w_up), halves(w_down.T), gn,
        cos2, sin2, seq_ids, block_ids,
    )
    cot = cot.reshape(2 * n, d)
    wqkv = wqkv.reshape(d, -1)
    wot = wot.reshape(d, -1)
    wg, wu, wdt = (w.reshape(d, FH) for w in (wg, wu, wdt))
    g1, g2 = gains[0:1], gains[1:2]
    k, v = kv4[0, :, :HD], kv4[2, :, :HD]
    q = (q * 8).reshape(n, hq, HD)
    allowed = (seq_ids[:, None] == seq_ids[None, :]) & (block_ids[None, :] <= block_ids[:, None])
    s = jnp.where(allowed[None], ein("thd,sd->hts", q, k) * scale, -1e30)
    top = jnp.max(s, -1, keepdims=True)
    e = jnp.exp(s - top)
    total = jnp.sum(e, -1, keepdims=True)
    p = e / total
    plow = p.astype(BF)
    xf = xf.reshape(2 * n, d)
    gate = mm(xf, wg)
    up = mm(xf, wu)
    sig = jax.nn.sigmoid(gate)
    silu = gate * sig
    hid = (silu * up).astype(BF)
    gh = mm(cot, wdt)
    dgate = (gh * up * (sig * (1.0 + gate * (1.0 - sig)))).astype(BF)
    dup = (gh * silu).astype(BF)
    fback = (mm(dgate, wg, NT) + mm(dup, wu, NT)).astype(BF)
    gm_all, gmid = k3(fback.reshape(2, 4, rows, d), mid, cotangent, g2)
    gm_all = gm_all.reshape(n, d)
    fout = mm(hid, wdt, NT).astype(BF)
    pd = mm(cot, hid, TN).astype(BF)
    pg = mm(xf, dgate, TN).astype(BF)
    pu = mm(xf, dup, TN).astype(BF)

    gatt = mm(gm_all, wot).astype(BF)
    po = mm(gm_all, att, TN).astype(BF)
    gatt3 = gatt.reshape(n, hq, HD)
    gp = ein("thd,sd->hts", gatt3, v)
    gv = ein("hts,thd->sd", plow, gatt3).astype(BF)
    inner = jnp.sum(p * gp, -1, keepdims=True)
    graw = (p * (gp - inner) * scale).astype(BF)
    gq = ein("hts,sd->thd", graw, k)
    gk = ein("hts,thd->sd", graw, q)
    dq = rotate_back(gq, cosine, sine).reshape(n, hq * HD).astype(BF)
    dk = rotate_back(gk[:, None], cosine, sine)[:, 0].astype(BF)
    dqkv = jnp.concatenate([dq, dk, gv], 1)
    aback = mm(dqkv, wqkv, NT).astype(BF)
    pq = mm(xn, dqkv, TN).astype(BF)

    grads = [w.reshape(2, 4, 4, 64, w.shape[1]) for w in (pg, pu, pd, po, pq)]
    og, ou, od, oo, oq, res, gtok = k4(
        grads, fout.reshape(2, 4, rows, d), aback.reshape(4, rows, d), mid, tokens_in, gmid, g1
    )

    def join(o):
        return jnp.concatenate([o[0], o[1]], 1)[:, :ff].astype(F32)

    og, ou, od = join(og), join(ou), join(od)
    dg1 = jnp.sum(oq * wq.astype(F32), 1) / attn_gain.astype(F32)
    dg2 = jnp.sum(og * w_gate.astype(F32) + ou * w_up.astype(F32), 1) / ffn_gain.astype(F32)
    dg1, dg2 = lax.psum((dg1, dg2), "tensor")
    nq = hq * HD
    return (
        res, gtok, dg1, dg2, oq[:, :nq], oq[:, nq : nq + HD], oq[:, nq + HD :], oo.T, og, ou, od.T,
    )


def solution(mesh):
    both, dp, cols, rows = P(("dp", "tensor"), None), P("dp"), P("dp", "tensor"), P("tensor", "dp")
    return jax.shard_map(
        per_device,
        mesh=mesh,
        in_specs=(both, both, dp, dp, dp, dp, dp, cols, cols, cols, rows, cols, cols, rows),
        out_specs=(both, both, dp, dp, cols, cols, cols, rows, cols, cols, rows),
        check_vma=False,
    )
```

```python
import functools
import math

import jax
import jax.numpy as jnp
from jax import lax
from jax.experimental import pallas as pl
from jax.experimental.pallas import tpu as pltpu
from jax.sharding import PartitionSpec as P

HD = 64
EPSILON = 1e-05
ROPE_BASE = 10000.0
MESH = pl.DeviceIdType.MESH
BF = jnp.bfloat16
F32 = jnp.float32
ANY = pl.BlockSpec(memory_space=pl.ANY)
VM = pl.BlockSpec(memory_space=pltpu.VMEM)
FH = 768


class Net:
    def __init__(self, send, recv, loc):
        self.send, self.recv, self.loc = send, recv, loc
        self.n = self.m = 0
        dp, t = lax.axis_index("dp"), lax.axis_index("tensor")
        self.a = lax.div(dp, 16)
        self.z = lax.rem(lax.div(dp, 4), 4)
        self.x = lax.rem(dp, 4)
        self.hi = lax.div(t, 2)
        self.c = lax.rem(t, 2)
        self.t = t
        self.sends = []

    def dev(self, a=None, z=None, x=None, hi=None, c=None):
        a = self.a if a is None else a
        z = self.z if z is None else z
        x = self.x if x is None else x
        hi = self.hi if hi is None else hi
        c = self.c if c is None else c
        return (a * 16 + z * 4 + x, hi * 2 + c)

    def xp(self, s):
        return self.dev(x=lax.rem(self.x + s, 4))

    def zp(self, s):
        return self.dev(z=lax.rem(self.z + s, 4))

    def first(self, s, own):
        k = self.a if own else 1 - self.a
        return self.dev(z=lax.rem(self.z + s * k, 4), x=lax.rem(self.x + s * (1 - k), 4))

    def flip(self, da, dh):
        return self.dev(a=1 - self.a if da else None, hi=1 - self.hi if dh else None)

    def sib(self):
        return self.dev(c=1 - self.c)

    def greet(self, peers):
        bar = pltpu.get_barrier_semaphore()
        for p in peers:
            pl.semaphore_signal(bar, inc=1, device_id=p, device_id_type=MESH)
        pl.semaphore_wait(bar, len(peers))

    def put(self, src, dst, dev):
        i = self.n
        self.n += 1
        cp = pltpu.make_async_remote_copy(
            src_ref=src, dst_ref=dst, send_sem=self.send.at[i], recv_sem=self.recv.at[i],
            device_id=dev, device_id_type=MESH,
        )
        cp.start()
        self.sends.append(cp)
        return cp

    def copy(self, src, dst):
        i = self.m
        self.m += 1
        cp = pltpu.make_async_copy(src, dst, self.loc.at[i])
        cp.start()
        return cp

    def finish(self):
        for cp in self.sends:
            cp.wait_send()


FLIP4 = ((0, 1),)
FLIP8 = ((1, 0), (1, 1), (0, 1))
ORDER = (1, 3, 2)


def sems(n, m):
    return [pltpu.SemaphoreType.DMA((n,)), pltpu.SemaphoreType.DMA((n,)), pltpu.SemaphoreType.DMA((m,))]


def all_peers(net):
    return (
        [net.xp(s) for s in ORDER]
        + [net.zp(s) for s in ORDER]
        + [net.sib()]
        + [net.flip(*f) for f in FLIP8]
    )


def rms_unit(u):
    return lax.rsqrt(jnp.mean(u * u, -1, keepdims=True) + EPSILON)


def add_to(dst, terms, rows, step=32):
    @pl.loop(0, rows // step)
    def _(i):
        sl = pl.ds(pl.multiple_of(i * step, step), step)
        total = terms[0][sl, :].astype(F32)
        for ref in terms[1:]:
            total += ref[sl, :].astype(F32)
        dst[sl, :] = total.astype(dst.dtype)


def dot(l, r, dims=((1,), (0,))):
    return lax.dot_general(l, r, (dims, ((), ())), preferred_element_type=F32)


NT = ((1,), (1,))
TN = ((0,), (0,))


def low_half(shape):
    return lax.broadcasted_iota(jnp.int32, shape, 1) < HD


def first_quarter(shape):
    lane = lax.broadcasted_iota(jnp.int32, shape, 1)
    return lax.rem(lane, HD) < HD // 2


def rot(u, cos, sin):
    near = jnp.where(first_quarter(u.shape), pltpu.roll(u, 96, 1), pltpu.roll(u, 32, 1))
    return u * cos + near * sin


def rot_back(w, cos, sin):
    y = w * sin
    near = jnp.where(first_quarter(w.shape), pltpu.roll(y, 96, 1), pltpu.roll(y, 32, 1))
    return w * cos + near


class Gather:
    def __init__(self, net, src, dst, half):
        self.net, self.dst = net, dst
        self.own = src.at[net.a] if half else src
        self.other = src.at[1 - net.a] if half else src
        self.here = dst.at[net.a, net.z, net.x]

    def local(self):
        self.lc = self.net.copy(self.own, self.here)

    def over_y(self):
        self.yc = self.net.put(self.other, self.here, self.net.flip(1, 0))

    def stage_own(self):
        self.st = [self.net.put(self.own, self.here, self.net.first(s, True)) for s in ORDER]

    def stage_other(self):
        net = self.net
        self.yc.wait_recv()
        there = self.dst.at[1 - net.a, net.z, net.x]
        self.st += [net.put(there, there, net.first(s, False)) for s in ORDER]

    def stage_two(self):
        net, dst = self.net, self.dst
        self.lc.wait()
        for cp in self.st:
            cp.wait_recv()
        z, x = net.z, net.x
        self.last = []
        for s in ORDER:
            self.last.append(net.put(dst.at[0, z], dst.at[0, z], net.zp(s)))
            self.last.append(net.put(dst.at[1, :, x], dst.at[1, :, x], net.xp(s)))

    def done(self):
        for cp in self.last:
            cp.wait_recv()


def m1_body(
    tok, cot, wq, wo, wg, wu, wd, gn, cos, sin, seqr, seqc, blkr, blkc,
    xf, mid, xn, q, kv4, att, gains, aq, ao, cot_all, ag, au, ad,
    tall, an, bias, ones2, kvf, part, rc, rh, send, recv, loc,
):
    net = Net(send, recv, loc)
    a, z, x, t, hi, c = net.a, net.z, net.x, net.t, net.hi, net.c
    rows, d = tok.shape
    n = 4 * rows
    net.greet(all_peers(net))
    far, near = 1 - hi, hi
    tt = far * 2 + c
    sib, chip = net.sib(), net.flip(0, 1)
    tl = net.copy(tok, tall.at[t])
    tf = net.put(tok, tall.at[t], chip)
    ts = [net.put(tok, tall.at[t], sib)]
    gg, gq, go = Gather(net, gn, an, False), Gather(net, wq, aq, False), Gather(net, wo, ao, False)
    ffn = [Gather(net, w, o, True) for w, o in ((wg, ag), (wu, au), (wd, ad))]
    for g in (gg, gq, go):
        g.over_y()
        g.local()
        g.stage_own()
    for g in ffn:
        g.local()
    cl = net.copy(cot, cot_all.at[a, t])
    bias[...] = jnp.where(
        (seqc[...] == seqr[...]) & (blkr[...] <= blkc[...]), jnp.float32(0.0), jnp.float32(-1e30)
    )
    for g in (gg, gq, go):
        g.stage_other()
    for g in (gg, gq, go):
        g.stage_two()
    tf.wait_recv()
    ts.append(net.put(tall.at[tt], tall.at[tt], sib))
    cf = [net.put(cot, cot_all.at[a, t], net.flip(*f)) for f in FLIP8]
    cs = [net.put(cot, cot_all.at[a, t], sib)]
    for g in ffn:
        g.over_y()
    tl.wait()
    for cp in ts:
        cp.wait_recv()
    gg.done()
    for i in range(16):
        k = 2 * i
        pair = an[k // 16, k // 4 % 4, k % 4] + an[k // 16, k // 4 % 4, k % 4 + 1]
        gains[:, 128 * i : 128 * i + 128] = pair
    step = 32

    @pl.loop(0, n // step)
    def _(i):
        b = lax.div(i, rows // step)
        u = tall[b, pl.ds(pl.multiple_of(lax.rem(i, rows // step) * step, step), step), :].astype(F32)
        xn[pl.ds(pl.multiple_of(i * step, step), step), :] = (u * rms_unit(u) * gains[0:1, :]).astype(BF)

    gq.done()
    for g in ffn:
        g.stage_own()
    scale = 1.0 / math.sqrt(HD)
    for lo, width in ((0, 256), (256, 256), (512, 128)):
        w = aq[:, :, :, :, lo : lo + width].reshape(d, width)
        val = dot(xn[...], w)
        if lo < 512:
            for i in range(2):
                at = lo + 128 * i
                q[:, at : at + 128] = (rot(val[:, 128 * i : 128 * i + 128], cos[...], sin[...]) * scale).astype(BF)
        else:
            low = low_half(val.shape)
            ke = jnp.where(low, rot(val, cos[...], sin[...]), 0.0)
            vo = jnp.where(low, 0.0, val)
            ve = pltpu.roll(vo, 64, 1)
            kv4[0] = ke.astype(BF)
            kv4[1] = pltpu.roll(ke, 64, 1).astype(BF)
            kv4[2] = ve.astype(BF)
            kv4[3] = vo.astype(BF)
            ones2[0] = jnp.where(low, ve, 1.0).astype(BF)
            ones2[1] = jnp.where(low, 1.0, vo).astype(BF)
    for g in ffn:
        g.stage_other()

    @pl.loop(0, 4)
    def _(j):
        ln = pl.ds(pl.multiple_of(j * 128, 128), 128)
        qp = q[:, ln]
        low = low_half((n, 128))
        o = []
        for h in range(2):
            s = dot(qp, kv4[h], NT) + bias[...]
            e = jnp.exp(s - jnp.max(s, -1, keepdims=True)).astype(BF)
            o.append(dot(e, ones2[h]))
        total = jnp.where(low, pltpu.roll(o[0], 64, 1), pltpu.roll(o[1], 64, 1))
        att[:, ln] = (jnp.where(low, o[0], o[1]) / total).astype(BF)

    go.done()
    for i in range(4):
        w = ao[i // 2, 2 * (i % 2) : 2 * (i % 2) + 2].reshape(512, 512)
        part[:, :, 512 * i : 512 * i + 512] = dot(att[...], w, NT).reshape(4, rows, 512).astype(BF)
    cc = [net.put(part.at[h * 2 + (1 - c)], rc.at[i], sib) for i, h in enumerate((far, near))]
    for g in ffn:
        g.stage_two()
    cc[0].wait_recv()
    pf = part.at[far * 2 + c]
    add_to(pf, [pf, rc.at[0]], rows)
    ch = net.put(pf, rh, chip)
    for (da, dh), cp in zip(FLIP8, cf):
        cp.wait_recv()
        blk = cot_all.at[1 - a if da else a, tt if dh else t]
        cs.append(net.put(blk, blk, sib))
    cc[1].wait_recv()
    ch.wait_recv()
    mine_part = part.at[near * 2 + c]

    @pl.loop(0, rows // step)
    def _(i):
        sl = pl.ds(pl.multiple_of(i * step, step), step)
        m = (
            tall[t, sl, :].astype(F32)
            + (mine_part[sl, :].astype(F32) + rc[1, sl, :].astype(F32))
            + rh[sl, :].astype(F32)
        )
        mid[sl, :] = m
        xf[a, t, sl, :] = (m * rms_unit(m) * gains[1:2, :]).astype(BF)

    mine = xf.at[a, t]
    got = [net.put(mine, mine, net.flip(*f)) for f in FLIP8]
    tail = [net.put(mine, mine, sib)]
    for (da, dh), cp in zip(FLIP8, got):
        cp.wait_recv()
        blk = xf.at[1 - a if da else a, tt if dh else t]
        tail.append(net.put(blk, blk, sib))
    cl.wait()
    for g in ffn:
        g.done()
    for cp in tail + cs:
        cp.wait_recv()
    net.finish()


def m1(tok, cot, wq, wo, wg, wu, wd, gn, cos, sin, seq, blk):
    rows, d = tok.shape
    n = 4 * rows
    sd = jax.ShapeDtypeStruct
    col = lambda v: v.reshape(n, 1)
    row = lambda v: v.reshape(1, n)
    return pl.pallas_call(
        m1_body,
        out_shape=[
            sd((2, 4, rows, d), BF), sd((rows, d), F32), sd((n, d), BF), sd((n, 512), BF), sd((4, n, 128), BF),
            sd((n, 512), BF), sd((8, d), F32), sd((2, 4, 4) + wq.shape, BF), sd((2, 4, 4) + wo.shape, BF),
            sd((2, 4, rows, d), BF),
        ] + [sd((2, 4, 4) + w.shape[1:], BF) for w in (wg, wu, wd)],
        in_specs=[ANY] * 8 + [VM] * 6,
        out_specs=[VM] * 9 + [ANY] * 4,
        scratch_shapes=[
            pltpu.VMEM((4, rows, d), BF), pltpu.VMEM((2, 4, 4, 8, 128), F32), pltpu.VMEM((n, n), F32),
            pltpu.VMEM((2, n, 128), BF), pltpu.VMEM((n, 128), F32), pltpu.VMEM((4, rows, d), BF),
            pltpu.VMEM((2, rows, d), BF), pltpu.VMEM((rows, d), BF),
        ] + sems(110, 12),
        compiler_params=pltpu.CompilerParams(collective_id=1, has_side_effects=True, vmem_limit_bytes=56 << 20),
        name="attention_forward",
    )(tok, cot, wq, wo, wg, wu, wd, gn, cos, sin, row(seq), col(seq), row(blk), col(blk))


def scatter8_start(net, part, ploc, rc):
    a, hi, c = net.a, net.hi, net.c
    chips = [(1 - a if da else a, 1 - hi if dh else hi) for da, dh in FLIP8 + ((0, 0),)]
    cc = [net.put(part.at[b, h * 2 + (1 - c)], rc.at[i], net.sib()) for i, (b, h) in enumerate(chips)]
    lc = [net.copy(part.at[b, h * 2 + c], ploc.at[i]) for i, (b, h) in enumerate(chips)]
    return cc, lc


def scatter8_send(net, cc, lc, ploc, rc, ry, rows):
    out = []
    for i, f in enumerate(FLIP8):
        lc[i].wait()
        cc[i].wait_recv()
        add_to(ploc.at[i], [ploc.at[i], rc.at[i]], rows)
        out.append(net.put(ploc.at[i], ry.at[i], net.flip(*f)))
    lc[3].wait()
    cc[3].wait_recv()
    return out


def norm_back(u, g, gain):
    r = rms_unit(u)
    unit = u * r
    gvec = g * gain
    return r * (gvec - unit * jnp.mean(gvec * unit, -1, keepdims=True))


class Scatter:
    def __init__(self, net, part, r1, r2, loc=None):
        self.net, self.part, self.r1, self.r2 = net, part, r1, r2
        self.loc = loc

    def stage_one(self):
        net, p, r1 = self.net, self.part, self.r1
        z, x = net.z, net.x
        self.lc = None
        if self.loc is not None:
            self.lc = [net.copy(p.at[0, z], self.loc.at[0]), net.copy(p.at[1, :, x], self.loc.at[1])]
        self.got = [[], []]
        for k, s in enumerate(ORDER):
            zz, xx = lax.rem(z + s, 4), lax.rem(x + s, 4)
            self.got[0].append(net.put(p.at[0, zz], r1.at[0, k], net.zp(s)))
            self.got[1].append(net.put(p.at[1, :, xx], r1.at[1, k], net.xp(s)))

    def stage_two(self):
        net, r1, r2 = self.net, self.r1, self.r2
        self.nxt = []
        for h in range(2):
            if self.lc is not None:
                self.lc[h].wait()
            for cp in self.got[h]:
                cp.wait_recv()
            me = net.x if h == 0 else net.z
            blocks = []
            for b in range(4):
                if self.loc is not None:
                    mine = self.loc.at[h, b]
                else:
                    mine = self.part.at[0, net.z, b] if h == 0 else self.part.at[1, b, net.x]
                dst = r1.at[h, 0, b]
                add_to(dst, [mine] + [r1.at[h, k, b] for k in range(3)], 64)
            self.nxt.append([
                net.put(r1.at[h, 0, lax.rem(me + s, 4)], r2.at[h, k], net.xp(s) if h == 0 else net.zp(s))
                for k, s in enumerate(ORDER)
            ])

    def stage_y(self, dst):
        net, r1, r2 = self.net, self.r1, self.r2
        for h in range(2):
            for cp in self.nxt[h]:
                cp.wait_recv()
            me = net.x if h == 0 else net.z
            add_to(r2.at[h, 0], [r1.at[h, 0, me]] + [r2.at[h, k] for k in range(3)], 64)
        self.yc = net.put(r2.at[1 - net.a, 0], dst, net.flip(1, 0))


def m3_body(names, *refs):
    r = dict(zip(names, refs))
    net = Net(r["send"], r["recv"], r["loc"])
    a, z, x, t, hi, c = net.a, net.z, net.x, net.t, net.hi, net.c
    net.greet(all_peers(net))
    mid, cot, tok, gains = r["mid"], r["cot"], r["tok"], r["gains"]
    rows, d = cot.shape
    n = 4 * rows
    step = 32
    far, near = 1 - hi, hi
    sib, chip = net.sib(), net.flip(0, 1)
    bcc, blc = scatter8_start(net, r["fback"], r["bl"], r["bc"])
    ffn = [Scatter(net, r["p" + k], r["r1" + k], r["r2" + k], r["l" + k]) for k in "gud"]
    for sc in ffn:
        sc.stage_one()
    bgot = scatter8_send(net, bcc, blc, r["bl"], r["bc"], r["by"], rows)
    bias = r["bias"]
    bias[...] = jnp.where(
        (r["seqc"][...] == r["seqr"][...]) & (r["blkc"][...] <= r["blkr"][...]), jnp.float32(0.0), jnp.float32(-1e30)
    )
    for cp in bgot:
        cp.wait_recv()
    gm, gmid, bl, bc, by = r["gm"], r["gmid"], r["bl"], r["bc"], r["by"]

    @pl.loop(0, rows // step)
    def _(i):
        sl = pl.ds(pl.multiple_of(i * step, step), step)
        g = bl[3, sl, :].astype(F32) + bc[3, sl, :].astype(F32)
        for j in range(3):
            g += by[j, sl, :].astype(F32)
        m = cot[sl, :].astype(F32) + norm_back(mid[sl, :], g, gains[1:2, :])
        gmid[sl, :] = m
        gm[t, sl, :] = m.astype(BF)

    mine = gm.at[t]
    mf = net.put(mine, mine, chip)
    ms = [net.put(mine, mine, sib)]
    fcc, flc = scatter8_start(net, r["fout"], r["fl"], r["fc"])
    fgot = scatter8_send(net, fcc, flc, r["fl"], r["fc"], r["fy"], rows)
    mf.wait_recv()
    theirs = gm.at[far * 2 + c]
    ms.append(net.put(theirs, theirs, sib))
    for cp in ms:
        cp.wait_recv()
    gatt, att, q, kv4, wq, wo = r["gatt"], r["att"], r["q"], r["kv4"], r["wq"], r["wo"]
    for i in range(2):
        w = wo[:, :, :, :, 256 * i : 256 * i + 256].reshape(d, 256)
        gatt[:, 256 * i : 256 * i + 256] = dot(gm[...].reshape(n, d), w).astype(BF)
    po, pq, xn, dqkv = r["po"], r["pq"], r["xn"], r["dqkv"]

    @pl.loop(0, 8)
    def _(i):
        ln = pl.ds(pl.multiple_of(i * 256, 256), 256)
        left = gm[:, :, ln].reshape(n, 256)
        po[lax.div(i, 4), lax.rem(i, 4)] = dot(left, att[...], TN).reshape(4, 64, 512).astype(BF)

    so = Scatter(net, po, r["r1o"], r["r2o"])
    so.stage_one()
    ak, av = r["ak"], r["av"]
    ak[...] = jnp.zeros_like(ak)
    av[...] = jnp.zeros_like(av)
    cos, sin = r["cos"], r["sin"]
    low = low_half((n, 128))
    scale = 1.0 / math.sqrt(HD)

    @pl.loop(0, 4)
    def _(j):
        ln = pl.ds(pl.multiple_of(j * 128, 128), 128)
        qp, gp = q[:, ln], gatt[:, ln]
        cv, ck, gq = [], [], None
        for h in range(2):
            s = dot(kv4[h], qp, NT) + bias[...]
            e = jnp.exp(s - jnp.max(s, 0, keepdims=True))
            p = e * (1.0 / jnp.sum(e, 0, keepdims=True))
            pg = p * dot(kv4[2 + h], gp, NT)
            graw = (pg - p * jnp.sum(pg, 0, keepdims=True)).astype(BF)
            cv.append(dot(p.astype(BF), gp))
            ck.append(dot(graw, qp))
            term = dot(kv4[h], graw, TN)
            gq = term if gq is None else gq + term
        av[...] += jnp.where(low, cv[0], cv[1])
        ak[...] += jnp.where(low, ck[0], ck[1])
        dqkv[:, ln] = (rot_back(gq.T, cos[...], sin[...]) * scale).astype(BF)

    tk = ak[...] + pltpu.roll(ak[...], 64, 1)
    tv = av[...] + pltpu.roll(av[...], 64, 1)
    dqkv[:, 512:640] = jnp.where(low, rot_back(tk, cos[...], sin[...]), tv).astype(BF)

    @pl.loop(0, 8)
    def _(i):
        ln = pl.ds(pl.multiple_of(i * 256, 256), 256)
        pq[lax.div(i, 4), lax.rem(i, 4)] = dot(xn[:, ln], dqkv[...], TN).reshape(4, 64, 640).astype(BF)

    sq = Scatter(net, pq, r["r1q"], r["r2q"])
    sq.stage_one()
    ap, arc, arh = r["ap"], r["arc"], r["arh"]
    for i in range(4):
        w = wq[i // 2, 2 * (i % 2) : 2 * (i % 2) + 2].reshape(512, 640)
        ap[:, :, 512 * i : 512 * i + 512] = dot(dqkv[...], w, NT).reshape(4, rows, 512).astype(BF)
    acc = [net.put(ap.at[h * 2 + (1 - c)], arc.at[i], sib) for i, h in enumerate((far, near))]
    acc[0].wait_recv()
    af = ap.at[far * 2 + c]
    add_to(af, [af, arc.at[0]], rows)
    ach = net.put(af, arh, chip)
    for sc in ffn:
        sc.stage_two()
    so.stage_two()
    for cp in fgot:
        cp.wait_recv()
    fl, fc, fy, res, gtok = r["fl"], r["fc"], r["fy"], r["res"], r["gtok"]

    @pl.loop(0, rows // step)
    def _(i):
        sl = pl.ds(pl.multiple_of(i * step, step), step)
        g = fl[3, sl, :].astype(F32) + fc[3, sl, :].astype(F32)
        for j in range(3):
            g += fy[j, sl, :].astype(F32)
        res[sl, :] = (mid[sl, :] + g).astype(BF)

    sq.stage_two()
    acc[1].wait_recv()
    ach.wait_recv()
    an = ap.at[near * 2 + c]

    @pl.loop(0, rows // step)
    def _(i):
        sl = pl.ds(pl.multiple_of(i * step, step), step)
        g = an[sl, :].astype(F32) + arc[1, sl, :].astype(F32) + arh[sl, :].astype(F32)
        gtok[sl, :] = (gmid[sl, :] + norm_back(tok[sl, :].astype(F32), g, gains[0:1, :])).astype(BF)

    outs = [r["og"], r["ou"], r["od"]]
    for sc, o in zip(ffn, outs):
        sc.stage_y(o.at[a])
        o[a] = sc.r2[a, 0]
    so.stage_y(r["yo"])
    sq.stage_y(r["yq"])
    for sc in ffn:
        sc.yc.wait_recv()
    for sc, o, y in ((so, r["oo"], r["yo"]), (sq, r["oq"], r["yq"])):
        sc.yc.wait_recv()
        add_to(o, [sc.r2.at[a, 0], y], 64)
    net.finish()


def m3(fback, fout, pg, pu, pd, mid, cot, tok, gains, xn, q, kv4, att, wq, wo, cos, sin, seq, blk):
    rows, d = tok.shape
    n = 4 * rows
    sd = jax.ShapeDtypeStruct
    v = pltpu.VMEM
    col = lambda u: u.reshape(n, 1)
    row = lambda u: u.reshape(1, n)
    ins = dict(
        fback=fback, fout=fout, pg=pg, pu=pu, pd=pd,
        mid=mid, cot=cot, tok=tok, gains=gains, xn=xn, q=q, kv4=kv4, att=att, wq=wq, wo=wo, cos=cos, sin=sin,
        seqr=row(seq), seqc=col(seq), blkr=row(blk), blkc=col(blk),
    )
    w3 = (2, 64, FH)
    outs = dict(
        og=sd(w3, BF), ou=sd(w3, BF), od=sd(w3, BF), oo=sd((64, 512), F32), oq=sd((64, 640), F32),
        res=sd((rows, d), BF), gtok=sd((rows, d), BF),
    )
    scr = dict(
        bl=v((4, rows, d), BF), bc=v((4, rows, d), BF), by=v((3, rows, d), BF),
        fl=v((4, rows, d), BF), fc=v((4, rows, d), BF), fy=v((3, rows, d), BF),
        gm=v((4, rows, d), BF), gmid=v((rows, d), F32), bias=v((n, n), F32), gatt=v((n, 512), BF),
        dqkv=v((n, 640), BF), ak=v((n, 128), F32), av=v((n, 128), F32),
        po=v((2, 4, 4, 64, 512), BF), pq=v((2, 4, 4, 64, 640), BF),
        ap=v((4, rows, d), BF), arc=v((2, rows, d), BF), arh=v((rows, d), BF),
        yo=v((64, 512), BF), yq=v((64, 640), BF),
    )
    for k, w in (("g", FH), ("u", FH), ("d", FH), ("o", 512), ("q", 640)):
        scr["r1" + k] = v((2, 3, 4, 64, w), BF)
        scr["r2" + k] = v((2, 3, 64, w), BF)
    for k in "gud":
        scr["l" + k] = v((2, 4, 64, FH), BF)
    sem = sems(100, 24)
    names = list(ins) + list(outs) + list(scr) + ["send", "recv", "loc"]
    got = pl.pallas_call(
        functools.partial(m3_body, names),
        out_shape=list(outs.values()),
        in_specs=[ANY] * 5 + [VM] * (len(ins) - 5),
        out_specs=[VM] * len(outs),
        scratch_shapes=list(scr.values()) + sem,
        compiler_params=pltpu.CompilerParams(collective_id=3, has_side_effects=True, vmem_limit_bytes=62 << 20),
        name="attention_backward",
    )(*ins.values())
    return dict(zip(outs, got))


def rope_tables(places, head_width):
    half_width = head_width // 2
    inv_freq = 1.0 / ROPE_BASE ** (jnp.arange(half_width, dtype=F32) * 2.0 / head_width)
    angles = places.astype(F32)[:, None] * inv_freq[None, :]
    angles = jnp.concatenate([angles, angles], -1)
    return (jnp.cos(angles), jnp.sin(angles))


def mm(l, r, dims=((1,), (0,))):
    return lax.dot_general(l, r, (dims, ((), ())), preferred_element_type=F32)


def halves(w):
    w = jnp.pad(w, ((0, 0), (0, 2 * FH - w.shape[1])))
    return jnp.stack([w[:, :FH], w[:, FH:]])


def per_device(
    tokens_in, cotangent, seq_ids, block_ids, positions, attn_gain, ffn_gain,
    w_query, w_key, w_value, w_out, w_gate, w_up, w_down,
):
    rows, d = tokens_in.shape
    n = seq_ids.shape[0]
    ff = w_gate.shape[1]
    hq = w_query.shape[1] // HD
    wq = jnp.concatenate([w_query, w_key, w_value], 1)
    wo = w_out.T
    gn = jnp.pad(jnp.stack([attn_gain, ffn_gain]).astype(F32), ((0, 6), (0, 64)))
    gn = jnp.where(lax.rem(lax.axis_index("dp"), 2) == 0, gn, jnp.roll(gn, 64, 1))
    cosine, sine = rope_tables(positions, HD)
    half = HD // 2
    signed = jnp.concatenate([-sine[:, :half], sine[:, half:]], -1)
    cos2, sin2 = jnp.concatenate([cosine] * 2, -1), jnp.concatenate([signed] * 2, -1)
    xf, mid, xn, q, kv4, att, gains, wqkv, wot, cot, wg, wu, wdt = m1(
        tokens_in, cotangent, wq, wo, halves(w_gate), halves(w_up), halves(w_down.T), gn,
        cos2, sin2, seq_ids, block_ids,
    )
    cot = cot.reshape(2 * n, d)
    wg, wu, wdt = (w.reshape(d, FH) for w in (wg, wu, wdt))
    xf = xf.reshape(2 * n, d)
    gate = mm(xf, wg)
    up = mm(xf, wu)
    sig = jax.nn.sigmoid(gate)
    silu = gate * sig
    hid = (silu * up).astype(BF)
    gh = mm(cot, wdt)
    dgate = (gh * up * (sig * (1.0 + gate * (1.0 - sig)))).astype(BF)
    dup = (gh * silu).astype(BF)
    fback = (mm(dgate, wg, NT) + mm(dup, wu, NT)).astype(BF).reshape(2, 4, rows, d)
    fout = mm(hid, wdt, NT).astype(BF).reshape(2, 4, rows, d)
    pd = mm(cot, hid, TN).astype(BF)
    pg = mm(xf, dgate, TN).astype(BF)
    pu = mm(xf, dup, TN).astype(BF)
    pg, pu, pd = (w.reshape(2, 4, 4, 64, FH) for w in (pg, pu, pd))
    out = m3(
        fback, fout, pg, pu, pd, mid, cotangent, tokens_in, gains, xn, q, kv4, att, wqkv, wot,
        cos2, sin2, seq_ids, block_ids,
    )
    og, ou, od, oo, oq, res, gtok = (out[k] for k in ("og", "ou", "od", "oo", "oq", "res", "gtok"))

    def join(o):
        return jnp.concatenate([o[0], o[1]], 1)[:, :ff].astype(F32)

    og, ou, od = join(og), join(ou), join(od)
    dg1 = jnp.sum(oq * wq.astype(F32), 1) / attn_gain.astype(F32)
    dg2 = jnp.sum(og * w_gate.astype(F32) + ou * w_up.astype(F32), 1) / ffn_gain.astype(F32)
    dg1, dg2 = lax.psum((dg1, dg2), "tensor")
    nq = hq * HD
    return (
        res, gtok, dg1, dg2, oq[:, :nq], oq[:, nq : nq + HD], oq[:, nq + HD :], oo.T, og, ou, od.T,
    )


def solution(mesh):
    both, dp, cols, rows = P(("dp", "tensor"), None), P("dp"), P("dp", "tensor"), P("tensor", "dp")
    return jax.shard_map(
        per_device,
        mesh=mesh,
        in_specs=(both, both, dp, dp, dp, dp, dp, cols, cols, cols, rows, cols, cols, rows),
        out_specs=(both, both, dp, dp, cols, cols, cols, rows, cols, cols, rows),
        check_vma=False,
    )
```

```python
import functools
import math

import jax
import jax.numpy as jnp
import numpy as np
from jax import lax
from jax.experimental import pallas as pl
from jax.experimental.pallas import tpu as pltpu
from jax.sharding import PartitionSpec as P

HD = 64
EPSILON = 1e-05
ROPE_BASE = 10000.0
MESH = pl.DeviceIdType.MESH
BF = jnp.bfloat16
F32 = jnp.float32
ANY = pl.BlockSpec(memory_space=pl.ANY)
VM = pl.BlockSpec(memory_space=pltpu.VMEM)
FH = 768


class Net:
    def __init__(self, send, recv, loc):
        self.send, self.recv, self.loc = send, recv, loc
        self.n = self.m = 0
        dp, t = lax.axis_index("dp"), lax.axis_index("tensor")
        self.a = lax.div(dp, 16)
        self.z = lax.rem(lax.div(dp, 4), 4)
        self.x = lax.rem(dp, 4)
        self.hi = lax.div(t, 2)
        self.c = lax.rem(t, 2)
        self.t = t
        self.sends = []

    def dev(self, a=None, z=None, x=None, hi=None, c=None):
        a = self.a if a is None else a
        z = self.z if z is None else z
        x = self.x if x is None else x
        hi = self.hi if hi is None else hi
        c = self.c if c is None else c
        return (a * 16 + z * 4 + x, hi * 2 + c)

    def xp(self, s):
        return self.dev(x=lax.rem(self.x + s, 4))

    def zp(self, s):
        return self.dev(z=lax.rem(self.z + s, 4))

    def first(self, s, own):
        k = self.a if own else 1 - self.a
        return self.dev(z=lax.rem(self.z + s * k, 4), x=lax.rem(self.x + s * (1 - k), 4))

    def flip(self, da, dh):
        return self.dev(a=1 - self.a if da else None, hi=1 - self.hi if dh else None)

    def sib(self):
        return self.dev(c=1 - self.c)

    def hello(self, peers):
        bar = pltpu.get_barrier_semaphore()
        for p in peers:
            pl.semaphore_signal(bar, inc=1, device_id=p, device_id_type=MESH)

    def met(self, peers):
        pl.semaphore_wait(pltpu.get_barrier_semaphore(), len(peers))

    def greet(self, peers):
        self.hello(peers)
        self.met(peers)

    def put(self, src, dst, dev):
        i = self.n
        self.n += 1
        cp = pltpu.make_async_remote_copy(
            src_ref=src, dst_ref=dst, send_sem=self.send.at[i], recv_sem=self.recv.at[i],
            device_id=dev, device_id_type=MESH,
        )
        cp.start()
        self.sends.append(cp)
        return cp

    def copy(self, src, dst):
        i = self.m
        self.m += 1
        cp = pltpu.make_async_copy(src, dst, self.loc.at[i])
        cp.start()
        return cp

    def drop(self, cp):
        self.sends = [s for s in self.sends if s is not cp]

    def finish(self):
        for cp in self.sends:
            cp.wait_send()


FLIP4 = ((0, 1),)
FLIP8 = ((1, 0), (1, 1), (0, 1))
ORDER = (1, 3, 2)


def sems(n, m):
    return [pltpu.SemaphoreType.DMA((n,)), pltpu.SemaphoreType.DMA((n,)), pltpu.SemaphoreType.DMA((m,))]


def all_peers(net):
    return (
        [net.xp(s) for s in ORDER]
        + [net.zp(s) for s in ORDER]
        + [net.sib()]
        + [net.flip(*f) for f in FLIP8]
    )


def rms_unit(u):
    return lax.rsqrt(jnp.mean(u * u, -1, keepdims=True) + EPSILON)


def add_to(dst, terms, rows, step=32):
    @pl.loop(0, rows // step)
    def _(i):
        sl = pl.ds(pl.multiple_of(i * step, step), step)
        total = terms[0][sl, :].astype(F32)
        for ref in terms[1:]:
            total += ref[sl, :].astype(F32)
        dst[sl, :] = total.astype(dst.dtype)


def dot(l, r, dims=((1,), (0,))):
    return lax.dot_general(l, r, (dims, ((), ())), preferred_element_type=F32)


NT = ((1,), (1,))
TN = ((0,), (0,))


def low_half(shape):
    return lax.broadcasted_iota(jnp.int32, shape, 1) < HD


def first_quarter(shape):
    lane = lax.broadcasted_iota(jnp.int32, shape, 1)
    return lax.rem(lane, HD) < HD // 2


def rot(u, cos, sin):
    near = jnp.where(first_quarter(u.shape), pltpu.roll(u, 96, 1), pltpu.roll(u, 32, 1))
    return u * cos + near * sin


def rot_back(w, cos, sin):
    y = w * sin
    near = jnp.where(first_quarter(w.shape), pltpu.roll(y, 96, 1), pltpu.roll(y, 32, 1))
    return w * cos + near


class Gather:
    def __init__(self, net, src, dst, half):
        self.net, self.dst = net, dst
        self.own = src.at[net.a] if half else src
        self.other = src.at[1 - net.a] if half else src
        self.here = dst.at[net.a, net.z, net.x]

    def local(self):
        self.lc = self.net.copy(self.own, self.here)

    def over_y(self):
        self.yc = self.net.put(self.other, self.here, self.net.flip(1, 0))

    def stage_own(self):
        self.st = [self.net.put(self.own, self.here, self.net.first(s, True)) for s in ORDER]

    def stage_other(self):
        net = self.net
        self.yc.wait_recv()
        there = self.dst.at[1 - net.a, net.z, net.x]
        self.st += [net.put(there, there, net.first(s, False)) for s in ORDER]

    def stage_two(self):
        net, dst = self.net, self.dst
        self.lc.wait()
        for cp in self.st:
            cp.wait_recv()
        z, x = net.z, net.x
        self.near = [
            (net.put(dst.at[0, z], dst.at[0, z], net.zp(s)), net.put(dst.at[1, :, x], dst.at[1, :, x], net.xp(s)))
            for s in (1, 3)
        ]

    def forward(self):
        net, dst = self.net, self.dst
        self.last = []
        for (cz, cx), s, lo in zip(self.near, (1, 3), (0, 2)):
            cz.wait_recv()
            blk = dst.at[0, lax.rem(net.z + 4 - s, 4), lo : lo + 2]
            self.last.append(net.put(blk, blk, net.zp(s)))
            cx.wait_recv()
            blk = dst.at[1, lo : lo + 2, lax.rem(net.x + 4 - s, 4)]
            self.last.append(net.put(blk, blk, net.xp(s)))

    def done(self):
        for cp in self.last:
            cp.wait_recv()


def pack_halves(dst, w):
    rest = w.shape[1] - FH
    dst[0] = w[:, :FH]
    dst[1, :, :rest] = w[:, FH:]
    dst[1, :, rest:] = jnp.zeros((w.shape[0], FH - rest), BF)


def column(row, n):
    return jnp.broadcast_to(row, (128, n)).T


def m1_body(
    tok, cot, w_q, w_k, w_v, wo, w_g, w_u, w_d, g_a, g_f, freq, seqr, blkr, posr,
    xf, mid, xn, q, kv4, att, gains, aq, ao, cos, sin, bias_t, cot_all, ag, au, ad,
    wq, wf, gn, tall, an, bias, ones2, part, rc, rh, send, recv, loc,
):
    net = Net(send, recv, loc)
    a, z, x, t, hi, c = net.a, net.z, net.x, net.t, net.hi, net.c
    rows, d = tok.shape
    n = 4 * rows
    nq = w_q.shape[1]
    net.hello(all_peers(net))
    lane = lax.broadcasted_iota(jnp.int32, (1, 128), 1)
    here = lax.div(lane, HD) == lax.rem(x, 2)
    gn[...] = jnp.zeros_like(gn)
    for i, g in enumerate((g_a, g_f)):
        g = g[...].astype(F32)
        gn[i : i + 1, :] = jnp.where(here, jnp.concatenate([g, g], 1), 0.0)
    wq[:, :nq] = w_q[...]
    wq[:, nq : nq + HD] = w_k[...]
    wq[:, nq + HD :] = w_v[...]
    net.met(all_peers(net))
    far, near = 1 - hi, hi
    tt = far * 2 + c
    sib, chip = net.sib(), net.flip(0, 1)
    tl = net.copy(tok, tall.at[t])
    tf = net.put(tok, tall.at[t], chip)
    ts = [net.put(tok, tall.at[t], sib)]
    gg, gq, go = Gather(net, gn, an, False), Gather(net, wq, aq, False), Gather(net, wo, ao, False)
    for g in (gg, gq, go):
        g.over_y()
        g.local()
        g.stage_own()
    cl = net.copy(cot, cot_all.at[a, t])
    for i, w in enumerate((w_g, w_u, w_d)):
        pack_halves(wf.at[i], w)
    ffn = [Gather(net, wf.at[i], o, True) for i, o in enumerate((ag, au, ad))]
    for g in ffn:
        g.local()
    for g in (gg, gq, go):
        g.stage_other()
    seq, blk = seqr[...].astype(F32), blkr[...].astype(F32)
    same = column(seq, n)[:, :1] == seq
    blkc = column(blk, n)[:, :1]
    bias[...] = jnp.where(same & (blk <= blkc), jnp.float32(0.0), jnp.float32(-1e30))
    bias_t[...] = jnp.where(same & (blkc <= blk), jnp.float32(0.0), jnp.float32(-1e30))
    for g in (gg, gq, go):
        g.stage_two()
    tf.wait_recv()
    ts.append(net.put(tall.at[tt], tall.at[tt], sib))
    cf = [net.put(cot, cot_all.at[a, t], net.flip(*f)) for f in FLIP8]
    cs = [net.put(cot, cot_all.at[a, t], sib)]
    for g in ffn:
        g.over_y()
    angles = column(posr[...].astype(F32), n) * freq[...]
    cos[...] = jnp.cos(angles)
    sine = jnp.sin(angles)
    sin[...] = jnp.where(first_quarter(sine.shape), -sine, sine)
    tl.wait()
    for cp in ts:
        cp.wait_recv()
    gg.forward()
    gq.forward()
    gg.done()
    for i in range(16):
        k = 2 * i
        pair = an[k // 16, k // 4 % 4, k % 4] + an[k // 16, k // 4 % 4, k % 4 + 1]
        gains[:, 128 * i : 128 * i + 128] = pair
    step = 32

    @pl.loop(0, n // step)
    def _(i):
        b = lax.div(i, rows // step)
        u = tall[b, pl.ds(pl.multiple_of(lax.rem(i, rows // step) * step, step), step), :].astype(F32)
        xn[pl.ds(pl.multiple_of(i * step, step), step), :] = (u * rms_unit(u) * gains[0:1, :]).astype(BF)

    go.forward()
    gq.done()
    for g in ffn:
        g.stage_own()
    scale = 1.0 / math.sqrt(HD)
    for lo, width in ((0, 256), (256, 256), (512, 128)):
        w = aq[:, :, :, :, lo : lo + width].reshape(d, width)
        val = dot(xn[...], w)
        if lo < 512:
            for i in range(2):
                at = lo + 128 * i
                q[:, at : at + 128] = (rot(val[:, 128 * i : 128 * i + 128], cos[...], sin[...]) * scale).astype(BF)
        else:
            low = low_half(val.shape)
            ke = jnp.where(low, rot(val, cos[...], sin[...]), 0.0)
            vo = jnp.where(low, 0.0, val)
            ve = pltpu.roll(vo, 64, 1)
            kv4[0] = ke.astype(BF)
            kv4[1] = pltpu.roll(ke, 64, 1).astype(BF)
            kv4[2] = ve.astype(BF)
            kv4[3] = vo.astype(BF)
            ones2[0] = jnp.where(low, ve, 1.0).astype(BF)
            ones2[1] = jnp.where(low, 1.0, vo).astype(BF)
    for g in ffn:
        g.stage_other()

    @pl.loop(0, 4)
    def _(j):
        ln = pl.ds(pl.multiple_of(j * 128, 128), 128)
        qp = q[:, ln]
        low = low_half((n, 128))
        o = []
        for h in range(2):
            s = dot(qp, kv4[h], NT) + bias[...]
            e = jnp.exp(s - jnp.max(s, -1, keepdims=True)).astype(BF)
            o.append(dot(e, ones2[h]))
        total = jnp.where(low, pltpu.roll(o[0], 64, 1), pltpu.roll(o[1], 64, 1))
        att[:, ln] = (jnp.where(low, o[0], o[1]) / total).astype(BF)

    go.done()
    for i in range(4):
        w = ao[i // 2, 2 * (i % 2) : 2 * (i % 2) + 2].reshape(512, 512)
        part[:, :, 512 * i : 512 * i + 512] = dot(att[...], w, NT).reshape(4, rows, 512).astype(BF)
    cc = [net.put(part.at[h * 2 + (1 - c)], rc.at[i], sib) for i, h in enumerate((far, near))]
    for g in ffn:
        g.stage_two()
    cc[0].wait_recv()
    pf = part.at[far * 2 + c]
    add_to(pf, [pf, rc.at[0]], rows)
    ch = net.put(pf, rh, chip)
    for (da, dh), cp in zip(FLIP8, cf):
        cp.wait_recv()
        blk = cot_all.at[1 - a if da else a, tt if dh else t]
        cs.append(net.put(blk, blk, sib))
    cc[1].wait_recv()
    ch.wait_recv()
    ffn[0].forward()
    mine_part = part.at[near * 2 + c]

    @pl.loop(0, rows // step)
    def _(i):
        sl = pl.ds(pl.multiple_of(i * step, step), step)
        m = (
            tall[t, sl, :].astype(F32)
            + (mine_part[sl, :].astype(F32) + rc[1, sl, :].astype(F32))
            + rh[sl, :].astype(F32)
        )
        mid[sl, :] = m
        xf[a, t, sl, :] = (m * rms_unit(m) * gains[1:2, :]).astype(BF)

    mine = xf.at[a, t]
    got = [net.put(mine, mine, net.flip(*f)) for f in FLIP8]
    tail = [net.put(mine, mine, sib)]
    ffn[1].forward()
    ffn[2].forward()
    for (da, dh), cp in zip(FLIP8, got):
        cp.wait_recv()
        blk = xf.at[1 - a if da else a, tt if dh else t]
        tail.append(net.put(blk, blk, sib))
    cl.wait()
    for g in ffn:
        g.done()
    for cp in tail + cs:
        cp.wait_recv()
    net.finish()


def m1(tok, cot, weights, g_a, g_f, seq, blk, pos):
    rows, d = tok.shape
    n = 4 * rows
    sd = jax.ShapeDtypeStruct
    v = pltpu.VMEM
    row = lambda u: u.reshape(1, n)
    freq = 1.0 / ROPE_BASE ** (np.arange(HD // 2, dtype=np.float32) * 2.0 / HD)
    freq = jnp.asarray(np.tile(freq, 4)[None], F32)
    ffn = [sd((2, 4, 4, 64, FH), BF)] * 3
    return pl.pallas_call(
        m1_body,
        out_shape=[
            sd((2, 4, rows, d), BF), sd((rows, d), F32), sd((n, d), BF), sd((n, 512), BF), sd((4, n, 128), BF),
            sd((n, 512), BF), sd((8, d), F32), sd((2, 4, 4, 64, 640), BF), sd((2, 4, 4, 64, 512), BF),
            sd((n, 128), F32), sd((n, 128), F32), sd((n, n), F32), sd((2, 4, rows, d), BF),
        ] + ffn,
        in_specs=[ANY] * 2 + [VM] * 13,
        out_specs=[VM] * 12 + [ANY] * 4,
        scratch_shapes=[
            v((64, 640), BF), v((3, 2, 64, FH), BF), v((8, 128), F32),
            v((4, rows, d), BF), v((2, 4, 4, 8, 128), F32), v((n, n), F32),
            v((2, n, 128), BF), v((4, rows, d), BF), v((2, rows, d), BF), v((rows, d), BF),
        ] + sems(124, 12),
        compiler_params=pltpu.CompilerParams(collective_id=1, has_side_effects=True, vmem_limit_bytes=56 << 20),
        name="attention_forward",
    )(tok, cot, *weights, g_a, g_f, freq, row(seq), row(blk), row(pos))


def scatter8_start(net, part, ploc, rc):
    a, hi, c = net.a, net.hi, net.c
    chips = [(1 - a if da else a, 1 - hi if dh else hi) for da, dh in FLIP8 + ((0, 0),)]
    cc = [net.put(part.at[b, h * 2 + (1 - c)], rc.at[i], net.sib()) for i, (b, h) in enumerate(chips)]
    lc = [net.copy(part.at[b, h * 2 + c], ploc.at[i]) for i, (b, h) in enumerate(chips)]
    return cc, lc


def scatter8_send(net, cc, lc, ploc, rc, ry, rows):
    out = []
    for i, f in enumerate(FLIP8):
        lc[i].wait()
        cc[i].wait_recv()
        add_to(ploc.at[i], [ploc.at[i], rc.at[i]], rows)
        out.append(net.put(ploc.at[i], ry.at[i], net.flip(*f)))
    lc[3].wait()
    cc[3].wait_recv()
    return out


def norm_back(u, g, gain):
    r = rms_unit(u)
    unit = u * r
    gvec = g * gain
    return r * (gvec - unit * jnp.mean(gvec * unit, -1, keepdims=True))


class Scatter:
    def __init__(self, net, part, r1, r2, loc=None):
        self.net, self.part, self.r1, self.r2 = net, part, r1, r2
        self.loc = loc

    def stage_one(self):
        net, p, r1 = self.net, self.part, self.r1
        z, x = net.z, net.x
        self.lc = None
        if self.loc is not None:
            self.lc = [net.copy(p.at[0, z], self.loc.at[0]), net.copy(p.at[1, :, x], self.loc.at[1])]
        self.got = [[], []]
        for k, s in enumerate(ORDER):
            zz, xx = lax.rem(z + s, 4), lax.rem(x + s, 4)
            self.got[0].append(net.put(p.at[0, zz], r1.at[0, k], net.zp(s)))
            self.got[1].append(net.put(p.at[1, :, xx], r1.at[1, k], net.xp(s)))

    def stage_two(self):
        net, r1, r2 = self.net, self.r1, self.r2
        self.nxt = []
        for h in range(2):
            if self.lc is not None:
                self.lc[h].wait()
            for cp in self.got[h]:
                cp.wait_recv()
            me = net.x if h == 0 else net.z
            blocks = []
            for b in range(4):
                if self.loc is not None:
                    mine = self.loc.at[h, b]
                else:
                    mine = self.part.at[0, net.z, b] if h == 0 else self.part.at[1, b, net.x]
                dst = r1.at[h, 0, b]
                add_to(dst, [mine] + [r1.at[h, k, b] for k in range(3)], 64)
            self.nxt.append([
                net.put(r1.at[h, 0, lax.rem(me + s, 4)], r2.at[h, k], net.xp(s) if h == 0 else net.zp(s))
                for k, s in enumerate(ORDER)
            ])

    def stage_y(self, dst):
        net, r1, r2 = self.net, self.r1, self.r2
        for h in range(2):
            for cp in self.nxt[h]:
                cp.wait_recv()
            me = net.x if h == 0 else net.z
            add_to(r2.at[h, 0], [r1.at[h, 0, me]] + [r2.at[h, k] for k in range(3)], 64)
        self.yc = net.put(r2.at[1 - net.a, 0], dst, net.flip(1, 0))


def weight_grad(net, left, right, out, chunk, stage, csem, ssem):
    def load(i, k):
        sl = pl.ds(pl.multiple_of(i * 256, 256), 256)
        return pltpu.make_async_copy(left.at[:, sl], chunk.at[k], csem.at[k])

    def save(i, k):
        return pltpu.make_async_copy(stage.at[k], out.at[lax.div(i, 4), lax.rem(i, 4)], ssem.at[k])

    load(0, 0).start()

    @pl.loop(0, 4)
    def _(j):
        for k in range(2):
            i = 2 * j + k
            load(i, k).wait()
            if k == 0:
                load(i + 1, 1).start()
            else:

                @pl.when(j < 3)
                def _():
                    load(i + 1, 0).start()

            @pl.when(j > 0)
            def _():
                save(i - 2, k).wait()

            stage[k] = dot(chunk[k], right[...], TN).reshape(4, 64, FH).astype(BF)
            save(i, k).start()

    save(6, 0).wait()
    save(7, 1).wait()


def m3_body(names, *refs):
    r = dict(zip(names, refs))
    net = Net(r["send"], r["recv"], r["loc"])
    a, z, x, t, hi, c = net.a, net.z, net.x, net.t, net.hi, net.c
    net.greet(all_peers(net))
    mid, cot, tok, gains = r["mid"], r["cot"], r["tok"], r["gains"]
    rows, d = cot.shape
    n = 4 * rows
    step = 32
    far, near = 1 - hi, hi
    sib, chip = net.sib(), net.flip(0, 1)
    bcc, blc = scatter8_start(net, r["fback"], r["bl"], r["bc"])
    bias = r["bias"]
    ffn = []
    for i, (k, left, right) in enumerate((("d", "call", "hid"), ("g", "xf", "dgate"), ("u", "xf", "dup"))):
        weight_grad(net, r[left], r[right], r["p" + k], r["chunk"], r["stage"], r["csem"], r["ssem"])
        ffn.append(Scatter(net, r["p" + k], r["r1" + k], r["r2" + k], r["l" + k]))
        ffn[i].stage_one()
        if i == 0:
            bgot = scatter8_send(net, bcc, blc, r["bl"], r["bc"], r["by"], rows)
    for cp in bgot:
        cp.wait_recv()
    gm, gmid, bl, bc, by = r["gm"], r["gmid"], r["bl"], r["bc"], r["by"]

    @pl.loop(0, rows // step)
    def _(i):
        sl = pl.ds(pl.multiple_of(i * step, step), step)
        g = bl[3, sl, :].astype(F32) + bc[3, sl, :].astype(F32)
        for j in range(3):
            g += by[j, sl, :].astype(F32)
        m = cot[sl, :].astype(F32) + norm_back(mid[sl, :], g, gains[1:2, :])
        gmid[sl, :] = m
        gm[t, sl, :] = m.astype(BF)

    free = r["free"]
    for f in FLIP8:
        pl.semaphore_signal(free, inc=1, device_id=net.flip(*f), device_id_type=MESH)
    mine = gm.at[t]
    mf = net.put(mine, mine, chip)
    ms = [net.put(mine, mine, sib)]
    mf.wait_recv()
    theirs = gm.at[far * 2 + c]
    ms.append(net.put(theirs, theirs, sib))
    for cp in ms:
        cp.wait_recv()
    for cp in bgot:
        cp.wait_send()
        net.drop(cp)
    pl.semaphore_wait(free, len(FLIP8))
    fcc, flc = scatter8_start(net, r["fout"], bl, bc)
    fgot = scatter8_send(net, fcc, flc, bl, bc, by, rows)
    gatt, att, q, kv4, wq, wo = r["gatt"], r["att"], r["q"], r["kv4"], r["wq"], r["wo"]
    for i in range(2):
        w = wo[:, :, :, :, 256 * i : 256 * i + 256].reshape(d, 256)
        gatt[:, 256 * i : 256 * i + 256] = dot(gm[...].reshape(n, d), w).astype(BF)
    po, pq, xn, dqkv = r["po"], r["pq"], r["xn"], r["dqkv"]

    @pl.loop(0, 8)
    def _(i):
        ln = pl.ds(pl.multiple_of(i * 256, 256), 256)
        left = gm[:, :, ln].reshape(n, 256)
        po[lax.div(i, 4), lax.rem(i, 4)] = dot(left, att[...], TN).reshape(4, 64, 512).astype(BF)

    so = Scatter(net, po, r["r1o"], r["r2o"])
    so.stage_one()
    ak, av = r["ak"], r["av"]
    ak[...] = jnp.zeros_like(ak)
    av[...] = jnp.zeros_like(av)
    cos, sin = r["cos"], r["sin"]
    low = low_half((n, 128))
    scale = 1.0 / math.sqrt(HD)

    @pl.loop(0, 4)
    def _(j):
        ln = pl.ds(pl.multiple_of(j * 128, 128), 128)
        qp, gp = q[:, ln], gatt[:, ln]
        cv, ck, gq = [], [], None
        for h in range(2):
            s = dot(kv4[h], qp, NT) + bias[...]
            e = jnp.exp(s - jnp.max(s, 0, keepdims=True))
            p = e * (1.0 / jnp.sum(e, 0, keepdims=True))
            pg = p * dot(kv4[2 + h], gp, NT)
            graw = (pg - p * jnp.sum(pg, 0, keepdims=True)).astype(BF)
            cv.append(dot(p.astype(BF), gp))
            ck.append(dot(graw, qp))
            term = dot(kv4[h], graw, TN)
            gq = term if gq is None else gq + term
        av[...] += jnp.where(low, cv[0], cv[1])
        ak[...] += jnp.where(low, ck[0], ck[1])
        dqkv[:, ln] = (rot_back(gq.T, cos[...], sin[...]) * scale).astype(BF)

    tk = ak[...] + pltpu.roll(ak[...], 64, 1)
    tv = av[...] + pltpu.roll(av[...], 64, 1)
    dqkv[:, 512:640] = jnp.where(low, rot_back(tk, cos[...], sin[...]), tv).astype(BF)

    @pl.loop(0, 8)
    def _(i):
        ln = pl.ds(pl.multiple_of(i * 256, 256), 256)
        pq[lax.div(i, 4), lax.rem(i, 4)] = dot(xn[:, ln], dqkv[...], TN).reshape(4, 64, 640).astype(BF)

    sq = Scatter(net, pq, r["r1q"], r["r2q"])
    sq.stage_one()
    ap, arc, arh = r["ap"], r["arc"], r["arh"]
    for i in range(4):
        w = wq[i // 2, 2 * (i % 2) : 2 * (i % 2) + 2].reshape(512, 640)
        ap[:, :, 512 * i : 512 * i + 512] = dot(dqkv[...], w, NT).reshape(4, rows, 512).astype(BF)
    acc = [net.put(ap.at[h * 2 + (1 - c)], arc.at[i], sib) for i, h in enumerate((far, near))]
    acc[0].wait_recv()
    af = ap.at[far * 2 + c]
    add_to(af, [af, arc.at[0]], rows)
    ach = net.put(af, arh, chip)
    for sc in ffn:
        sc.stage_two()
    so.stage_two()
    for cp in fgot:
        cp.wait_recv()
    res, gtok = r["res"], r["gtok"]

    @pl.loop(0, rows // step)
    def _(i):
        sl = pl.ds(pl.multiple_of(i * step, step), step)
        g = bl[3, sl, :].astype(F32) + bc[3, sl, :].astype(F32)
        for j in range(3):
            g += by[j, sl, :].astype(F32)
        res[sl, :] = (mid[sl, :] + g).astype(BF)

    sq.stage_two()
    acc[1].wait_recv()
    ach.wait_recv()
    an = ap.at[near * 2 + c]

    @pl.loop(0, rows // step)
    def _(i):
        sl = pl.ds(pl.multiple_of(i * step, step), step)
        g = an[sl, :].astype(F32) + arc[1, sl, :].astype(F32) + arh[sl, :].astype(F32)
        gtok[sl, :] = (gmid[sl, :] + norm_back(tok[sl, :].astype(F32), g, gains[0:1, :])).astype(BF)

    for sc, k in zip(ffn, "dgu"):
        o = r["y" + k]
        sc.stage_y(o.at[a])
        o[a] = sc.r2[a, 0]
    so.stage_y(r["yo"])
    sq.stage_y(r["yq"])
    dg = r["dg"]
    for sc in ffn:
        sc.yc.wait_recv()
    tot = jnp.zeros((64, 128), F32)
    for k in "gu":
        y, w = r["y" + k], r["w_" + k]
        for i in range(w.shape[1] // 128):
            lo, half = 128 * i % FH, 128 * i // FH
            tot += y[half, :, lo : lo + 128].astype(F32) * w[:, 128 * i : 128 * i + 128].astype(F32)
    dg[1] = tot
    so.yc.wait_recv()
    add_to(r["oo"], [so.r2.at[a, 0], r["yo"]], 64)
    sq.yc.wait_recv()
    dw = sq.r2[a, 0].astype(F32) + r["yq"][...].astype(F32)
    nq = r["oq"].shape[1]
    dk, dv = dw[:, nq : nq + HD], dw[:, nq + HD :]
    r["oq"][...] = dw[:, :nq]
    r["ok"][...] = dk
    r["ov"][...] = dv
    tot = jnp.zeros((64, 128), F32)
    for i in range(nq // 128):
        sl = slice(128 * i, 128 * i + 128)
        tot += dw[:, sl] * r["w_q"][:, sl].astype(F32)
    small = dk * r["w_k"][...].astype(F32) + dv * r["w_v"][...].astype(F32)
    dg[0] = tot + jnp.concatenate([small, jnp.zeros_like(small)], 1)
    for at, peer in enumerate((sib, chip)):
        cp = net.put(dg, r["dy"].at[at], peer)
        cp.wait()
        net.drop(cp)
        dg[...] += r["dy"][at]
    for i, (o, g) in enumerate((("dg1", "g_a"), ("dg2", "g_f"))):
        r[o][...] = jnp.sum(dg[i].T, 0, keepdims=True) / r[g][...].astype(F32)
    net.finish()


def m3(hbm, vmem, shapes):
    rows, d = shapes
    n = 4 * rows
    sd = jax.ShapeDtypeStruct
    v = pltpu.VMEM
    part = (2, 4, 4, 64, FH)
    outs = dict(
        yg=sd((2, 64, FH), BF), yu=sd((2, 64, FH), BF), yd=sd((2, 64, FH), BF), oo=sd((64, 512), F32),
        oq=sd((64, 512), F32), ok=sd((64, HD), F32), ov=sd((64, HD), F32),
        res=sd((rows, d), BF), gtok=sd((rows, d), BF), dg1=sd((1, 64), F32), dg2=sd((1, 64), F32),
        pg=sd(part, BF), pu=sd(part, BF), pd=sd(part, BF),
    )
    scr = dict(
        bl=v((4, rows, d), BF), bc=v((4, rows, d), BF), by=v((3, rows, d), BF),
        gm=v((4, rows, d), BF), gmid=v((rows, d), F32), gatt=v((n, 512), BF),
        dqkv=v((n, 640), BF), ak=v((n, 128), F32), av=v((n, 128), F32),
        po=v((2, 4, 4, 64, 512), BF), pq=v((2, 4, 4, 64, 640), BF),
        ap=v((4, rows, d), BF), arc=v((2, rows, d), BF), arh=v((rows, d), BF),
        yo=v((64, 512), BF), yq=v((64, 640), BF), dg=v((2, 64, 128), F32), dy=v((2, 2, 64, 128), F32),
        chunk=v((2, 2 * n, 256), BF), stage=v((2, 4, 64, FH), BF),
        csem=pltpu.SemaphoreType.DMA((2,)), ssem=pltpu.SemaphoreType.DMA((2,)), free=pltpu.SemaphoreType.REGULAR,
    )
    for k, w in (("g", FH), ("u", FH), ("d", FH), ("o", 512), ("q", 640)):
        scr["r1" + k] = v((2, 3, 4, 64, w), BF)
        scr["r2" + k] = v((2, 3, 64, w), BF)
    for k in "gud":
        scr["l" + k] = v((2, 4, 64, FH), BF)
    sem = sems(100, 24)
    names = list(hbm) + list(vmem) + list(outs) + list(scr) + ["send", "recv", "loc"]
    got = pl.pallas_call(
        functools.partial(m3_body, names),
        out_shape=list(outs.values()),
        in_specs=[ANY] * len(hbm) + [VM] * len(vmem),
        out_specs=[VM] * (len(outs) - 3) + [ANY] * 3,
        scratch_shapes=list(scr.values()) + sem,
        compiler_params=pltpu.CompilerParams(collective_id=3, has_side_effects=True, vmem_limit_bytes=62 << 20),
        name="attention_backward",
    )(*hbm.values(), *vmem.values())
    return dict(zip(outs, got))


def mm(l, r, dims=((1,), (0,))):
    return lax.dot_general(l, r, (dims, ((), ())), preferred_element_type=F32)


def final_body(yg, yu, yd, *refs):
    k = (len(refs) - 3) // 2
    for y, o in zip((yg, yu, yd), refs[k : k + 3]):
        rest = o.shape[1] - FH
        o[:, :FH] = y[0].astype(F32)
        o[:, FH:] = y[1, :, :rest].astype(F32)
    for i, o in zip(refs[:k], refs[k + 3 :]):
        o[...] = i[...]


def final(halves, others, ff):
    sd = jax.ShapeDtypeStruct
    return pl.pallas_call(
        final_body,
        out_shape=[sd((64, ff), F32)] * 3 + [sd(o.shape, o.dtype) for o in others],
        in_specs=[VM] * (3 + len(others)),
        out_specs=[VM] * (3 + len(others)),
        name="final",
    )(*halves, *others)


def per_device(
    tokens_in, cotangent, seq_ids, block_ids, positions, attn_gain, ffn_gain,
    w_query, w_key, w_value, w_out, w_gate, w_up, w_down,
):
    rows, d = tokens_in.shape
    n = seq_ids.shape[0]
    weights = (w_query, w_key, w_value, w_out.T, w_gate, w_up, w_down.T)
    g_a, g_f = attn_gain.reshape(1, -1), ffn_gain.reshape(1, -1)
    xf, mid, xn, q, kv4, att, gains, wqkv, wot, cos, sin, bias_t, cot, wg, wu, wdt = m1(
        tokens_in, cotangent, weights, g_a, g_f, seq_ids, block_ids, positions
    )
    cot = cot.reshape(2 * n, d)
    wg, wu, wdt = (w.reshape(d, FH) for w in (wg, wu, wdt))
    xf = xf.reshape(2 * n, d)
    gate = mm(xf, wg)
    up = mm(xf, wu)
    sig = jax.nn.sigmoid(gate)
    silu = gate * sig
    hid = (silu * up).astype(BF)
    gh = mm(cot, wdt)
    dgate = (gh * up * (sig * (1.0 + gate * (1.0 - sig)))).astype(BF)
    dup = (gh * silu).astype(BF)
    fback = (mm(dgate, wg, NT) + mm(dup, wu, NT)).astype(BF).reshape(2, 4, rows, d)
    fout = mm(hid, wdt, NT).astype(BF).reshape(2, 4, rows, d)
    out = m3(
        dict(fback=fback, fout=fout, xf=xf, call=cot),
        dict(
            hid=hid, dgate=dgate, dup=dup, mid=mid, cot=cotangent, tok=tokens_in, gains=gains, xn=xn, q=q, kv4=kv4,
            att=att, wq=wqkv, wo=wot, cos=cos, sin=sin, bias=bias_t,
            w_q=w_query, w_k=w_key, w_v=w_value, w_g=w_gate, w_u=w_up, g_a=g_a, g_f=g_f,
        ),
        (rows, d),
    )
    keep = ("res", "gtok", "dg1", "dg2", "oq", "ok", "ov", "oo")
    og, ou, od, res, gtok, dg1, dg2, oq, ok, ov, oo = final(
        [out[k] for k in ("yg", "yu", "yd")], [out[k] for k in keep], w_gate.shape[1]
    )
    return (res, gtok, dg1.reshape(-1), dg2.reshape(-1), oq, ok, ov, oo.T, og, ou, od.T)


def solution(mesh):
    both, dp, cols, rows = P(("dp", "tensor"), None), P("dp"), P("dp", "tensor"), P("tensor", "dp")
    return jax.shard_map(
        per_device,
        mesh=mesh,
        in_specs=(both, both, dp, dp, dp, dp, dp, cols, cols, cols, rows, cols, cols, rows),
        out_specs=(both, both, dp, dp, cols, cols, cols, rows, cols, cols, rows),
        check_vma=False,
    )
```

```python
import functools
import math

import jax
import jax.numpy as jnp
import numpy as np
from jax import lax
from jax.experimental import pallas as pl
from jax.experimental.pallas import tpu as pltpu
from jax.sharding import PartitionSpec as P

HD = 64
EPSILON = 1e-05
ROPE_BASE = 10000.0
MESH = pl.DeviceIdType.MESH
BF = jnp.bfloat16
F32 = jnp.float32
ANY = pl.BlockSpec(memory_space=pl.ANY)
VM = pl.BlockSpec(memory_space=pltpu.VMEM)
FH = 768


class Net:
    def __init__(self, send, recv, loc):
        self.send, self.recv, self.loc = send, recv, loc
        self.n = self.m = 0
        dp, t = lax.axis_index("dp"), lax.axis_index("tensor")
        self.a = lax.div(dp, 16)
        self.z = lax.rem(lax.div(dp, 4), 4)
        self.x = lax.rem(dp, 4)
        self.hi = lax.div(t, 2)
        self.c = lax.rem(t, 2)
        self.t = t
        self.sends = []

    def dev(self, a=None, z=None, x=None, hi=None, c=None):
        a = self.a if a is None else a
        z = self.z if z is None else z
        x = self.x if x is None else x
        hi = self.hi if hi is None else hi
        c = self.c if c is None else c
        return (a * 16 + z * 4 + x, hi * 2 + c)

    def xp(self, s):
        return self.dev(x=lax.rem(self.x + s, 4))

    def zp(self, s):
        return self.dev(z=lax.rem(self.z + s, 4))

    def first(self, s, own):
        k = self.a if own else 1 - self.a
        return self.dev(z=lax.rem(self.z + s * k, 4), x=lax.rem(self.x + s * (1 - k), 4))

    def flip(self, da, dh):
        return self.dev(a=1 - self.a if da else None, hi=1 - self.hi if dh else None)

    def ring(self, s):
        a, hi = self.a, self.hi
        k = a if s == 1 else 1 - a
        return (a, 1 - hi) if s == 2 else (1 - a, hi + k - 2 * hi * k)

    def yp(self, s):
        a, hi = self.ring(s)
        return self.dev(a=a, hi=hi)

    def sib(self):
        return self.dev(c=1 - self.c)

    def hello(self, peers):
        bar = pltpu.get_barrier_semaphore()
        for p in peers:
            pl.semaphore_signal(bar, inc=1, device_id=p, device_id_type=MESH)

    def met(self, peers):
        pl.semaphore_wait(pltpu.get_barrier_semaphore(), len(peers))

    def greet(self, peers):
        self.hello(peers)
        self.met(peers)

    def put(self, src, dst, dev):
        i = self.n
        self.n += 1
        cp = pltpu.make_async_remote_copy(
            src_ref=src, dst_ref=dst, send_sem=self.send.at[i], recv_sem=self.recv.at[i],
            device_id=dev, device_id_type=MESH,
        )
        cp.start()
        self.sends.append(cp)
        return cp

    def copy(self, src, dst):
        i = self.m
        self.m += 1
        cp = pltpu.make_async_copy(src, dst, self.loc.at[i])
        cp.start()
        return cp

    def drop(self, cp):
        self.sends = [s for s in self.sends if s is not cp]

    def finish(self):
        assert self.n <= self.send.shape[0] and self.m <= self.loc.shape[0]
        for cp in self.sends:
            cp.wait_send()


FLIP8 = ((1, 0), (1, 1), (0, 1))
ORDER = (1, 3, 2)


def sems(n, m):
    return [pltpu.SemaphoreType.DMA((n,)), pltpu.SemaphoreType.DMA((n,)), pltpu.SemaphoreType.DMA((m,))]


def all_peers(net):
    return (
        [net.xp(s) for s in ORDER]
        + [net.zp(s) for s in ORDER]
        + [net.sib()]
        + [net.flip(*f) for f in FLIP8]
    )


def rms_unit(u):
    return lax.rsqrt(jnp.mean(u * u, -1, keepdims=True) + EPSILON)


def add_to(dst, terms, rows, step=32):
    @pl.loop(0, rows // step)
    def _(i):
        sl = pl.ds(pl.multiple_of(i * step, step), step)
        total = terms[0][sl, :].astype(F32)
        for ref in terms[1:]:
            total += ref[sl, :].astype(F32)
        dst[sl, :] = total.astype(dst.dtype)


def dot(l, r, dims=((1,), (0,))):
    return lax.dot_general(l, r, (dims, ((), ())), preferred_element_type=F32)


NT = ((1,), (1,))
TN = ((0,), (0,))


def low_half(shape):
    return lax.broadcasted_iota(jnp.int32, shape, 1) < HD


def first_quarter(shape):
    lane = lax.broadcasted_iota(jnp.int32, shape, 1)
    return lax.rem(lane, HD) < HD // 2


def rot(u, cos, sin):
    near = jnp.where(first_quarter(u.shape), pltpu.roll(u, 96, 1), pltpu.roll(u, 32, 1))
    return u * cos + near * sin


def rot_back(w, cos, sin):
    y = w * sin
    near = jnp.where(first_quarter(w.shape), pltpu.roll(y, 96, 1), pltpu.roll(y, 32, 1))
    return w * cos + near


class Gather:
    def __init__(self, net, src, dst, half):
        self.net, self.dst = net, dst
        self.own = src.at[net.a] if half else src
        self.other = src.at[1 - net.a] if half else src
        self.here = dst.at[net.a, net.z, net.x]

    def local(self):
        self.lc = self.net.copy(self.own, self.here)

    def over_y(self):
        self.yc = self.net.put(self.other, self.here, self.net.flip(1, 0))

    def stage_own(self):
        self.st = [self.net.put(self.own, self.here, self.net.first(s, True)) for s in ORDER]

    def stage_other(self):
        net = self.net
        self.yc.wait_recv()
        there = self.dst.at[1 - net.a, net.z, net.x]
        self.st += [net.put(there, there, net.first(s, False)) for s in ORDER]

    def stage_two(self):
        net, dst = self.net, self.dst
        self.lc.wait()
        for cp in self.st:
            cp.wait_recv()
        z, x = net.z, net.x
        self.near = [
            (net.put(dst.at[0, z], dst.at[0, z], net.zp(s)), net.put(dst.at[1, :, x], dst.at[1, :, x], net.xp(s)))
            for s in (1, 3)
        ]

    def forward(self):
        net, dst = self.net, self.dst
        self.last = []
        for (cz, cx), s, lo in zip(self.near, (1, 3), (0, 2)):
            cz.wait_recv()
            blk = dst.at[0, lax.rem(net.z + 4 - s, 4), lo : lo + 2]
            self.last.append(net.put(blk, blk, net.zp(s)))
            cx.wait_recv()
            blk = dst.at[1, lo : lo + 2, lax.rem(net.x + 4 - s, 4)]
            self.last.append(net.put(blk, blk, net.xp(s)))

    def done(self):
        for cp in self.last:
            cp.wait_recv()


class Rows8:
    def __init__(self, net, mine, dst):
        self.net, self.dst, self.half = net, dst, mine.shape[0] // 2
        at = dst.at[net.a, net.t]
        self.up, self.down = net.put(mine, at, net.yp(1)), net.put(mine, at, net.yp(3))
        self.side = [net.put(mine, at, net.sib())]

    def at(self, s):
        a, hi = self.net.ring(s)
        return self.dst.at[a, hi * 2 + self.net.c]

    def forward(self):
        net, h = self.net, self.half
        self.last = []
        for cp, src, to, lo in ((self.up, 3, 1, 0), (self.down, 1, 3, h)):
            cp.wait_recv()
            blk = self.at(src)
            part = blk.at[lo : lo + h]
            self.last.append(net.put(part, part, net.yp(to)))
            self.side.append(net.put(blk, blk, net.sib()))

    def finish(self):
        for cp in self.last:
            cp.wait_recv()
        blk = self.at(2)
        self.side.append(self.net.put(blk, blk, self.net.sib()))

    def done(self):
        for cp in self.side:
            cp.wait_recv()


def pack_halves(dst, w):
    rest = w.shape[1] - FH
    dst[0] = w[:, :FH]
    dst[1, :, :rest] = w[:, FH:]
    dst[1, :, rest:] = jnp.zeros((w.shape[0], FH - rest), BF)


def column(row, n):
    return jnp.broadcast_to(row, (128, n)).T


def m1_body(
    tok, cot, w_q, w_k, w_v, wo, w_g, w_u, w_d, g_a, g_f, freq, seqr, blkr, posr,
    xf, mid, gains, h_xn, h_q, h_kv4, h_att, h_aq, h_ao, h_cos, h_sin, h_bias_t, cot_all, ag, au, ad,
    xn, q, kv4, att, aq, ao, cos, sin, bias_t, wq, wf, gn, tall, an, bias, ones2, part, rc, rh, send, recv, loc,
):
    net = Net(send, recv, loc)
    a, z, x, t, hi, c = net.a, net.z, net.x, net.t, net.hi, net.c
    rows, d = tok.shape
    n = 4 * rows
    nq = w_q.shape[1]
    net.hello(all_peers(net))
    lane = lax.broadcasted_iota(jnp.int32, (1, 128), 1)
    here = lax.div(lane, HD) == lax.rem(x, 2)
    gn[...] = jnp.zeros_like(gn)
    for i, g in enumerate((g_a, g_f)):
        g = g[...].astype(F32)
        gn[i : i + 1, :] = jnp.where(here, jnp.concatenate([g, g], 1), 0.0)
    wq[:, :nq] = w_q[...]
    wq[:, nq : nq + HD] = w_k[...]
    wq[:, nq + HD :] = w_v[...]
    net.met(all_peers(net))
    far, near = 1 - hi, hi
    tt = far * 2 + c
    sib, chip = net.sib(), net.flip(0, 1)
    tl = net.copy(tok, tall.at[t])
    tf = net.put(tok, tall.at[t], chip)
    ts = [net.put(tok, tall.at[t], sib)]
    gg, gq, go = Gather(net, gn, an, False), Gather(net, wq, aq, False), Gather(net, wo, ao, False)
    for g in (gg, gq, go):
        g.over_y()
        g.local()
        g.stage_own()
    cl = net.copy(cot, cot_all.at[a, t])
    for i, w in enumerate((w_g, w_u, w_d)):
        pack_halves(wf.at[i], w)
    ffn = [Gather(net, wf.at[i], o, True) for i, o in enumerate((ag, au, ad))]
    for g in ffn:
        g.local()
    for g in (gg, gq, go):
        g.stage_other()
    seq, blk = seqr[...].astype(F32), blkr[...].astype(F32)
    same = column(seq, n)[:, :1] == seq
    blkc = column(blk, n)[:, :1]
    bias[...] = jnp.where(same & (blk <= blkc), jnp.float32(0.0), jnp.float32(-1e30))
    bias_t[...] = jnp.where(same & (blkc <= blk), jnp.float32(0.0), jnp.float32(-1e30))
    for g in (gg, gq, go):
        g.stage_two()
    tf.wait_recv()
    ts.append(net.put(tall.at[tt], tall.at[tt], sib))
    for g in ffn:
        g.over_y()
    cots = Rows8(net, cot, cot_all)
    angles = column(posr[...].astype(F32), n) * freq[...]
    cos[...] = jnp.cos(angles)
    sine = jnp.sin(angles)
    sin[...] = jnp.where(first_quarter(sine.shape), -sine, sine)
    tl.wait()
    for cp in ts:
        cp.wait_recv()
    gg.forward()
    gq.forward()
    out = [net.copy(*p) for p in ((bias_t, h_bias_t), (cos, h_cos), (sin, h_sin))]
    gg.done()
    for i in range(16):
        k = 2 * i
        pair = an[k // 16, k // 4 % 4, k % 4] + an[k // 16, k // 4 % 4, k % 4 + 1]
        gains[:, 128 * i : 128 * i + 128] = pair
    step = 32

    @pl.loop(0, n // step)
    def _(i):
        b = lax.div(i, rows // step)
        u = tall[b, pl.ds(pl.multiple_of(lax.rem(i, rows // step) * step, step), step), :].astype(F32)
        xn[pl.ds(pl.multiple_of(i * step, step), step), :] = (u * rms_unit(u) * gains[0:1, :]).astype(BF)

    go.forward()
    gq.done()
    for g in ffn:
        g.stage_own()
    scale = 1.0 / math.sqrt(HD)
    for lo, width in ((0, 256), (256, 256), (512, 128)):
        w = aq[:, :, :, :, lo : lo + width].reshape(d, width)
        val = dot(xn[...], w)
        if lo < 512:
            for i in range(2):
                at = lo + 128 * i
                q[:, at : at + 128] = (rot(val[:, 128 * i : 128 * i + 128], cos[...], sin[...]) * scale).astype(BF)
        else:
            low = low_half(val.shape)
            ke = jnp.where(low, rot(val, cos[...], sin[...]), 0.0)
            vo = jnp.where(low, 0.0, val)
            ve = pltpu.roll(vo, 64, 1)
            kv4[0] = ke.astype(BF)
            kv4[1] = pltpu.roll(ke, 64, 1).astype(BF)
            kv4[2] = ve.astype(BF)
            kv4[3] = vo.astype(BF)
            ones2[0] = jnp.where(low, ve, 1.0).astype(BF)
            ones2[1] = jnp.where(low, 1.0, vo).astype(BF)
    for g in ffn:
        g.stage_other()

    @pl.loop(0, 4)
    def _(j):
        ln = pl.ds(pl.multiple_of(j * 128, 128), 128)
        qp = q[:, ln]
        low = low_half((n, 128))
        o = []
        for h in range(2):
            s = dot(qp, kv4[h], NT) + bias[...]
            e = jnp.exp(s - jnp.max(s, -1, keepdims=True)).astype(BF)
            o.append(dot(e, ones2[h]))
        total = jnp.where(low, pltpu.roll(o[0], 64, 1), pltpu.roll(o[1], 64, 1))
        att[:, ln] = (jnp.where(low, o[0], o[1]) / total).astype(BF)

    go.done()
    for i in range(4):
        w = ao[i // 2, 2 * (i % 2) : 2 * (i % 2) + 2].reshape(512, 512)
        part[:, :, 512 * i : 512 * i + 512] = dot(att[...], w, NT).reshape(4, rows, 512).astype(BF)
    out += [
        net.copy(*p)
        for p in ((xn, h_xn), (q, h_q), (kv4, h_kv4), (att, h_att), (aq, h_aq), (ao, h_ao))
    ]
    cc = [net.put(part.at[h * 2 + (1 - c)], rc.at[i], sib) for i, h in enumerate((far, near))]
    for g in ffn:
        g.stage_two()
    cc[0].wait_recv()
    pf = part.at[far * 2 + c]
    add_to(pf, [pf, rc.at[0]], rows)
    ch = net.put(pf, rh, chip)
    cots.forward()
    cc[1].wait_recv()
    ch.wait_recv()
    ffn[0].forward()
    mine_part = part.at[near * 2 + c]

    @pl.loop(0, rows // step)
    def _(i):
        sl = pl.ds(pl.multiple_of(i * step, step), step)
        m = (
            tall[t, sl, :].astype(F32)
            + (mine_part[sl, :].astype(F32) + rc[1, sl, :].astype(F32))
            + rh[sl, :].astype(F32)
        )
        mid[sl, :] = m
        xf[a, t, sl, :] = (m * rms_unit(m) * gains[1:2, :]).astype(BF)

    mine = xf.at[a, t]
    rows8 = Rows8(net, mine, xf)
    cots.finish()
    ffn[1].forward()
    rows8.forward()
    ffn[2].forward()
    rows8.finish()
    for cp in [cl] + out:
        cp.wait()
    for g in ffn:
        g.done()
    cots.done()
    rows8.done()
    net.finish()


def m1(tok, cot, weights, g_a, g_f, seq, blk, pos):
    rows, d = tok.shape
    n = 4 * rows
    sd = jax.ShapeDtypeStruct
    v = pltpu.VMEM
    row = lambda u: u.reshape(1, n)
    freq = 1.0 / ROPE_BASE ** (np.arange(HD // 2, dtype=np.float32) * 2.0 / HD)
    freq = jnp.asarray(np.tile(freq, 4)[None], F32)
    ffn = [sd((2, 4, 4, 64, FH), BF)] * 3
    kept = [
        ((n, d), BF), ((n, 512), BF), ((4, n, 128), BF), ((n, 512), BF), ((2, 4, 4, 64, 640), BF),
        ((2, 4, 4, 64, 512), BF), ((n, 128), F32), ((n, 128), F32), ((n, n), F32),
    ]
    return pl.pallas_call(
        m1_body,
        out_shape=[sd((2, 4, rows, d), BF), sd((rows, d), F32), sd((8, d), F32)]
        + [sd(*k) for k in kept] + [sd((2, 4, rows, d), BF)] + ffn,
        in_specs=[ANY] * 2 + [VM] * 13,
        out_specs=[VM] * 3 + [ANY] * 13,
        scratch_shapes=[v(*k) for k in kept] + [
            v((64, 640), BF), v((3, 2, 64, FH), BF), v((8, 128), F32),
            v((4, rows, d), BF), v((2, 4, 4, 8, 128), F32), v((n, n), F32),
            v((2, n, 128), BF), v((4, rows, d), BF), v((2, rows, d), BF), v((rows, d), BF),
        ] + sems(124, 24),
        compiler_params=pltpu.CompilerParams(collective_id=1, has_side_effects=True, vmem_limit_bytes=56 << 20),
        name="attention_forward",
    )(tok, cot, *weights, g_a, g_f, freq, row(seq), row(blk), row(pos))


class Sum8:
    def __init__(self, net, part, ploc, rc, thru, ry):
        self.net, self.ploc, self.rc, self.thru, self.ry = net, ploc, rc, thru, ry
        c = net.c
        chips = [net.ring(s) for s in (2, 1, 3)] + [(net.a, net.hi)]
        self.cc = [net.put(part.at[b, h * 2 + (1 - c)], rc.at[i], net.sib()) for i, (b, h) in enumerate(chips)]
        self.lc = [net.copy(part.at[b, h * 2 + c], ploc.at[i]) for i, (b, h) in enumerate(chips)]

    def send(self):
        net, ploc, thru, ry = self.net, self.ploc, self.thru, self.ry
        rows = ploc.shape[1]
        h = rows // 2

        def ready(i):
            self.lc[i].wait()
            self.cc[i].wait_recv()
            if i < 3:
                add_to(ploc.at[i], [ploc.at[i], self.rc.at[i]], rows)

        ready(0)
        self.far = [
            net.put(ploc.at[0, 0:h], thru.at[0], net.yp(1)), net.put(ploc.at[0, h:rows], thru.at[1], net.yp(3)),
        ]
        ready(1)
        self.near = [net.put(ploc.at[1, h:rows], ry.at[0, h:rows], net.yp(1))]
        ready(2)
        self.near.append(net.put(ploc.at[2, 0:h], ry.at[1, 0:h], net.yp(3)))
        ready(3)

    def mid(self):
        net, ploc, thru, ry = self.net, self.ploc, self.thru, self.ry
        h = ploc.shape[1] // 2
        for k, (to, lo) in enumerate(((1, 0), (3, h))):
            self.far[k].wait_recv()
            part = ploc.at[1 + k, lo : lo + h]
            add_to(part, [part, thru.at[k]], h)
            self.near.append(net.put(part, ry.at[k, lo : lo + h], net.yp(to)))

    def arrived(self):
        for cp in self.near:
            cp.wait_recv()

    def drained(self):
        for cp in self.far + self.near:
            cp.wait_send()
            self.net.drop(cp)

    def rows(self, sl):
        total = self.ploc[3, sl, :].astype(F32) + self.rc[3, sl, :].astype(F32)
        for j in range(2):
            total += self.ry[j, sl, :].astype(F32)
        return total


def norm_back(u, g, gain):
    r = rms_unit(u)
    unit = u * r
    gvec = g * gain
    return r * (gvec - unit * jnp.mean(gvec * unit, -1, keepdims=True))


class Scatter:
    def __init__(self, net, part, thru, r1, r2, loc=None):
        self.net, self.part, self.thru, self.r1, self.r2, self.loc = net, part, thru, r1, r2, loc

    def block(self, h, s):
        p, net = self.part, self.net
        if h == 0:
            zz = lax.rem(net.z + s, 4)
            return lambda lo, hi: p.at[0, zz, lo:hi]
        xx = lax.rem(net.x + s, 4)
        return lambda lo, hi: p.at[1, lo:hi, xx]

    def stage_one(self):
        net, r1, thru = self.net, self.r1, self.thru
        self.got, self.lc, self.add = [], [], []
        for h in range(2):
            to = net.zp if h == 0 else net.xp
            far, up, down, own = (self.block(h, s) for s in (2, 1, 3, 0))
            self.got.append([
                net.put(far(0, 2), thru.at[h, 0], to(1)), net.put(far(2, 4), thru.at[h, 1], to(3)),
                net.put(up(2, 4), r1.at[h, 0, 2:4], to(1)), net.put(down(0, 2), r1.at[h, 1, 0:2], to(3)),
            ])
            if self.loc is None:
                self.lc.append([])
                self.add.append((up(0, 2), down(2, 4), own(0, 4)))
            else:
                l = self.loc
                self.add.append((l.at[h, 0:2], l.at[h, 2:4], l.at[h, 4:8]))
                self.lc.append([net.copy(f, t) for f, t in zip((up(0, 2), down(2, 4), own(0, 4)), self.add[h])])

    def stage_mid(self):
        net, r1, thru = self.net, self.r1, self.thru
        self.more = []
        for h in range(2):
            to = net.zp if h == 0 else net.xp
            for cp in self.lc[h]:
                cp.wait()
            for k, s in enumerate((1, 3)):
                self.got[h][k].wait_recv()
                for b in range(2):
                    t = thru.at[h, k, b]
                    add_to(t, [t, self.add[h][k].at[b]], 64)
                self.more.append(net.put(thru.at[h, k], r1.at[h, k, 2 * k : 2 * k + 2], to(s)))

    def stage_two(self):
        net, r1, r2 = self.net, self.r1, self.r2
        self.nxt = []
        for h in range(2):
            for cp in self.got[h][2:] + self.more[2 * h : 2 * h + 2]:
                cp.wait_recv()
            for b in range(4):
                dst = r1.at[h, 0, b]
                add_to(dst, [self.add[h][2].at[b], dst, r1.at[h, 1, b]], 64)
            me = net.x if h == 0 else net.z
            self.nxt.append([
                net.put(r1.at[h, 0, lax.rem(me + s, 4)], r2.at[h, k], net.xp(s) if h == 0 else net.zp(s))
                for k, s in enumerate(ORDER)
            ])

    def stage_y(self, dst):
        net, r1, r2 = self.net, self.r1, self.r2
        for h in range(2):
            for cp in self.nxt[h]:
                cp.wait_recv()
            me = net.x if h == 0 else net.z
            add_to(r2.at[h, 0], [r1.at[h, 0, me]] + [r2.at[h, k] for k in range(3)], 64)
        self.yc = net.put(r2.at[1 - net.a, 0], dst, net.flip(1, 0))


def weight_grads(left, pairs, chunk, stage, csem, ssem):
    n = len(pairs)

    def load(i, k):
        sl = pl.ds(pl.multiple_of(i * 256, 256), 256)
        return pltpu.make_async_copy(left.at[:, sl], chunk.at[k], csem.at[k])

    def save(i, w, k):
        return pltpu.make_async_copy(stage.at[k], pairs[w][1].at[lax.div(i, 4), lax.rem(i, 4)], ssem.at[k])

    for i in range(3):
        load(i, i).start()

    @pl.loop(0, 2)
    def _(j):
        for k in range(4):
            i = 4 * j + k
            load(i, k).wait()
            if k == 0:
                load(i + 3, 3).start()
            else:

                @pl.when(j < 1)
                def _():
                    load(i + 3, k - 1).start()

            for w in range(n):
                slot = n * (k % 2) + w
                if k > 1:
                    save(i - 2, w, slot).wait()
                else:

                    @pl.when(j > 0)
                    def _():
                        save(i - 2, w, slot).wait()

                stage[slot] = dot(chunk[k], pairs[w][0][...], TN).reshape(4, 64, FH).astype(BF)
                save(i, w, slot).start()

    for i in (6, 7):
        for w in range(n):
            save(i, w, n * (i % 2) + w).wait()


SOON = ("hid", "dgate", "dup")
LATE = SOON + ("xn", "q", "kv4", "att", "wq", "wo", "cos", "sin", "bias", "tok", "w_q", "w_k", "w_v", "w_g", "w_u")


def m3_body(names, *refs):
    r = dict(zip(names, refs))
    net = Net(r["send"], r["recv"], r["loc"])
    a, z, x, t, hi, c = net.a, net.z, net.x, net.t, net.hi, net.c
    diag = net.dev(hi=1 - net.hi, c=1 - net.c)
    net.greet(all_peers(net) + [diag])
    mid, cot, tok, gains = r["mid"], r["cot"], r["tok"], r["gains"]
    rows, d = cot.shape
    n = 4 * rows
    step = 32
    far, near = 1 - hi, hi
    sib, chip = net.sib(), net.flip(0, 1)
    bl, bc, bt, by = r["bl"], r["bc"], r["bt"], r["by"]
    late = [net.copy(r["h_" + k], r[k]) for k in LATE if k not in SOON]
    soon = [net.copy(r["h_" + k], r[k]) for k in SOON]
    back = Sum8(net, r["fback"], bl, bc, bt, by)
    bias = r["bias"]
    ffn = [Scatter(net, r["p" + k], r["t" + k], r["r1" + k], r["r2" + k], r["l" + k]) for k in "dgu"]
    work = (r["chunk"], r["stage"], r["csem"], r["ssem"])
    soon[0].wait()
    weight_grads(r["call"], [(r["hid"], r["pd"])], *work)
    back.send()
    ffn[0].stage_one()
    soon[1].wait()
    soon[2].wait()
    weight_grads(r["xf"], [(r["dgate"], r["pg"]), (r["dup"], r["pu"])], *work)
    back.mid()
    ffn[1].stage_one()
    ffn[2].stage_one()
    back.arrived()
    gm, gmid = r["gm"], r["gmid"]

    @pl.loop(0, rows // step)
    def _(i):
        sl = pl.ds(pl.multiple_of(i * step, step), step)
        g = back.rows(sl)
        m = cot[sl, :].astype(F32) + norm_back(mid[sl, :], g, gains[1:2, :])
        gmid[sl, :] = m
        gm[t, sl, :] = m.astype(BF)

    free = r["free"]
    for s in (1, 3):
        pl.semaphore_signal(free, inc=1, device_id=net.yp(s), device_id_type=MESH)
    mine = gm.at[t]
    mf = net.put(mine, mine, chip)
    ms = [net.put(mine, mine, sib)]
    ffn[0].stage_mid()
    ms[0].wait_recv()
    back.drained()
    fwd = Sum8(net, r["fout"], bl, bc, bt, by)
    pl.semaphore_wait(free, 2)
    mf.wait_recv()
    theirs = gm.at[far * 2 + c]
    ms.append(net.put(theirs, theirs, sib))
    fwd.send()
    ffn[1].stage_mid()
    ms[1].wait_recv()
    for cp in late:
        cp.wait()
    gatt, att, q, kv4, wq, wo = r["gatt"], r["att"], r["q"], r["kv4"], r["wq"], r["wo"]
    for i in range(2):
        w = wo[:, :, :, :, 256 * i : 256 * i + 256].reshape(d, 256)
        gatt[:, 256 * i : 256 * i + 256] = dot(gm[...].reshape(n, d), w).astype(BF)
    po, pq, xn, dqkv = r["po"], r["pq"], r["xn"], r["dqkv"]

    @pl.loop(0, 8)
    def _(i):
        ln = pl.ds(pl.multiple_of(i * 256, 256), 256)
        left = gm[:, :, ln].reshape(n, 256)
        po[lax.div(i, 4), lax.rem(i, 4)] = dot(left, att[...], TN).reshape(4, 64, 512).astype(BF)

    so = Scatter(net, po, r["to"], r["r1o"], r["r2o"])
    so.stage_one()
    ffn[2].stage_mid()
    ak, av = r["ak"], r["av"]
    ak[...] = jnp.zeros_like(ak)
    av[...] = jnp.zeros_like(av)
    cos, sin = r["cos"], r["sin"]
    low = low_half((n, 128))
    scale = 1.0 / math.sqrt(HD)

    def pair(j):
        ln = pl.ds(pl.multiple_of(j * 128, 128), 128)
        qp, gp = q[:, ln], gatt[:, ln]
        cv, ck, gq = [], [], None
        for h in range(2):
            s = dot(kv4[h], qp, NT) + bias[...]
            e = jnp.exp(s - jnp.max(s, 0, keepdims=True))
            p = e * (1.0 / jnp.sum(e, 0, keepdims=True))
            pg = p * dot(kv4[2 + h], gp, NT)
            graw = (pg - p * jnp.sum(pg, 0, keepdims=True)).astype(BF)
            cv.append(dot(p.astype(BF), gp))
            ck.append(dot(graw, qp))
            term = dot(kv4[h], graw, TN)
            gq = term if gq is None else gq + term
        av[...] += jnp.where(low, cv[0], cv[1])
        ak[...] += jnp.where(low, ck[0], ck[1])
        dqkv[:, ln] = (rot_back(gq.T, cos[...], sin[...]) * scale).astype(BF)

    pl.loop(0, 2)(pair)
    fwd.mid()
    ffn[0].stage_two()
    ffn[1].stage_two()
    so.stage_mid()
    pl.loop(2, 4)(pair)
    tk = ak[...] + pltpu.roll(ak[...], 64, 1)
    tv = av[...] + pltpu.roll(av[...], 64, 1)
    dqkv[:, 512:640] = jnp.where(low, rot_back(tk, cos[...], sin[...]), tv).astype(BF)

    ap, arc, arh = r["ap"], r["arc"], r["arh"]
    for i in range(4):
        w = wq[i // 2, 2 * (i % 2) : 2 * (i % 2) + 2].reshape(512, 640)
        ap[:, :, 512 * i : 512 * i + 512] = dot(dqkv[...], w, NT).reshape(4, rows, 512).astype(BF)
    acc = [net.put(ap.at[h * 2 + (1 - c)], arc.at[i], sib) for i, h in enumerate((far, near))]

    @pl.loop(0, 8)
    def _(i):
        ln = pl.ds(pl.multiple_of(i * 256, 256), 256)
        pq[lax.div(i, 4), lax.rem(i, 4)] = dot(xn[:, ln], dqkv[...], TN).reshape(4, 64, 640).astype(BF)

    sq = Scatter(net, pq, r["tq"], r["r1q"], r["r2q"])
    sq.stage_one()
    acc[0].wait_recv()
    af = ap.at[far * 2 + c]
    add_to(af, [af, arc.at[0]], rows)
    ach = net.put(af, arh, chip)
    ffn[2].stage_two()
    sq.stage_mid()
    so.stage_two()
    for sc, k in zip(ffn, "dgu"):
        o = r["y" + k]
        sc.stage_y(o.at[a])
        o[a] = sc.r2[a, 0]
    fwd.arrived()
    res, gtok = r["res"], r["gtok"]

    @pl.loop(0, rows // step)
    def _(i):
        sl = pl.ds(pl.multiple_of(i * step, step), step)
        g = fwd.rows(sl)
        res[sl, :] = (mid[sl, :] + g).astype(BF)

    dg = r["dg"]
    for sc in ffn:
        sc.yc.wait_recv()
    tot = jnp.zeros((64, 128), F32)
    for k in "gu":
        y, w = r["y" + k], r["w_" + k]
        for i in range(w.shape[1] // 128):
            lo, half = 128 * i % FH, 128 * i // FH
            tot += y[half, :, lo : lo + 128].astype(F32) * w[:, 128 * i : 128 * i + 128].astype(F32)
    dg[1] = tot
    sq.stage_two()
    so.stage_y(r["yo"])
    acc[1].wait_recv()
    ach.wait_recv()
    an = ap.at[near * 2 + c]

    @pl.loop(0, rows // step)
    def _(i):
        sl = pl.ds(pl.multiple_of(i * step, step), step)
        g = an[sl, :].astype(F32) + arc[1, sl, :].astype(F32) + arh[sl, :].astype(F32)
        gtok[sl, :] = (gmid[sl, :] + norm_back(tok[sl, :].astype(F32), g, gains[0:1, :])).astype(BF)

    sq.stage_y(r["yq"])
    so.yc.wait_recv()
    add_to(r["oo"], [so.r2.at[a, 0], r["yo"]], 64)
    sq.yc.wait_recv()
    dw = sq.r2[a, 0].astype(F32) + r["yq"][...].astype(F32)
    nq = r["oq"].shape[1]
    dk, dv = dw[:, nq : nq + HD], dw[:, nq + HD :]
    r["oq"][...] = dw[:, :nq]
    r["ok"][...] = dk
    r["ov"][...] = dv
    tot = jnp.zeros((64, 128), F32)
    for i in range(nq // 128):
        sl = slice(128 * i, 128 * i + 128)
        tot += dw[:, sl] * r["w_q"][:, sl].astype(F32)
    small = dk * r["w_k"][...].astype(F32) + dv * r["w_v"][...].astype(F32)
    dg[0] = tot + jnp.concatenate([small, jnp.zeros_like(small)], 1)
    dy = r["dy"]
    sums = [net.put(dg, dy.at[at], peer) for at, peer in enumerate((sib, chip, diag))]
    for cp in sums:
        cp.wait_recv()
    for i, (o, g) in enumerate((("dg1", "g_a"), ("dg2", "g_f"))):
        r[o][...] = jnp.sum((dg[i] + dy[0, i] + dy[1, i] + dy[2, i]).T, 0, keepdims=True) / r[g][...].astype(F32)
    net.finish()


def m3(hbm, vmem, shapes):
    rows, d = shapes
    n = 4 * rows
    sd = jax.ShapeDtypeStruct
    v = pltpu.VMEM
    part = (2, 4, 4, 64, FH)
    outs = dict(
        yg=sd((2, 64, FH), BF), yu=sd((2, 64, FH), BF), yd=sd((2, 64, FH), BF), oo=sd((64, 512), F32),
        oq=sd((64, 512), F32), ok=sd((64, HD), F32), ov=sd((64, HD), F32),
        res=sd((rows, d), BF), gtok=sd((rows, d), BF), dg1=sd((1, 64), F32), dg2=sd((1, 64), F32),
        pg=sd(part, BF), pu=sd(part, BF), pd=sd(part, BF),
    )
    scr = dict(
        bl=v((4, rows, d), BF), bc=v((4, rows, d), BF), by=v((2, rows, d), BF), bt=v((2, rows // 2, d), BF),
        gm=v((4, rows, d), BF), gmid=v((rows, d), F32), gatt=v((n, 512), BF),
        dqkv=v((n, 640), BF), ak=v((n, 128), F32), av=v((n, 128), F32),
        po=v((2, 4, 4, 64, 512), BF), pq=v((2, 4, 4, 64, 640), BF),
        ap=v((4, rows, d), BF), arc=v((2, rows, d), BF), arh=v((rows, d), BF),
        yo=v((64, 512), BF), yq=v((64, 640), BF), dg=v((2, 64, 128), F32), dy=v((3, 2, 64, 128), F32),
        chunk=v((4, 2 * n, 256), BF), stage=v((4, 4, 64, FH), BF),
        csem=pltpu.SemaphoreType.DMA((4,)), ssem=pltpu.SemaphoreType.DMA((4,)), free=pltpu.SemaphoreType.REGULAR,
    )
    for k, w in (("g", FH), ("u", FH), ("d", FH), ("o", 512), ("q", 640)):
        scr["t" + k] = v((2, 2, 2, 64, w), BF)
        scr["r1" + k] = v((2, 2, 4, 64, w), BF)
        scr["r2" + k] = v((2, 3, 64, w), BF)
    for k in "gud":
        scr["l" + k] = v((2, 8, 64, FH), BF)
    sem = sems(132, 56)
    for k in LATE:
        u = vmem.pop(k)
        hbm["h_" + k] = u
        scr[k] = v(u.shape, u.dtype)
    names = list(hbm) + list(vmem) + list(outs) + list(scr) + ["send", "recv", "loc"]
    got = pl.pallas_call(
        functools.partial(m3_body, names),
        out_shape=list(outs.values()),
        in_specs=[ANY] * len(hbm) + [VM] * len(vmem),
        out_specs=[VM] * (len(outs) - 3) + [ANY] * 3,
        scratch_shapes=list(scr.values()) + sem,
        compiler_params=pltpu.CompilerParams(collective_id=3, has_side_effects=True, vmem_limit_bytes=62 << 20),
        name="attention_backward",
    )(*hbm.values(), *vmem.values())
    return dict(zip(outs, got))


def mm(l, r, dims=((1,), (0,))):
    return lax.dot_general(l, r, (dims, ((), ())), preferred_element_type=F32)


def final_body(yg, yu, yd, *refs):
    k = (len(refs) - 3) // 2
    for y, o in zip((yg, yu, yd), refs[k : k + 3]):
        rest = o.shape[1] - FH
        o[:, :FH] = y[0].astype(F32)
        o[:, FH:] = y[1, :, :rest].astype(F32)
    for i, o in zip(refs[:k], refs[k + 3 :]):
        o[...] = i[...]


def final(halves, others, ff):
    sd = jax.ShapeDtypeStruct
    return pl.pallas_call(
        final_body,
        out_shape=[sd((64, ff), F32)] * 3 + [sd(o.shape, o.dtype) for o in others],
        in_specs=[VM] * (3 + len(others)),
        out_specs=[VM] * (3 + len(others)),
        name="final",
    )(*halves, *others)


def per_device(
    tokens_in, cotangent, seq_ids, block_ids, positions, attn_gain, ffn_gain,
    w_query, w_key, w_value, w_out, w_gate, w_up, w_down,
):
    rows, d = tokens_in.shape
    n = seq_ids.shape[0]
    weights = (w_query, w_key, w_value, w_out.T, w_gate, w_up, w_down.T)
    g_a, g_f = attn_gain.reshape(1, -1), ffn_gain.reshape(1, -1)
    xf, mid, gains, xn, q, kv4, att, wqkv, wot, cos, sin, bias_t, cot, wg, wu, wdt = m1(
        tokens_in, cotangent, weights, g_a, g_f, seq_ids, block_ids, positions
    )
    cot = cot.reshape(2 * n, d)
    wg, wu, wdt = (w.reshape(d, FH) for w in (wg, wu, wdt))
    xf = xf.reshape(2 * n, d)
    gate = mm(xf, wg)
    up = mm(xf, wu)
    sig = jax.nn.sigmoid(gate)
    silu = gate * sig
    hid = (silu * up).astype(BF)
    gh = mm(cot, wdt)
    dgate = (gh * up * (sig * (1.0 + gate * (1.0 - sig)))).astype(BF)
    dup = (gh * silu).astype(BF)
    fback = (mm(dgate, wg, NT) + mm(dup, wu, NT)).astype(BF).reshape(2, 4, rows, d)
    fout = mm(hid, wdt, NT).astype(BF).reshape(2, 4, rows, d)
    out = m3(
        dict(fback=fback, fout=fout, xf=xf, call=cot),
        dict(
            hid=hid, dgate=dgate, dup=dup, mid=mid, cot=cotangent, tok=tokens_in, gains=gains, xn=xn, q=q, kv4=kv4,
            att=att, wq=wqkv, wo=wot, cos=cos, sin=sin, bias=bias_t,
            w_q=w_query, w_k=w_key, w_v=w_value, w_g=w_gate, w_u=w_up, g_a=g_a, g_f=g_f,
        ),
        (rows, d),
    )
    keep = ("res", "gtok", "dg1", "dg2", "oq", "ok", "ov", "oo")
    og, ou, od, res, gtok, dg1, dg2, oq, ok, ov, oo = final(
        [out[k] for k in ("yg", "yu", "yd")], [out[k] for k in keep], w_gate.shape[1]
    )
    return (res, gtok, dg1.reshape(-1), dg2.reshape(-1), oq, ok, ov, oo.T, og, ou, od.T)


def solution(mesh):
    both, dp, cols, rows = P(("dp", "tensor"), None), P("dp"), P("dp", "tensor"), P("tensor", "dp")
    return jax.shard_map(
        per_device,
        mesh=mesh,
        in_specs=(both, both, dp, dp, dp, dp, dp, cols, cols, cols, rows, cols, cols, rows),
        out_specs=(both, both, dp, dp, cols, cols, cols, rows, cols, cols, rows),
        check_vma=False,
    )
```

```python
import functools
import math

import jax
import jax.numpy as jnp
import numpy as np
from jax import lax
from jax.experimental import pallas as pl
from jax.experimental.pallas import tpu as pltpu
from jax.sharding import PartitionSpec as P

HD = 64
EPSILON = 1e-05
ROPE_BASE = 10000.0
MESH = pl.DeviceIdType.MESH
BF = jnp.bfloat16
F32 = jnp.float32
ANY = pl.BlockSpec(memory_space=pl.ANY)
VM = pl.BlockSpec(memory_space=pltpu.VMEM)
FH = 768


class Net:
    def __init__(self, send, recv, loc):
        self.send, self.recv, self.loc = send, recv, loc
        self.n = self.m = 0
        dp, t = lax.axis_index("dp"), lax.axis_index("tensor")
        self.a = lax.div(dp, 16)
        self.z = lax.rem(lax.div(dp, 4), 4)
        self.x = lax.rem(dp, 4)
        self.hi = lax.div(t, 2)
        self.c = lax.rem(t, 2)
        self.t = t
        self.sends = []

    def dev(self, a=None, z=None, x=None, hi=None, c=None):
        a = self.a if a is None else a
        z = self.z if z is None else z
        x = self.x if x is None else x
        hi = self.hi if hi is None else hi
        c = self.c if c is None else c
        return (a * 16 + z * 4 + x, hi * 2 + c)

    def xp(self, s):
        return self.dev(x=lax.rem(self.x + s, 4))

    def zp(self, s):
        return self.dev(z=lax.rem(self.z + s, 4))

    def first(self, s, own):
        k = self.a if own else 1 - self.a
        return self.dev(z=lax.rem(self.z + s * k, 4), x=lax.rem(self.x + s * (1 - k), 4))

    def flip(self, da, dh):
        return self.dev(a=1 - self.a if da else None, hi=1 - self.hi if dh else None)

    def ring(self, s):
        a, hi = self.a, self.hi
        k = a if s == 1 else 1 - a
        return (a, 1 - hi) if s == 2 else (1 - a, hi + k - 2 * hi * k)

    def yp(self, s):
        a, hi = self.ring(s)
        return self.dev(a=a, hi=hi)

    def sib(self):
        return self.dev(c=1 - self.c)

    def hello(self, peers):
        bar = pltpu.get_barrier_semaphore()
        for p in peers:
            pl.semaphore_signal(bar, inc=1, device_id=p, device_id_type=MESH)

    def met(self, peers):
        pl.semaphore_wait(pltpu.get_barrier_semaphore(), len(peers))

    def greet(self, peers):
        self.hello(peers)
        self.met(peers)

    def put(self, src, dst, dev):
        i = self.n
        self.n += 1
        cp = pltpu.make_async_remote_copy(
            src_ref=src, dst_ref=dst, send_sem=self.send.at[i], recv_sem=self.recv.at[i],
            device_id=dev, device_id_type=MESH,
        )
        cp.start()
        self.sends.append(cp)
        return cp

    def copy(self, src, dst):
        i = self.m
        self.m += 1
        cp = pltpu.make_async_copy(src, dst, self.loc.at[i])
        cp.start()
        return cp

    def drop(self, cp):
        self.sends = [s for s in self.sends if s is not cp]

    def finish(self):
        assert self.n <= self.send.shape[0] and self.m <= self.loc.shape[0]
        for cp in self.sends:
            cp.wait_send()


FLIP8 = ((1, 0), (1, 1), (0, 1))
ORDER = (1, 3, 2)


def sems(n, m):
    return [pltpu.SemaphoreType.DMA((n,)), pltpu.SemaphoreType.DMA((n,)), pltpu.SemaphoreType.DMA((m,))]


def all_peers(net):
    return (
        [net.xp(s) for s in ORDER]
        + [net.zp(s) for s in ORDER]
        + [net.sib()]
        + [net.flip(*f) for f in FLIP8]
    )


def rms_unit(u):
    return lax.rsqrt(jnp.mean(u * u, -1, keepdims=True) + EPSILON)


def add_to(dst, terms, rows, step=32):
    @pl.loop(0, rows // step)
    def _(i):
        sl = pl.ds(pl.multiple_of(i * step, step), step)
        total = terms[0][sl, :].astype(F32)
        for ref in terms[1:]:
            total += ref[sl, :].astype(F32)
        dst[sl, :] = total.astype(dst.dtype)


def dot(l, r, dims=((1,), (0,))):
    return lax.dot_general(l, r, (dims, ((), ())), preferred_element_type=F32)


NT = ((1,), (1,))
TN = ((0,), (0,))


def low_half(shape):
    return lax.broadcasted_iota(jnp.int32, shape, 1) < HD


def first_quarter(shape):
    lane = lax.broadcasted_iota(jnp.int32, shape, 1)
    return lax.rem(lane, HD) < HD // 2


def rot(u, cos, sin):
    near = jnp.where(first_quarter(u.shape), pltpu.roll(u, 96, 1), pltpu.roll(u, 32, 1))
    return u * cos + near * sin


def rot_back(w, cos, sin):
    y = w * sin
    near = jnp.where(first_quarter(w.shape), pltpu.roll(y, 96, 1), pltpu.roll(y, 32, 1))
    return w * cos + near


class Gather:
    def __init__(self, net, src, dst, half):
        self.net, self.dst = net, dst
        self.own = src.at[net.a] if half else src
        self.other = src.at[1 - net.a] if half else src
        self.here = dst.at[net.a, net.z, net.x]

    def local(self):
        self.lc = self.net.copy(self.own, self.here)

    def over_y(self):
        self.yc = self.net.put(self.other, self.here, self.net.flip(1, 0))

    def stage_own(self):
        self.st = [self.net.put(self.own, self.here, self.net.first(s, True)) for s in ORDER]

    def stage_other(self):
        net = self.net
        self.yc.wait_recv()
        there = self.dst.at[1 - net.a, net.z, net.x]
        self.st += [net.put(there, there, net.first(s, False)) for s in ORDER]

    def stage_two(self):
        net, dst = self.net, self.dst
        self.lc.wait()
        for cp in self.st:
            cp.wait_recv()
        z, x = net.z, net.x
        self.near = [
            (net.put(dst.at[0, z], dst.at[0, z], net.zp(s)), net.put(dst.at[1, :, x], dst.at[1, :, x], net.xp(s)))
            for s in (1, 3)
        ]

    def forward(self):
        net, dst = self.net, self.dst
        self.last = []
        for (cz, cx), s, lo in zip(self.near, (1, 3), (0, 2)):
            cz.wait_recv()
            blk = dst.at[0, lax.rem(net.z + 4 - s, 4), lo : lo + 2]
            self.last.append(net.put(blk, blk, net.zp(s)))
            cx.wait_recv()
            blk = dst.at[1, lo : lo + 2, lax.rem(net.x + 4 - s, 4)]
            self.last.append(net.put(blk, blk, net.xp(s)))

    def done(self):
        for cp in self.last:
            cp.wait_recv()


class Rows8:
    def __init__(self, net, mine, dst):
        self.net, self.dst, self.half = net, dst, mine.shape[0] // 2
        at = dst.at[net.a, net.t]
        self.up, self.down = net.put(mine, at, net.yp(1)), net.put(mine, at, net.yp(3))
        self.side = [net.put(mine, at, net.sib())]

    def at(self, s):
        a, hi = self.net.ring(s)
        return self.dst.at[a, hi * 2 + self.net.c]

    def forward(self):
        net, h = self.net, self.half
        self.last = []
        for cp, src, to, lo in ((self.up, 3, 1, 0), (self.down, 1, 3, h)):
            cp.wait_recv()
            blk = self.at(src)
            part = blk.at[lo : lo + h]
            self.last.append(net.put(part, part, net.yp(to)))
            self.side.append(net.put(blk, blk, net.sib()))

    def finish(self):
        for cp in self.last:
            cp.wait_recv()
        blk = self.at(2)
        self.side.append(self.net.put(blk, blk, self.net.sib()))

    def done(self):
        for cp in self.side:
            cp.wait_recv()


def pack_halves(dst, w):
    rest = w.shape[1] - FH
    dst[0] = w[:, :FH]
    dst[1, :, :rest] = w[:, FH:]
    dst[1, :, rest:] = jnp.zeros((w.shape[0], FH - rest), BF)


def column(row, n):
    return jnp.broadcast_to(row, (128, n)).T


def m1_body(
    tok, cot, w_q, w_k, w_v, wo, w_g, w_u, w_d, g_a, g_f, freq, seqr, blkr, posr,
    xf, mid, gains, h_xn, h_q, h_kv4, h_att, h_aq, h_ao, h_cos, h_sin, h_bias_t, cot_all, ag, au, ad,
    xn, q, kv4, att, aq, ao, cos, sin, bias_t, wq, wf, gn, tall, an, bias, ones2, part, rc, rh, send, recv, loc,
):
    net = Net(send, recv, loc)
    a, z, x, t, hi, c = net.a, net.z, net.x, net.t, net.hi, net.c
    rows, d = tok.shape
    n = 4 * rows
    nq = w_q.shape[1]
    net.hello(all_peers(net))
    lane = lax.broadcasted_iota(jnp.int32, (1, 128), 1)
    here = lax.div(lane, HD) == lax.rem(x, 2)
    gn[...] = jnp.zeros_like(gn)
    for i, g in enumerate((g_a, g_f)):
        g = g[...].astype(F32)
        gn[i : i + 1, :] = jnp.where(here, jnp.concatenate([g, g], 1), 0.0)
    wq[:, :nq] = w_q[...]
    wq[:, nq : nq + HD] = w_k[...]
    wq[:, nq + HD :] = w_v[...]
    net.met(all_peers(net))
    far, near = 1 - hi, hi
    tt = far * 2 + c
    sib, chip = net.sib(), net.flip(0, 1)
    tl = net.copy(tok, tall.at[t])
    tf = net.put(tok, tall.at[t], chip)
    ts = [net.put(tok, tall.at[t], sib)]
    gg, gq, go = Gather(net, gn, an, False), Gather(net, wq, aq, False), Gather(net, wo, ao, False)
    for g in (gg, gq, go):
        g.over_y()
        g.local()
        g.stage_own()
    cl = net.copy(cot, cot_all.at[a, t])
    for i, w in enumerate((w_g, w_u, w_d)):
        pack_halves(wf.at[i], w)
    ffn = [Gather(net, wf.at[i], o, True) for i, o in enumerate((ag, au, ad))]
    for g in ffn:
        g.local()
    for g in (gg, gq, go):
        g.stage_other()
    seq, blk = seqr[...].astype(F32), blkr[...].astype(F32)
    same = column(seq, n)[:, :1] == seq
    blkc = column(blk, n)[:, :1]
    bias[...] = jnp.where(same & (blk <= blkc), jnp.float32(0.0), jnp.float32(-1e30))
    bias_t[...] = jnp.where(same & (blkc <= blk), jnp.float32(0.0), jnp.float32(-1e30))
    for g in (gg, gq, go):
        g.stage_two()
    tf.wait_recv()
    ts.append(net.put(tall.at[tt], tall.at[tt], sib))
    for g in ffn:
        g.over_y()
    cots = Rows8(net, cot, cot_all)
    angles = column(posr[...].astype(F32), n) * freq[...]
    cos[...] = jnp.cos(angles)
    sine = jnp.sin(angles)
    sin[...] = jnp.where(first_quarter(sine.shape), -sine, sine)
    tl.wait()
    for cp in ts:
        cp.wait_recv()
    gg.forward()
    gq.forward()
    out = [net.copy(*p) for p in ((bias_t, h_bias_t), (cos, h_cos), (sin, h_sin))]
    gg.done()
    for i in range(16):
        k = 2 * i
        pair = an[k // 16, k // 4 % 4, k % 4] + an[k // 16, k // 4 % 4, k % 4 + 1]
        gains[:, 128 * i : 128 * i + 128] = pair
    step = 32

    @pl.loop(0, n // step)
    def _(i):
        b = lax.div(i, rows // step)
        u = tall[b, pl.ds(pl.multiple_of(lax.rem(i, rows // step) * step, step), step), :].astype(F32)
        xn[pl.ds(pl.multiple_of(i * step, step), step), :] = (u * rms_unit(u) * gains[0:1, :]).astype(BF)

    go.forward()
    gq.done()
    for g in ffn:
        g.stage_own()
    scale = 1.0 / math.sqrt(HD)
    for lo, width in ((0, 256), (256, 256), (512, 128)):
        w = aq[:, :, :, :, lo : lo + width].reshape(d, width)
        val = dot(xn[...], w)
        if lo < 512:
            for i in range(2):
                at = lo + 128 * i
                q[:, at : at + 128] = (rot(val[:, 128 * i : 128 * i + 128], cos[...], sin[...]) * scale).astype(BF)
        else:
            low = low_half(val.shape)
            ke = jnp.where(low, rot(val, cos[...], sin[...]), 0.0)
            vo = jnp.where(low, 0.0, val)
            ve = pltpu.roll(vo, 64, 1)
            kv4[0] = ke.astype(BF)
            kv4[1] = pltpu.roll(ke, 64, 1).astype(BF)
            kv4[2] = ve.astype(BF)
            kv4[3] = vo.astype(BF)
            ones2[0] = jnp.where(low, ve, 1.0).astype(BF)
            ones2[1] = jnp.where(low, 1.0, vo).astype(BF)
    for g in ffn:
        g.stage_other()

    @pl.loop(0, 4)
    def _(j):
        ln = pl.ds(pl.multiple_of(j * 128, 128), 128)
        qp = q[:, ln]
        low = low_half((n, 128))
        o = []
        for h in range(2):
            s = dot(qp, kv4[h], NT) + bias[...]
            e = jnp.exp(s - jnp.max(s, -1, keepdims=True)).astype(BF)
            o.append(dot(e, ones2[h]))
        total = jnp.where(low, pltpu.roll(o[0], 64, 1), pltpu.roll(o[1], 64, 1))
        att[:, ln] = (jnp.where(low, o[0], o[1]) / total).astype(BF)

    go.done()
    for i in range(4):
        w = ao[i // 2, 2 * (i % 2) : 2 * (i % 2) + 2].reshape(512, 512)
        part[:, :, 512 * i : 512 * i + 512] = dot(att[...], w, NT).reshape(4, rows, 512).astype(BF)
    out += [
        net.copy(*p)
        for p in ((xn, h_xn), (q, h_q), (kv4, h_kv4), (att, h_att), (aq, h_aq), (ao, h_ao))
    ]
    cc = [net.put(part.at[h * 2 + (1 - c)], rc.at[i], sib) for i, h in enumerate((far, near))]
    for g in ffn:
        g.stage_two()
    cc[0].wait_recv()
    pf = part.at[far * 2 + c]
    add_to(pf, [pf, rc.at[0]], rows)
    ch = net.put(pf, rh, chip)
    cots.forward()
    cc[1].wait_recv()
    ch.wait_recv()
    ffn[0].forward()
    mine_part = part.at[near * 2 + c]

    @pl.loop(0, rows // step)
    def _(i):
        sl = pl.ds(pl.multiple_of(i * step, step), step)
        m = (
            tall[t, sl, :].astype(F32)
            + (mine_part[sl, :].astype(F32) + rc[1, sl, :].astype(F32))
            + rh[sl, :].astype(F32)
        )
        mid[sl, :] = m
        xf[a, t, sl, :] = (m * rms_unit(m) * gains[1:2, :]).astype(BF)

    mine = xf.at[a, t]
    rows8 = Rows8(net, mine, xf)
    cots.finish()
    ffn[1].forward()
    rows8.forward()
    ffn[2].forward()
    rows8.finish()
    for cp in [cl] + out:
        cp.wait()
    for g in ffn:
        g.done()
    cots.done()
    rows8.done()
    net.finish()


def m1(tok, cot, weights, g_a, g_f, seq, blk, pos):
    rows, d = tok.shape
    n = 4 * rows
    sd = jax.ShapeDtypeStruct
    v = pltpu.VMEM
    row = lambda u: u.reshape(1, n)
    freq = 1.0 / ROPE_BASE ** (np.arange(HD // 2, dtype=np.float32) * 2.0 / HD)
    freq = jnp.asarray(np.tile(freq, 4)[None], F32)
    ffn = [sd((2, 4, 4, 64, FH), BF)] * 3
    kept = [
        ((n, d), BF), ((n, 512), BF), ((4, n, 128), BF), ((n, 512), BF), ((2, 4, 4, 64, 640), BF),
        ((2, 4, 4, 64, 512), BF), ((n, 128), F32), ((n, 128), F32), ((n, n), F32),
    ]
    return pl.pallas_call(
        m1_body,
        out_shape=[sd((2, 4, rows, d), BF), sd((rows, d), F32), sd((8, d), F32)]
        + [sd(*k) for k in kept] + [sd((2, 4, rows, d), BF)] + ffn,
        in_specs=[ANY] * 2 + [VM] * 13,
        out_specs=[VM] * 3 + [ANY] * 13,
        scratch_shapes=[v(*k) for k in kept] + [
            v((64, 640), BF), v((3, 2, 64, FH), BF), v((8, 128), F32),
            v((4, rows, d), BF), v((2, 4, 4, 8, 128), F32), v((n, n), F32),
            v((2, n, 128), BF), v((4, rows, d), BF), v((2, rows, d), BF), v((rows, d), BF),
        ] + sems(124, 24),
        compiler_params=pltpu.CompilerParams(collective_id=1, has_side_effects=True, vmem_limit_bytes=56 << 20),
        name="attention_forward",
    )(tok, cot, *weights, g_a, g_f, freq, row(seq), row(blk), row(pos))


def add_blocks(dst, terms, blocks):
    @pl.loop(0, blocks)
    def _(b):
        total = terms[0][b].astype(F32)
        for ref in terms[1:]:
            total += ref[b].astype(F32)
        dst[b] = total.astype(dst.dtype)


class Sum8:
    def __init__(self, net, part, ploc, rc, thru, ry):
        self.net, self.ploc, self.rc, self.thru, self.ry = net, ploc, rc, thru, ry
        c = net.c
        chips = [net.ring(s) for s in (2, 1, 3)] + [(net.a, net.hi)]
        self.cc = [net.put(part.at[b, h * 2 + (1 - c)], rc.at[i], net.sib()) for i, (b, h) in enumerate(chips)]
        self.lc = [net.copy(part.at[b, h * 2 + c], ploc.at[i]) for i, (b, h) in enumerate(chips)]

    def send(self):
        net, ploc, thru, ry = self.net, self.ploc, self.thru, self.ry
        rows = ploc.shape[1]
        h = rows // 2

        def ready(i):
            self.lc[i].wait()
            self.cc[i].wait_recv()
            if i < 3:
                add_to(ploc.at[i], [ploc.at[i], self.rc.at[i]], rows)

        ready(0)
        self.far = [
            net.put(ploc.at[0, 0:h], thru.at[0], net.yp(1)), net.put(ploc.at[0, h:rows], thru.at[1], net.yp(3)),
        ]
        ready(1)
        self.near = [net.put(ploc.at[1, h:rows], ry.at[0, h:rows], net.yp(1))]
        ready(2)
        self.near.append(net.put(ploc.at[2, 0:h], ry.at[1, 0:h], net.yp(3)))
        ready(3)

    def mid(self):
        net, ploc, thru, ry = self.net, self.ploc, self.thru, self.ry
        h = ploc.shape[1] // 2
        for k, (to, lo) in enumerate(((1, 0), (3, h))):
            self.far[k].wait_recv()
            part = ploc.at[1 + k, lo : lo + h]
            add_to(part, [part, thru.at[k]], h)
            self.near.append(net.put(part, ry.at[k, lo : lo + h], net.yp(to)))

    def arrived(self):
        for cp in self.near:
            cp.wait_recv()

    def drained(self):
        for cp in self.far + self.near:
            cp.wait_send()
            self.net.drop(cp)

    def rows(self, sl):
        total = self.ploc[3, sl, :].astype(F32) + self.rc[3, sl, :].astype(F32)
        for j in range(2):
            total += self.ry[j, sl, :].astype(F32)
        return total


def norm_back(u, g, gain):
    r = rms_unit(u)
    unit = u * r
    gvec = g * gain
    return r * (gvec - unit * jnp.mean(gvec * unit, -1, keepdims=True))


class Scatter:
    def __init__(self, net, part, thru, r1, r2, loc=None):
        self.net, self.part, self.thru, self.r1, self.r2, self.loc = net, part, thru, r1, r2, loc

    def block(self, h, s):
        p, net = self.part, self.net
        if h == 0:
            zz = lax.rem(net.z + s, 4)
            return lambda lo, hi: p.at[0, zz, lo:hi]
        xx = lax.rem(net.x + s, 4)
        return lambda lo, hi: p.at[1, lo:hi, xx]

    def stage_one(self):
        net, r1, thru = self.net, self.r1, self.thru
        self.got, self.lc, self.add = [], [], []
        for h in range(2):
            to = net.zp if h == 0 else net.xp
            far, up, down, own = (self.block(h, s) for s in (2, 1, 3, 0))
            self.got.append([
                net.put(far(0, 2), thru.at[h, 0], to(1)), net.put(far(2, 4), thru.at[h, 1], to(3)),
                net.put(up(2, 4), r1.at[h, 0, 2:4], to(1)), net.put(down(0, 2), r1.at[h, 1, 0:2], to(3)),
            ])
            if self.loc is None:
                self.lc.append([])
                self.add.append((up(0, 2), down(2, 4), own(0, 4)))
            else:
                l = self.loc
                self.add.append((l.at[h, 0:2], l.at[h, 2:4], l.at[h, 4:8]))
                self.lc.append([net.copy(f, t) for f, t in zip((up(0, 2), down(2, 4), own(0, 4)), self.add[h])])

    def stage_mid(self):
        net, r1, thru = self.net, self.r1, self.thru
        self.more = []
        for h in range(2):
            to = net.zp if h == 0 else net.xp
            for cp in self.lc[h]:
                cp.wait()
            for k, s in enumerate((1, 3)):
                self.got[h][k].wait_recv()
                add_blocks(thru.at[h, k], [thru.at[h, k], self.add[h][k]], 2)
                self.more.append(net.put(thru.at[h, k], r1.at[h, k, 2 * k : 2 * k + 2], to(s)))

    def stage_two(self):
        net, r1, r2 = self.net, self.r1, self.r2
        self.nxt = []
        for h in range(2):
            for cp in self.got[h][2:] + self.more[2 * h : 2 * h + 2]:
                cp.wait_recv()
            add_blocks(r1.at[h, 0], [self.add[h][2], r1.at[h, 0], r1.at[h, 1]], 4)
            me = net.x if h == 0 else net.z
            self.nxt.append([
                net.put(r1.at[h, 0, lax.rem(me + s, 4)], r2.at[h, k], net.xp(s) if h == 0 else net.zp(s))
                for k, s in enumerate(ORDER)
            ])

    def stage_y(self, dst):
        net, r1, r2 = self.net, self.r1, self.r2
        for h in range(2):
            for cp in self.nxt[h]:
                cp.wait_recv()
            me = net.x if h == 0 else net.z
            add_to(r2.at[h, 0], [r1.at[h, 0, me]] + [r2.at[h, k] for k in range(3)], 64)
        self.yc = net.put(r2.at[1 - net.a, 0], dst, net.flip(1, 0))


def weight_grads(left, pairs, chunk, stage, csem, ssem):
    n = len(pairs)

    def load(i, k):
        sl = pl.ds(pl.multiple_of(i * 256, 256), 256)
        return pltpu.make_async_copy(left.at[:, sl], chunk.at[k], csem.at[k])

    def save(i, w, k):
        return pltpu.make_async_copy(stage.at[k], pairs[w][1].at[lax.div(i, 4), lax.rem(i, 4)], ssem.at[k])

    for i in range(3):
        load(i, i).start()

    @pl.loop(0, 2)
    def _(j):
        for k in range(4):
            i = 4 * j + k
            load(i, k).wait()
            if k == 0:
                load(i + 3, 3).start()
            else:

                @pl.when(j < 1)
                def _():
                    load(i + 3, k - 1).start()

            for w in range(n):
                slot = n * (k % 2) + w
                if k > 1:
                    save(i - 2, w, slot).wait()
                else:

                    @pl.when(j > 0)
                    def _():
                        save(i - 2, w, slot).wait()

                stage[slot] = dot(chunk[k], pairs[w][0][...], TN).reshape(4, 64, FH).astype(BF)
                save(i, w, slot).start()

    for i in (6, 7):
        for w in range(n):
            save(i, w, n * (i % 2) + w).wait()


SOON = ("hid", "dgate", "dup")
LATE = SOON + ("xn", "q", "kv4", "att", "wq", "wo", "cos", "sin", "bias", "tok", "w_q", "w_k", "w_v", "w_g", "w_u")


def m3_body(names, *refs):
    r = dict(zip(names, refs))
    net = Net(r["send"], r["recv"], r["loc"])
    a, z, x, t, hi, c = net.a, net.z, net.x, net.t, net.hi, net.c
    diag = net.dev(hi=1 - net.hi, c=1 - net.c)
    net.greet(all_peers(net) + [diag])
    mid, cot, tok, gains = r["mid"], r["cot"], r["tok"], r["gains"]
    rows, d = cot.shape
    n = 4 * rows
    step = 32
    far, near = 1 - hi, hi
    sib, chip = net.sib(), net.flip(0, 1)
    bl, bc, bt, by = r["bl"], r["bc"], r["bt"], r["by"]
    late = [net.copy(r["h_" + k], r[k]) for k in LATE if k not in SOON]
    soon = [net.copy(r["h_" + k], r[k]) for k in SOON]
    back = Sum8(net, r["fback"], bl, bc, bt, by)
    bias = r["bias"]
    ffn = [Scatter(net, r["p" + k], r["t" + k], r["r1" + k], r["r2" + k], r["l" + k]) for k in "dgu"]
    work = (r["chunk"], r["stage"], r["csem"], r["ssem"])
    soon[0].wait()
    weight_grads(r["call"], [(r["hid"], r["pd"])], *work)
    back.send()
    ffn[0].stage_one()
    soon[1].wait()
    soon[2].wait()
    weight_grads(r["xf"], [(r["dgate"], r["pg"]), (r["dup"], r["pu"])], *work)
    back.mid()
    ffn[1].stage_one()
    ffn[2].stage_one()
    back.arrived()
    gm, gmid = r["gm"], r["gmid"]

    @pl.loop(0, rows // step)
    def _(i):
        sl = pl.ds(pl.multiple_of(i * step, step), step)
        g = back.rows(sl)
        m = cot[sl, :].astype(F32) + norm_back(mid[sl, :], g, gains[1:2, :])
        gmid[sl, :] = m
        gm[t, sl, :] = m.astype(BF)

    free = r["free"]
    for s in (1, 3):
        pl.semaphore_signal(free, inc=1, device_id=net.yp(s), device_id_type=MESH)
    mine = gm.at[t]
    mf = net.put(mine, mine, chip)
    ms = [net.put(mine, mine, sib)]
    ffn[0].stage_mid()
    ms[0].wait_recv()
    back.drained()
    fwd = Sum8(net, r["fout"], bl, bc, bt, by)
    pl.semaphore_wait(free, 2)
    mf.wait_recv()
    theirs = gm.at[far * 2 + c]
    ms.append(net.put(theirs, theirs, sib))
    fwd.send()
    ffn[1].stage_mid()
    ms[1].wait_recv()
    for cp in late:
        cp.wait()
    gatt, att, q, kv4, wq, wo = r["gatt"], r["att"], r["q"], r["kv4"], r["wq"], r["wo"]
    for i in range(2):
        w = wo[:, :, :, :, 256 * i : 256 * i + 256].reshape(d, 256)
        gatt[:, 256 * i : 256 * i + 256] = dot(gm[...].reshape(n, d), w).astype(BF)
    po, pq, xn, dqkv = r["po"], r["pq"], r["xn"], r["dqkv"]

    @pl.loop(0, 8)
    def _(i):
        ln = pl.ds(pl.multiple_of(i * 256, 256), 256)
        left = gm[:, :, ln].reshape(n, 256)
        po[lax.div(i, 4), lax.rem(i, 4)] = dot(left, att[...], TN).reshape(4, 64, 512).astype(BF)

    so = Scatter(net, po, r["to"], r["r1o"], r["r2o"])
    so.stage_one()
    ffn[2].stage_mid()
    ak, av = r["ak"], r["av"]
    ak[...] = jnp.zeros_like(ak)
    av[...] = jnp.zeros_like(av)
    cos, sin = r["cos"], r["sin"]
    low = low_half((n, 128))
    scale = 1.0 / math.sqrt(HD)

    def pair(j):
        ln = pl.ds(pl.multiple_of(j * 128, 128), 128)
        qp, gp = q[:, ln], gatt[:, ln]
        cv, ck, gq = [], [], None
        for h in range(2):
            s = dot(kv4[h], qp, NT) + bias[...]
            e = jnp.exp(s - jnp.max(s, 0, keepdims=True))
            p = e * (1.0 / jnp.sum(e, 0, keepdims=True))
            pg = p * dot(kv4[2 + h], gp, NT)
            graw = (pg - p * jnp.sum(pg, 0, keepdims=True)).astype(BF)
            cv.append(dot(p.astype(BF), gp))
            ck.append(dot(graw, qp))
            term = dot(kv4[h], graw, TN)
            gq = term if gq is None else gq + term
        av[...] += jnp.where(low, cv[0], cv[1])
        ak[...] += jnp.where(low, ck[0], ck[1])
        dqkv[:, ln] = (rot_back(gq.T, cos[...], sin[...]) * scale).astype(BF)

    fwd.mid()
    ffn[0].stage_two()
    ffn[1].stage_two()
    pl.loop(0, 4)(pair)
    so.stage_mid()
    tk = ak[...] + pltpu.roll(ak[...], 64, 1)
    tv = av[...] + pltpu.roll(av[...], 64, 1)
    dqkv[:, 512:640] = jnp.where(low, rot_back(tk, cos[...], sin[...]), tv).astype(BF)


    def settle(i):
        o = r["y" + "dgu"[i]]
        ffn[i].stage_y(o.at[a])
        o[a] = ffn[i].r2[a, 0]

    ap, arc, arh = r["ap"], r["arc"], r["arh"]
    for i in range(4):
        w = wq[i // 2, 2 * (i % 2) : 2 * (i % 2) + 2].reshape(512, 640)
        ap[:, :, 512 * i : 512 * i + 512] = dot(dqkv[...], w, NT).reshape(4, rows, 512).astype(BF)
    acc = [net.put(ap.at[h * 2 + (1 - c)], arc.at[i], sib) for i, h in enumerate((far, near))]

    @pl.loop(0, 8)
    def _(i):
        ln = pl.ds(pl.multiple_of(i * 256, 256), 256)
        pq[lax.div(i, 4), lax.rem(i, 4)] = dot(xn[:, ln], dqkv[...], TN).reshape(4, 64, 640).astype(BF)

    sq = Scatter(net, pq, r["tq"], r["r1q"], r["r2q"])
    sq.stage_one()
    acc[0].wait_recv()
    af = ap.at[far * 2 + c]
    add_to(af, [af, arc.at[0]], rows)
    ach = net.put(af, arh, chip)
    ffn[2].stage_two()
    sq.stage_mid()
    so.stage_two()
    for i in range(3):
        settle(i)
    fwd.arrived()
    res, gtok = r["res"], r["gtok"]

    @pl.loop(0, rows // step)
    def _(i):
        sl = pl.ds(pl.multiple_of(i * step, step), step)
        g = fwd.rows(sl)
        res[sl, :] = (mid[sl, :] + g).astype(BF)

    dg = r["dg"]
    for sc in ffn:
        sc.yc.wait_recv()
    tot = jnp.zeros((64, 128), F32)
    for k in "gu":
        y, w = r["y" + k], r["w_" + k]
        for i in range(w.shape[1] // 128):
            lo, half = 128 * i % FH, 128 * i // FH
            tot += y[half, :, lo : lo + 128].astype(F32) * w[:, 128 * i : 128 * i + 128].astype(F32)
    dg[1] = tot
    sq.stage_two()
    so.stage_y(r["yo"])
    acc[1].wait_recv()
    ach.wait_recv()
    an = ap.at[near * 2 + c]

    @pl.loop(0, rows // step)
    def _(i):
        sl = pl.ds(pl.multiple_of(i * step, step), step)
        g = an[sl, :].astype(F32) + arc[1, sl, :].astype(F32) + arh[sl, :].astype(F32)
        gtok[sl, :] = (gmid[sl, :] + norm_back(tok[sl, :].astype(F32), g, gains[0:1, :])).astype(BF)

    sq.stage_y(r["yq"])
    so.yc.wait_recv()
    add_to(r["oo"], [so.r2.at[a, 0], r["yo"]], 64)
    sq.yc.wait_recv()
    dw = sq.r2[a, 0].astype(F32) + r["yq"][...].astype(F32)
    nq = r["oq"].shape[1]
    dk, dv = dw[:, nq : nq + HD], dw[:, nq + HD :]
    r["oq"][...] = dw[:, :nq]
    r["ok"][...] = dk
    r["ov"][...] = dv
    tot = jnp.zeros((64, 128), F32)
    for i in range(nq // 128):
        sl = slice(128 * i, 128 * i + 128)
        tot += dw[:, sl] * r["w_q"][:, sl].astype(F32)
    small = dk * r["w_k"][...].astype(F32) + dv * r["w_v"][...].astype(F32)
    dg[0] = tot + jnp.concatenate([small, jnp.zeros_like(small)], 1)
    dy = r["dy"]
    sums = [net.put(dg, dy.at[at], peer) for at, peer in enumerate((sib, chip, diag))]
    for cp in sums:
        cp.wait_recv()
    for i, (o, g) in enumerate((("dg1", "g_a"), ("dg2", "g_f"))):
        r[o][...] = jnp.sum((dg[i] + dy[0, i] + dy[1, i] + dy[2, i]).T, 0, keepdims=True) / r[g][...].astype(F32)
    net.finish()


def m3(hbm, vmem, shapes):
    rows, d = shapes
    n = 4 * rows
    sd = jax.ShapeDtypeStruct
    v = pltpu.VMEM
    part = (2, 4, 4, 64, FH)
    outs = dict(
        yg=sd((2, 64, FH), BF), yu=sd((2, 64, FH), BF), yd=sd((2, 64, FH), BF), oo=sd((64, 512), F32),
        oq=sd((64, 512), F32), ok=sd((64, HD), F32), ov=sd((64, HD), F32),
        res=sd((rows, d), BF), gtok=sd((rows, d), BF), dg1=sd((1, 64), F32), dg2=sd((1, 64), F32),
        pg=sd(part, BF), pu=sd(part, BF), pd=sd(part, BF),
    )
    scr = dict(
        bl=v((4, rows, d), BF), bc=v((4, rows, d), BF), by=v((2, rows, d), BF), bt=v((2, rows // 2, d), BF),
        gm=v((4, rows, d), BF), gmid=v((rows, d), F32), gatt=v((n, 512), BF),
        dqkv=v((n, 640), BF), ak=v((n, 128), F32), av=v((n, 128), F32),
        po=v((2, 4, 4, 64, 512), BF), pq=v((2, 4, 4, 64, 640), BF),
        ap=v((4, rows, d), BF), arc=v((2, rows, d), BF), arh=v((rows, d), BF),
        yo=v((64, 512), BF), yq=v((64, 640), BF), dg=v((2, 64, 128), F32), dy=v((3, 2, 64, 128), F32),
        chunk=v((4, 2 * n, 256), BF), stage=v((4, 4, 64, FH), BF),
        csem=pltpu.SemaphoreType.DMA((4,)), ssem=pltpu.SemaphoreType.DMA((4,)), free=pltpu.SemaphoreType.REGULAR,
    )
    for k, w in (("g", FH), ("u", FH), ("d", FH), ("o", 512), ("q", 640)):
        scr["t" + k] = v((2, 2, 2, 64, w), BF)
        scr["r1" + k] = v((2, 2, 4, 64, w), BF)
        scr["r2" + k] = v((2, 3, 64, w), BF)
    for k in "gud":
        scr["l" + k] = v((2, 8, 64, FH), BF)
    sem = sems(132, 56)
    for k in LATE:
        u = vmem.pop(k)
        hbm["h_" + k] = u
        scr[k] = v(u.shape, u.dtype)
    names = list(hbm) + list(vmem) + list(outs) + list(scr) + ["send", "recv", "loc"]
    got = pl.pallas_call(
        functools.partial(m3_body, names),
        out_shape=list(outs.values()),
        in_specs=[ANY] * len(hbm) + [VM] * len(vmem),
        out_specs=[VM] * (len(outs) - 3) + [ANY] * 3,
        scratch_shapes=list(scr.values()) + sem,
        compiler_params=pltpu.CompilerParams(collective_id=3, has_side_effects=True, vmem_limit_bytes=62 << 20),
        name="attention_backward",
    )(*hbm.values(), *vmem.values())
    return dict(zip(outs, got))


def mm(l, r, dims=((1,), (0,))):
    return lax.dot_general(l, r, (dims, ((), ())), preferred_element_type=F32)


def final_body(yg, yu, yd, *refs):
    k = (len(refs) - 3) // 2
    for y, o in zip((yg, yu, yd), refs[k : k + 3]):
        rest = o.shape[1] - FH
        o[:, :FH] = y[0].astype(F32)
        o[:, FH:] = y[1, :, :rest].astype(F32)
    for i, o in zip(refs[:k], refs[k + 3 :]):
        o[...] = i[...]


def final(halves, others, ff):
    sd = jax.ShapeDtypeStruct
    return pl.pallas_call(
        final_body,
        out_shape=[sd((64, ff), F32)] * 3 + [sd(o.shape, o.dtype) for o in others],
        in_specs=[VM] * (3 + len(others)),
        out_specs=[VM] * (3 + len(others)),
        name="final",
    )(*halves, *others)


def per_device(
    tokens_in, cotangent, seq_ids, block_ids, positions, attn_gain, ffn_gain,
    w_query, w_key, w_value, w_out, w_gate, w_up, w_down,
):
    rows, d = tokens_in.shape
    n = seq_ids.shape[0]
    weights = (w_query, w_key, w_value, w_out.T, w_gate, w_up, w_down.T)
    g_a, g_f = attn_gain.reshape(1, -1), ffn_gain.reshape(1, -1)
    xf, mid, gains, xn, q, kv4, att, wqkv, wot, cos, sin, bias_t, cot, wg, wu, wdt = m1(
        tokens_in, cotangent, weights, g_a, g_f, seq_ids, block_ids, positions
    )
    cot = cot.reshape(2 * n, d)
    wg, wu, wdt = (w.reshape(d, FH) for w in (wg, wu, wdt))
    xf = xf.reshape(2 * n, d)
    gate = mm(xf, wg)
    up = mm(xf, wu)
    sig = jax.nn.sigmoid(gate)
    silu = gate * sig
    hid = (silu * up).astype(BF)
    gh = mm(cot, wdt)
    dgate = (gh * up * (sig * (1.0 + gate * (1.0 - sig)))).astype(BF)
    dup = (gh * silu).astype(BF)
    fback = (mm(dgate, wg, NT) + mm(dup, wu, NT)).astype(BF).reshape(2, 4, rows, d)
    fout = mm(hid, wdt, NT).astype(BF).reshape(2, 4, rows, d)
    out = m3(
        dict(fback=fback, fout=fout, xf=xf, call=cot),
        dict(
            hid=hid, dgate=dgate, dup=dup, mid=mid, cot=cotangent, tok=tokens_in, gains=gains, xn=xn, q=q, kv4=kv4,
            att=att, wq=wqkv, wo=wot, cos=cos, sin=sin, bias=bias_t,
            w_q=w_query, w_k=w_key, w_v=w_value, w_g=w_gate, w_u=w_up, g_a=g_a, g_f=g_f,
        ),
        (rows, d),
    )
    keep = ("res", "gtok", "dg1", "dg2", "oq", "ok", "ov", "oo")
    og, ou, od, res, gtok, dg1, dg2, oq, ok, ov, oo = final(
        [out[k] for k in ("yg", "yu", "yd")], [out[k] for k in keep], w_gate.shape[1]
    )
    return (res, gtok, dg1.reshape(-1), dg2.reshape(-1), oq, ok, ov, oo.T, og, ou, od.T)


def solution(mesh):
    both, dp, cols, rows = P(("dp", "tensor"), None), P("dp"), P("dp", "tensor"), P("tensor", "dp")
    return jax.shard_map(
        per_device,
        mesh=mesh,
        in_specs=(both, both, dp, dp, dp, dp, dp, cols, cols, cols, rows, cols, cols, rows),
        out_specs=(both, both, dp, dp, cols, cols, cols, rows, cols, cols, rows),
        check_vma=False,
    )
```

```python
import functools
import math

import jax
import jax.numpy as jnp
import numpy as np
from jax import lax
from jax.experimental import pallas as pl
from jax.experimental.pallas import tpu as pltpu
from jax.sharding import PartitionSpec as P

HD = 64
EPSILON = 1e-05
ROPE_BASE = 10000.0
MESH = pl.DeviceIdType.MESH
BF = jnp.bfloat16
F32 = jnp.float32
ANY = pl.BlockSpec(memory_space=pl.ANY)
VM = pl.BlockSpec(memory_space=pltpu.VMEM)
FH = 768


class Net:
    def __init__(self, send, recv, loc):
        self.send, self.recv, self.loc = send, recv, loc
        self.n = self.m = 0
        dp, t = lax.axis_index("dp"), lax.axis_index("tensor")
        self.a = lax.div(dp, 16)
        self.z = lax.rem(lax.div(dp, 4), 4)
        self.x = lax.rem(dp, 4)
        self.hi = lax.div(t, 2)
        self.c = lax.rem(t, 2)
        self.t = t
        self.sends = []

    def dev(self, a=None, z=None, x=None, hi=None, c=None):
        a = self.a if a is None else a
        z = self.z if z is None else z
        x = self.x if x is None else x
        hi = self.hi if hi is None else hi
        c = self.c if c is None else c
        return (a * 16 + z * 4 + x, hi * 2 + c)

    def xp(self, s):
        return self.dev(x=lax.rem(self.x + s, 4))

    def zp(self, s):
        return self.dev(z=lax.rem(self.z + s, 4))

    def first(self, s, own):
        k = self.a if own else 1 - self.a
        return self.dev(z=lax.rem(self.z + s * k, 4), x=lax.rem(self.x + s * (1 - k), 4))

    def flip(self, da, dh):
        return self.dev(a=1 - self.a if da else None, hi=1 - self.hi if dh else None)

    def ring(self, s):
        a, hi = self.a, self.hi
        k = a if s == 1 else 1 - a
        return (a, 1 - hi) if s == 2 else (1 - a, hi + k - 2 * hi * k)

    def yp(self, s):
        a, hi = self.ring(s)
        return self.dev(a=a, hi=hi)

    def sib(self):
        return self.dev(c=1 - self.c)

    def hello(self, peers):
        bar = pltpu.get_barrier_semaphore()
        for p in peers:
            pl.semaphore_signal(bar, inc=1, device_id=p, device_id_type=MESH)

    def met(self, peers):
        pl.semaphore_wait(pltpu.get_barrier_semaphore(), len(peers))

    def greet(self, peers):
        self.hello(peers)
        self.met(peers)

    def put(self, src, dst, dev):
        i = self.n
        self.n += 1
        cp = pltpu.make_async_remote_copy(
            src_ref=src, dst_ref=dst, send_sem=self.send.at[i], recv_sem=self.recv.at[i],
            device_id=dev, device_id_type=MESH,
        )
        cp.start()
        self.sends.append(cp)
        return cp

    def copy(self, src, dst):
        i = self.m
        self.m += 1
        cp = pltpu.make_async_copy(src, dst, self.loc.at[i])
        cp.start()
        return cp

    def drop(self, cp):
        self.sends = [s for s in self.sends if s is not cp]

    def finish(self):
        assert self.n <= self.send.shape[0] and self.m <= self.loc.shape[0]
        for cp in self.sends:
            cp.wait_send()


FLIP8 = ((1, 0), (1, 1), (0, 1))
ORDER = (1, 3, 2)


def sems(n, m):
    return [pltpu.SemaphoreType.DMA((n,)), pltpu.SemaphoreType.DMA((n,)), pltpu.SemaphoreType.DMA((m,))]


def all_peers(net):
    return (
        [net.xp(s) for s in ORDER]
        + [net.zp(s) for s in ORDER]
        + [net.sib()]
        + [net.flip(*f) for f in FLIP8]
    )


def rms_unit(u):
    return lax.rsqrt(jnp.mean(u * u, -1, keepdims=True) + EPSILON)


def add_to(dst, terms, rows, step=32):
    @pl.loop(0, rows // step)
    def _(i):
        sl = pl.ds(pl.multiple_of(i * step, step), step)
        total = terms[0][sl, :].astype(F32)
        for ref in terms[1:]:
            total += ref[sl, :].astype(F32)
        dst[sl, :] = total.astype(dst.dtype)


def dot(l, r, dims=((1,), (0,))):
    return lax.dot_general(l, r, (dims, ((), ())), preferred_element_type=F32)


NT = ((1,), (1,))
TN = ((0,), (0,))


def low_half(shape):
    return lax.broadcasted_iota(jnp.int32, shape, 1) < HD


def first_quarter(shape):
    lane = lax.broadcasted_iota(jnp.int32, shape, 1)
    return lax.rem(lane, HD) < HD // 2


def rot(u, cos, sin):
    near = jnp.where(first_quarter(u.shape), pltpu.roll(u, 96, 1), pltpu.roll(u, 32, 1))
    return u * cos + near * sin


def rot_back(w, cos, sin):
    y = w * sin
    near = jnp.where(first_quarter(w.shape), pltpu.roll(y, 96, 1), pltpu.roll(y, 32, 1))
    return w * cos + near


class Gather:
    def __init__(self, net, src, dst, half):
        self.net, self.dst = net, dst
        self.own = src.at[net.a] if half else src
        self.other = src.at[1 - net.a] if half else src
        self.here = dst.at[net.a, net.z, net.x]

    def local(self):
        self.lc = self.net.copy(self.own, self.here)

    def over_y(self):
        self.yc = self.net.put(self.other, self.here, self.net.flip(1, 0))

    def stage_own(self):
        self.st = [self.net.put(self.own, self.here, self.net.first(s, True)) for s in ORDER]

    def stage_other(self):
        net = self.net
        self.yc.wait_recv()
        there = self.dst.at[1 - net.a, net.z, net.x]
        self.st += [net.put(there, there, net.first(s, False)) for s in ORDER]

    def stage_two(self):
        net, dst = self.net, self.dst
        self.lc.wait()
        for cp in self.st:
            cp.wait_recv()
        z, x = net.z, net.x
        self.near = [
            (net.put(dst.at[0, z], dst.at[0, z], net.zp(s)), net.put(dst.at[1, :, x], dst.at[1, :, x], net.xp(s)))
            for s in (1, 3)
        ]

    def forward(self):
        net, dst = self.net, self.dst
        self.last = []
        for (cz, cx), s, lo in zip(self.near, (1, 3), (0, 2)):
            cz.wait_recv()
            blk = dst.at[0, lax.rem(net.z + 4 - s, 4), lo : lo + 2]
            self.last.append(net.put(blk, blk, net.zp(s)))
            cx.wait_recv()
            blk = dst.at[1, lo : lo + 2, lax.rem(net.x + 4 - s, 4)]
            self.last.append(net.put(blk, blk, net.xp(s)))

    def done(self):
        for cp in self.last:
            cp.wait_recv()


class Rows8:
    def __init__(self, net, mine, dst):
        self.net, self.dst, self.half = net, dst, mine.shape[0] // 2
        at = dst.at[net.a, net.t]
        self.up, self.down = net.put(mine, at, net.yp(1)), net.put(mine, at, net.yp(3))
        self.side = [net.put(mine, at, net.sib())]

    def at(self, s):
        a, hi = self.net.ring(s)
        return self.dst.at[a, hi * 2 + self.net.c]

    def forward(self):
        net, h = self.net, self.half
        self.last = []
        for cp, src, to, lo in ((self.up, 3, 1, 0), (self.down, 1, 3, h)):
            cp.wait_recv()
            blk = self.at(src)
            part = blk.at[lo : lo + h]
            self.last.append(net.put(part, part, net.yp(to)))
            self.side.append(net.put(blk, blk, net.sib()))

    def finish(self):
        for cp in self.last:
            cp.wait_recv()
        blk = self.at(2)
        self.side.append(self.net.put(blk, blk, self.net.sib()))

    def done(self):
        for cp in self.side:
            cp.wait_recv()


def pack_halves(dst, w):
    rest = w.shape[1] - FH
    dst[0] = w[:, :FH]
    dst[1, :, :rest] = w[:, FH:]
    dst[1, :, rest:] = jnp.zeros((w.shape[0], FH - rest), BF)


def column(row, n):
    return jnp.broadcast_to(row, (128, n)).T


def m1_body(
    tok, cot, w_q, w_k, w_v, wo, w_g, w_u, w_d, g_a, g_f, freq, seqr, blkr, posr,
    xf, mid, gains, h_xn, h_q, h_kv4, h_att, h_aq, h_ao, h_cos, h_sin, h_bias_t, cot_all, ag, au, ad,
    xn, q, kv4, att, aq, ao, cos, sin, bias_t, wq, wf, gn, tall, an, bias, ones2, part, rc, rh, send, recv, loc,
):
    net = Net(send, recv, loc)
    a, z, x, t, hi, c = net.a, net.z, net.x, net.t, net.hi, net.c
    rows, d = tok.shape
    n = 4 * rows
    nq = w_q.shape[1]
    net.hello(all_peers(net))
    lane = lax.broadcasted_iota(jnp.int32, (1, 128), 1)
    here = lax.div(lane, HD) == lax.rem(x, 2)
    gn[...] = jnp.zeros_like(gn)
    for i, g in enumerate((g_a, g_f)):
        g = g[...].astype(F32)
        gn[i : i + 1, :] = jnp.where(here, jnp.concatenate([g, g], 1), 0.0)
    wq[:, :nq] = w_q[...]
    wq[:, nq : nq + HD] = w_k[...]
    wq[:, nq + HD :] = w_v[...]
    net.met(all_peers(net))
    far, near = 1 - hi, hi
    tt = far * 2 + c
    sib, chip = net.sib(), net.flip(0, 1)
    tl = net.copy(tok, tall.at[t])
    tf = net.put(tok, tall.at[t], chip)
    ts = [net.put(tok, tall.at[t], sib)]
    gg, gq, go = Gather(net, gn, an, False), Gather(net, wq, aq, False), Gather(net, wo, ao, False)
    for g in (gg, gq, go):
        g.over_y()
        g.local()
        g.stage_own()
    cl = net.copy(cot, cot_all.at[a, t])
    for i, w in enumerate((w_g, w_u, w_d)):
        pack_halves(wf.at[i], w)
    ffn = [Gather(net, wf.at[i], o, True) for i, o in enumerate((ag, au, ad))]
    for g in ffn:
        g.local()
    for g in (gg, gq, go):
        g.stage_other()
    seq, blk = seqr[...].astype(F32), blkr[...].astype(F32)
    same = column(seq, n)[:, :1] == seq
    blkc = column(blk, n)[:, :1]
    bias[...] = jnp.where(same & (blk <= blkc), jnp.float32(0.0), jnp.float32(-1e30))
    bias_t[...] = jnp.where(same & (blkc <= blk), jnp.float32(0.0), jnp.float32(-1e30))
    for g in (gg, gq, go):
        g.stage_two()
    tf.wait_recv()
    ts.append(net.put(tall.at[tt], tall.at[tt], sib))
    for g in ffn:
        g.over_y()
    cots = Rows8(net, cot, cot_all)
    angles = column(posr[...].astype(F32), n) * freq[...]
    cos[...] = jnp.cos(angles)
    sine = jnp.sin(angles)
    sin[...] = jnp.where(first_quarter(sine.shape), -sine, sine)
    tl.wait()
    for cp in ts:
        cp.wait_recv()
    gg.forward()
    gq.forward()
    out = [net.copy(*p) for p in ((bias_t, h_bias_t), (cos, h_cos), (sin, h_sin))]
    gg.done()
    for i in range(16):
        k = 2 * i
        pair = an[k // 16, k // 4 % 4, k % 4] + an[k // 16, k // 4 % 4, k % 4 + 1]
        gains[:, 128 * i : 128 * i + 128] = pair
    step = 32

    @pl.loop(0, n // step)
    def _(i):
        b = lax.div(i, rows // step)
        u = tall[b, pl.ds(pl.multiple_of(lax.rem(i, rows // step) * step, step), step), :].astype(F32)
        xn[pl.ds(pl.multiple_of(i * step, step), step), :] = (u * rms_unit(u) * gains[0:1, :]).astype(BF)

    go.forward()
    gq.done()
    for g in ffn:
        g.stage_own()
    scale = 1.0 / math.sqrt(HD)
    for lo, width in ((0, 256), (256, 256), (512, 128)):
        w = aq[:, :, :, :, lo : lo + width].reshape(d, width)
        val = dot(xn[...], w)
        if lo < 512:
            for i in range(2):
                at = lo + 128 * i
                q[:, at : at + 128] = (rot(val[:, 128 * i : 128 * i + 128], cos[...], sin[...]) * scale).astype(BF)
        else:
            low = low_half(val.shape)
            ke = jnp.where(low, rot(val, cos[...], sin[...]), 0.0)
            vo = jnp.where(low, 0.0, val)
            ve = pltpu.roll(vo, 64, 1)
            kv4[0] = ke.astype(BF)
            kv4[1] = pltpu.roll(ke, 64, 1).astype(BF)
            kv4[2] = ve.astype(BF)
            kv4[3] = vo.astype(BF)
            ones2[0] = jnp.where(low, ve, 1.0).astype(BF)
            ones2[1] = jnp.where(low, 1.0, vo).astype(BF)
    for g in ffn:
        g.stage_other()

    @pl.loop(0, 4)
    def _(j):
        ln = pl.ds(pl.multiple_of(j * 128, 128), 128)
        qp = q[:, ln]
        low = low_half((n, 128))
        o = []
        for h in range(2):
            s = dot(qp, kv4[h], NT) + bias[...]
            e = jnp.exp(s - jnp.max(s, -1, keepdims=True)).astype(BF)
            o.append(dot(e, ones2[h]))
        total = jnp.where(low, pltpu.roll(o[0], 64, 1), pltpu.roll(o[1], 64, 1))
        att[:, ln] = (jnp.where(low, o[0], o[1]) / total).astype(BF)

    go.done()
    for i in range(4):
        w = ao[i // 2, 2 * (i % 2) : 2 * (i % 2) + 2].reshape(512, 512)
        part[:, :, 512 * i : 512 * i + 512] = dot(att[...], w, NT).reshape(4, rows, 512).astype(BF)
    out += [
        net.copy(*p)
        for p in ((xn, h_xn), (q, h_q), (kv4, h_kv4), (att, h_att), (aq, h_aq), (ao, h_ao))
    ]
    cc = [net.put(part.at[h * 2 + (1 - c)], rc.at[i], sib) for i, h in enumerate((far, near))]
    for g in ffn:
        g.stage_two()
    cc[0].wait_recv()
    pf = part.at[far * 2 + c]
    add_to(pf, [pf, rc.at[0]], rows)
    ch = net.put(pf, rh, chip)
    cots.forward()
    cc[1].wait_recv()
    ch.wait_recv()
    ffn[0].forward()
    mine_part = part.at[near * 2 + c]

    @pl.loop(0, rows // step)
    def _(i):
        sl = pl.ds(pl.multiple_of(i * step, step), step)
        m = (
            tall[t, sl, :].astype(F32)
            + (mine_part[sl, :].astype(F32) + rc[1, sl, :].astype(F32))
            + rh[sl, :].astype(F32)
        )
        mid[sl, :] = m
        xf[a, t, sl, :] = (m * rms_unit(m) * gains[1:2, :]).astype(BF)

    mine = xf.at[a, t]
    rows8 = Rows8(net, mine, xf)
    cots.finish()
    ffn[1].forward()
    rows8.forward()
    ffn[2].forward()
    rows8.finish()
    for cp in [cl] + out:
        cp.wait()
    for g in ffn:
        g.done()
    cots.done()
    rows8.done()
    net.finish()


def m1(tok, cot, weights, g_a, g_f, seq, blk, pos):
    rows, d = tok.shape
    n = 4 * rows
    sd = jax.ShapeDtypeStruct
    v = pltpu.VMEM
    row = lambda u: u.reshape(1, n)
    freq = 1.0 / ROPE_BASE ** (np.arange(HD // 2, dtype=np.float32) * 2.0 / HD)
    freq = jnp.asarray(np.tile(freq, 4)[None], F32)
    ffn = [sd((2, 4, 4, 64, FH), BF)] * 3
    kept = [
        ((n, d), BF), ((n, 512), BF), ((4, n, 128), BF), ((n, 512), BF), ((2, 4, 4, 64, 640), BF),
        ((2, 4, 4, 64, 512), BF), ((n, 128), F32), ((n, 128), F32), ((n, n), F32),
    ]
    return pl.pallas_call(
        m1_body,
        out_shape=[sd((2, 4, rows, d), BF), sd((rows, d), F32), sd((8, d), F32)]
        + [sd(*k) for k in kept] + [sd((2, 4, rows, d), BF)] + ffn,
        in_specs=[ANY] + [VM] * 14,
        out_specs=[VM] * 3 + [ANY] * 13,
        scratch_shapes=[v(*k) for k in kept] + [
            v((64, 640), BF), v((3, 2, 64, FH), BF), v((8, 128), F32),
            v((4, rows, d), BF), v((2, 4, 4, 8, 128), F32), v((n, n), F32),
            v((2, n, 128), BF), v((4, rows, d), BF), v((2, rows, d), BF), v((rows, d), BF),
        ] + sems(124, 24),
        compiler_params=pltpu.CompilerParams(collective_id=1, has_side_effects=True, vmem_limit_bytes=56 << 20),
        name="attention_forward",
    )(tok, cot, *weights, g_a, g_f, freq, row(seq), row(blk), row(pos))


def add_blocks(dst, terms, blocks):
    @pl.loop(0, blocks)
    def _(b):
        total = terms[0][b].astype(F32)
        for ref in terms[1:]:
            total += ref[b].astype(F32)
        dst[b] = total.astype(dst.dtype)


class Sum8:
    def __init__(self, net, part, ploc, rc, thru, ry):
        self.net, self.ploc, self.rc, self.thru, self.ry = net, ploc, rc, thru, ry
        c = net.c
        chips = [net.ring(s) for s in (2, 1, 3)] + [(net.a, net.hi)]
        self.cc = [net.put(part.at[b, h * 2 + (1 - c)], rc.at[i], net.sib()) for i, (b, h) in enumerate(chips)]
        self.lc = [net.copy(part.at[b, h * 2 + c], ploc.at[i]) for i, (b, h) in enumerate(chips)]

    def send(self):
        net, ploc, thru, ry = self.net, self.ploc, self.thru, self.ry
        rows = ploc.shape[1]
        h = rows // 2

        def ready(i):
            self.lc[i].wait()
            self.cc[i].wait_recv()
            if i < 3:
                add_to(ploc.at[i], [ploc.at[i], self.rc.at[i]], rows)

        ready(0)
        self.far = [
            net.put(ploc.at[0, 0:h], thru.at[0], net.yp(1)), net.put(ploc.at[0, h:rows], thru.at[1], net.yp(3)),
        ]
        ready(1)
        self.near = [net.put(ploc.at[1, h:rows], ry.at[0, h:rows], net.yp(1))]
        ready(2)
        self.near.append(net.put(ploc.at[2, 0:h], ry.at[1, 0:h], net.yp(3)))
        ready(3)

    def mid(self):
        net, ploc, thru, ry = self.net, self.ploc, self.thru, self.ry
        h = ploc.shape[1] // 2
        for k, (to, lo) in enumerate(((1, 0), (3, h))):
            self.far[k].wait_recv()
            part = ploc.at[1 + k, lo : lo + h]
            add_to(part, [part, thru.at[k]], h)
            self.near.append(net.put(part, ry.at[k, lo : lo + h], net.yp(to)))

    def arrived(self):
        for cp in self.near:
            cp.wait_recv()

    def drained(self):
        for cp in self.far + self.near:
            cp.wait_send()
            self.net.drop(cp)

    def rows(self, sl):
        total = self.ploc[3, sl, :].astype(F32) + self.rc[3, sl, :].astype(F32)
        for j in range(2):
            total += self.ry[j, sl, :].astype(F32)
        return total


def norm_back(u, g, gain):
    r = rms_unit(u)
    unit = u * r
    gvec = g * gain
    return r * (gvec - unit * jnp.mean(gvec * unit, -1, keepdims=True))


class Scatter:
    def __init__(self, net, part, thru, r1, r2, loc=None):
        self.net, self.part, self.thru, self.r1, self.r2, self.loc = net, part, thru, r1, r2, loc

    def block(self, h, s):
        p, net = self.part, self.net
        if h == 0:
            zz = lax.rem(net.z + s, 4)
            return lambda lo, hi: p.at[0, zz, lo:hi]
        xx = lax.rem(net.x + s, 4)
        return lambda lo, hi: p.at[1, lo:hi, xx]

    def stage_one(self):
        net, r1, thru = self.net, self.r1, self.thru
        self.got, self.lc, self.add = [], [], []
        for h in range(2):
            to = net.zp if h == 0 else net.xp
            far, up, down, own = (self.block(h, s) for s in (2, 1, 3, 0))
            self.got.append([
                net.put(far(0, 2), thru.at[h, 0], to(1)), net.put(far(2, 4), thru.at[h, 1], to(3)),
                net.put(up(2, 4), r1.at[h, 0, 2:4], to(1)), net.put(down(0, 2), r1.at[h, 1, 0:2], to(3)),
            ])
            if self.loc is None:
                self.lc.append([])
                self.add.append((up(0, 2), down(2, 4), own(0, 4)))
            else:
                l = self.loc
                self.add.append((l.at[h, 0:2], l.at[h, 2:4], l.at[h, 4:8]))
                self.lc.append([net.copy(f, t) for f, t in zip((up(0, 2), down(2, 4), own(0, 4)), self.add[h])])

    def stage_mid(self):
        net, r1, thru = self.net, self.r1, self.thru
        self.more = []
        for h in range(2):
            to = net.zp if h == 0 else net.xp
            for cp in self.lc[h]:
                cp.wait()
            for k, s in enumerate((1, 3)):
                self.got[h][k].wait_recv()
                add_blocks(thru.at[h, k], [thru.at[h, k], self.add[h][k]], 2)
                self.more.append(net.put(thru.at[h, k], r1.at[h, k, 2 * k : 2 * k + 2], to(s)))

    def stage_two(self):
        net, r1, r2 = self.net, self.r1, self.r2
        self.nxt = []
        for h in range(2):
            for cp in self.got[h][2:] + self.more[2 * h : 2 * h + 2]:
                cp.wait_recv()
            add_blocks(r1.at[h, 0], [self.add[h][2], r1.at[h, 0], r1.at[h, 1]], 4)
            me = net.x if h == 0 else net.z
            self.nxt.append([
                net.put(r1.at[h, 0, lax.rem(me + s, 4)], r2.at[h, k], net.xp(s) if h == 0 else net.zp(s))
                for k, s in enumerate(ORDER)
            ])

    def stage_y(self, dst):
        net, r1, r2 = self.net, self.r1, self.r2
        for h in range(2):
            for cp in self.nxt[h]:
                cp.wait_recv()
            me = net.x if h == 0 else net.z
            add_to(r2.at[h, 0], [r1.at[h, 0, me]] + [r2.at[h, k] for k in range(3)], 64)
        self.yc = net.put(r2.at[1 - net.a, 0], dst, net.flip(1, 0))


def weight_grads(left, pairs, chunk, stage, csem, ssem):
    n = len(pairs)

    def load(i, k):
        sl = pl.ds(pl.multiple_of(i * 256, 256), 256)
        return pltpu.make_async_copy(left.at[:, sl], chunk.at[k], csem.at[k])

    def save(i, w, k):
        return pltpu.make_async_copy(stage.at[k], pairs[w][1].at[lax.div(i, 4), lax.rem(i, 4)], ssem.at[k])

    for i in range(3):
        load(i, i).start()

    @pl.loop(0, 2)
    def _(j):
        for k in range(4):
            i = 4 * j + k
            load(i, k).wait()
            if k == 0:
                load(i + 3, 3).start()
            else:

                @pl.when(j < 1)
                def _():
                    load(i + 3, k - 1).start()

            for w in range(n):
                slot = n * (k % 2) + w
                if k > 1:
                    save(i - 2, w, slot).wait()
                else:

                    @pl.when(j > 0)
                    def _():
                        save(i - 2, w, slot).wait()

                stage[slot] = dot(chunk[k], pairs[w][0][...], TN).reshape(4, 64, FH).astype(BF)
                save(i, w, slot).start()

    for i in (6, 7):
        for w in range(n):
            save(i, w, n * (i % 2) + w).wait()


SOON = ("hid", "dgate", "dup", "cot", "mid")
LATE = SOON + ("xn", "q", "kv4", "att", "wq", "wo", "cos", "sin", "bias", "tok", "w_q", "w_k", "w_v", "w_g", "w_u")


def m3_body(names, *refs):
    r = dict(zip(names, refs))
    net = Net(r["send"], r["recv"], r["loc"])
    a, z, x, t, hi, c = net.a, net.z, net.x, net.t, net.hi, net.c
    diag = net.dev(hi=1 - net.hi, c=1 - net.c)
    net.greet(all_peers(net) + [diag])
    mid, cot, tok, gains = r["mid"], r["cot"], r["tok"], r["gains"]
    rows, d = cot.shape
    n = 4 * rows
    step = 32
    far, near = 1 - hi, hi
    sib, chip = net.sib(), net.flip(0, 1)
    bl, bc, bt, by = r["bl"], r["bc"], r["bt"], r["by"]
    late = [net.copy(r["h_" + k], r[k]) for k in LATE if k not in SOON]
    soon = [net.copy(r["h_" + k], r[k]) for k in SOON]
    back = Sum8(net, r["fback"], bl, bc, bt, by)
    bias = r["bias"]
    ffn = [Scatter(net, r["p" + k], r["t" + k], r["r1" + k], r["r2" + k], r["l" + k]) for k in "dgu"]
    work = (r["chunk"], r["stage"], r["csem"], r["ssem"])
    soon[0].wait()
    weight_grads(r["call"], [(r["hid"], r["pd"])], *work)
    back.send()
    ffn[0].stage_one()
    soon[1].wait()
    soon[2].wait()
    weight_grads(r["xf"], [(r["dgate"], r["pg"]), (r["dup"], r["pu"])], *work)
    back.mid()
    ffn[1].stage_one()
    ffn[2].stage_one()
    soon[3].wait()
    soon[4].wait()
    back.arrived()
    gm, gmid = r["gm"], r["gmid"]

    @pl.loop(0, rows // step)
    def _(i):
        sl = pl.ds(pl.multiple_of(i * step, step), step)
        g = back.rows(sl)
        m = cot[sl, :].astype(F32) + norm_back(mid[sl, :], g, gains[1:2, :])
        gmid[sl, :] = m
        gm[t, sl, :] = m.astype(BF)

    free = r["free"]
    for s in (1, 3):
        pl.semaphore_signal(free, inc=1, device_id=net.yp(s), device_id_type=MESH)
    mine = gm.at[t]
    mf = net.put(mine, mine, chip)
    ms = [net.put(mine, mine, sib)]
    ffn[0].stage_mid()
    ms[0].wait_recv()
    back.drained()
    fwd = Sum8(net, r["fout"], bl, bc, bt, by)
    pl.semaphore_wait(free, 2)
    mf.wait_recv()
    theirs = gm.at[far * 2 + c]
    ms.append(net.put(theirs, theirs, sib))
    fwd.send()
    ffn[1].stage_mid()
    ms[1].wait_recv()
    for cp in late:
        cp.wait()
    gatt, att, q, kv4, wq, wo = r["gatt"], r["att"], r["q"], r["kv4"], r["wq"], r["wo"]
    for i in range(2):
        w = wo[:, :, :, :, 256 * i : 256 * i + 256].reshape(d, 256)
        gatt[:, 256 * i : 256 * i + 256] = dot(gm[...].reshape(n, d), w).astype(BF)
    po, pq, xn, dqkv = r["po"], r["pq"], r["xn"], r["dqkv"]

    @pl.loop(0, 8)
    def _(i):
        ln = pl.ds(pl.multiple_of(i * 256, 256), 256)
        left = gm[:, :, ln].reshape(n, 256)
        po[lax.div(i, 4), lax.rem(i, 4)] = dot(left, att[...], TN).reshape(4, 64, 512).astype(BF)

    so = Scatter(net, po, r["to"], r["r1o"], r["r2o"])
    so.stage_one()
    ffn[2].stage_mid()
    ak, av = r["ak"], r["av"]
    ak[...] = jnp.zeros_like(ak)
    av[...] = jnp.zeros_like(av)
    cos, sin = r["cos"], r["sin"]
    low = low_half((n, 128))
    scale = 1.0 / math.sqrt(HD)

    def pair(j):
        ln = pl.ds(pl.multiple_of(j * 128, 128), 128)
        qp, gp = q[:, ln], gatt[:, ln]
        cv, ck, gq = [], [], None
        for h in range(2):
            s = dot(kv4[h], qp, NT) + bias[...]
            e = jnp.exp(s - jnp.max(s, 0, keepdims=True))
            p = e * (1.0 / jnp.sum(e, 0, keepdims=True))
            pg = p * dot(kv4[2 + h], gp, NT)
            graw = (pg - p * jnp.sum(pg, 0, keepdims=True)).astype(BF)
            cv.append(dot(p.astype(BF), gp))
            ck.append(dot(graw, qp))
            term = dot(kv4[h], graw, TN)
            gq = term if gq is None else gq + term
        av[...] += jnp.where(low, cv[0], cv[1])
        ak[...] += jnp.where(low, ck[0], ck[1])
        dqkv[:, ln] = (rot_back(gq.T, cos[...], sin[...]) * scale).astype(BF)

    fwd.mid()
    ffn[0].stage_two()
    ffn[1].stage_two()
    pl.loop(0, 4)(pair)
    so.stage_mid()
    tk = ak[...] + pltpu.roll(ak[...], 64, 1)
    tv = av[...] + pltpu.roll(av[...], 64, 1)
    dqkv[:, 512:640] = jnp.where(low, rot_back(tk, cos[...], sin[...]), tv).astype(BF)


    def settle(i):
        o = r["y" + "dgu"[i]]
        ffn[i].stage_y(o.at[a])
        o[a] = ffn[i].r2[a, 0]

    ap, arc, arh = r["ap"], r["arc"], r["arh"]
    for i in range(4):
        w = wq[i // 2, 2 * (i % 2) : 2 * (i % 2) + 2].reshape(512, 640)
        ap[:, :, 512 * i : 512 * i + 512] = dot(dqkv[...], w, NT).reshape(4, rows, 512).astype(BF)
    acc = [net.put(ap.at[h * 2 + (1 - c)], arc.at[i], sib) for i, h in enumerate((far, near))]

    @pl.loop(0, 8)
    def _(i):
        ln = pl.ds(pl.multiple_of(i * 256, 256), 256)
        pq[lax.div(i, 4), lax.rem(i, 4)] = dot(xn[:, ln], dqkv[...], TN).reshape(4, 64, 640).astype(BF)

    sq = Scatter(net, pq, r["tq"], r["r1q"], r["r2q"])
    sq.stage_one()
    acc[0].wait_recv()
    af = ap.at[far * 2 + c]
    add_to(af, [af, arc.at[0]], rows)
    ach = net.put(af, arh, chip)
    ffn[2].stage_two()
    sq.stage_mid()
    so.stage_two()
    for i in range(3):
        settle(i)
    fwd.arrived()
    res, gtok = r["res"], r["gtok"]

    @pl.loop(0, rows // step)
    def _(i):
        sl = pl.ds(pl.multiple_of(i * step, step), step)
        g = fwd.rows(sl)
        res[sl, :] = (mid[sl, :] + g).astype(BF)

    dg = r["dg"]
    for sc in ffn:
        sc.yc.wait_recv()
    tot = jnp.zeros((64, 128), F32)
    for k in "gu":
        y, w = r["y" + k], r["w_" + k]
        for i in range(w.shape[1] // 128):
            lo, half = 128 * i % FH, 128 * i // FH
            tot += y[half, :, lo : lo + 128].astype(F32) * w[:, 128 * i : 128 * i + 128].astype(F32)
    dg[1] = tot
    sq.stage_two()
    so.stage_y(r["yo"])
    acc[1].wait_recv()
    ach.wait_recv()
    an = ap.at[near * 2 + c]

    @pl.loop(0, rows // step)
    def _(i):
        sl = pl.ds(pl.multiple_of(i * step, step), step)
        g = an[sl, :].astype(F32) + arc[1, sl, :].astype(F32) + arh[sl, :].astype(F32)
        gtok[sl, :] = (gmid[sl, :] + norm_back(tok[sl, :].astype(F32), g, gains[0:1, :])).astype(BF)

    sq.stage_y(r["yq"])
    so.yc.wait_recv()
    add_to(r["oo"], [so.r2.at[a, 0], r["yo"]], 64)
    sq.yc.wait_recv()
    dw = sq.r2[a, 0].astype(F32) + r["yq"][...].astype(F32)
    nq = r["oq"].shape[1]
    dk, dv = dw[:, nq : nq + HD], dw[:, nq + HD :]
    r["oq"][...] = dw[:, :nq]
    r["ok"][...] = dk
    r["ov"][...] = dv
    tot = jnp.zeros((64, 128), F32)
    for i in range(nq // 128):
        sl = slice(128 * i, 128 * i + 128)
        tot += dw[:, sl] * r["w_q"][:, sl].astype(F32)
    small = dk * r["w_k"][...].astype(F32) + dv * r["w_v"][...].astype(F32)
    dg[0] = tot + jnp.concatenate([small, jnp.zeros_like(small)], 1)
    dy = r["dy"]
    sums = [net.put(dg, dy.at[at], peer) for at, peer in enumerate((sib, chip, diag))]
    for cp in sums:
        cp.wait_recv()
    for i, (o, g) in enumerate((("dg1", "g_a"), ("dg2", "g_f"))):
        r[o][...] = jnp.sum((dg[i] + dy[0, i] + dy[1, i] + dy[2, i]).T, 0, keepdims=True) / r[g][...].astype(F32)
    net.finish()


def m3(hbm, vmem, shapes):
    rows, d = shapes
    n = 4 * rows
    sd = jax.ShapeDtypeStruct
    v = pltpu.VMEM
    part = (2, 4, 4, 64, FH)
    outs = dict(
        yg=sd((2, 64, FH), BF), yu=sd((2, 64, FH), BF), yd=sd((2, 64, FH), BF), oo=sd((64, 512), F32),
        oq=sd((64, 512), F32), ok=sd((64, HD), F32), ov=sd((64, HD), F32),
        res=sd((rows, d), BF), gtok=sd((rows, d), BF), dg1=sd((1, 64), F32), dg2=sd((1, 64), F32),
        pg=sd(part, BF), pu=sd(part, BF), pd=sd(part, BF),
    )
    scr = dict(
        bl=v((4, rows, d), BF), bc=v((4, rows, d), BF), by=v((2, rows, d), BF), bt=v((2, rows // 2, d), BF),
        gm=v((4, rows, d), BF), gmid=v((rows, d), F32), gatt=v((n, 512), BF),
        dqkv=v((n, 640), BF), ak=v((n, 128), F32), av=v((n, 128), F32),
        po=v((2, 4, 4, 64, 512), BF), pq=v((2, 4, 4, 64, 640), BF),
        ap=v((4, rows, d), BF), arc=v((2, rows, d), BF), arh=v((rows, d), BF),
        yo=v((64, 512), BF), yq=v((64, 640), BF), dg=v((2, 64, 128), F32), dy=v((3, 2, 64, 128), F32),
        chunk=v((4, 2 * n, 256), BF), stage=v((4, 4, 64, FH), BF),
        csem=pltpu.SemaphoreType.DMA((4,)), ssem=pltpu.SemaphoreType.DMA((4,)), free=pltpu.SemaphoreType.REGULAR,
    )
    for k, w in (("g", FH), ("u", FH), ("d", FH), ("o", 512), ("q", 640)):
        scr["t" + k] = v((2, 2, 2, 64, w), BF)
        scr["r1" + k] = v((2, 2, 4, 64, w), BF)
        scr["r2" + k] = v((2, 3, 64, w), BF)
    for k in "gud":
        scr["l" + k] = v((2, 8, 64, FH), BF)
    sem = sems(132, 56)
    for k in LATE:
        u = vmem.pop(k)
        hbm["h_" + k] = u
        scr[k] = v(u.shape, u.dtype)
    names = list(hbm) + list(vmem) + list(outs) + list(scr) + ["send", "recv", "loc"]
    got = pl.pallas_call(
        functools.partial(m3_body, names),
        out_shape=list(outs.values()),
        in_specs=[ANY] * len(hbm) + [VM] * len(vmem),
        out_specs=[VM] * (len(outs) - 3) + [ANY] * 3,
        scratch_shapes=list(scr.values()) + sem,
        compiler_params=pltpu.CompilerParams(collective_id=3, has_side_effects=True, vmem_limit_bytes=62 << 20),
        name="attention_backward",
    )(*hbm.values(), *vmem.values())
    return dict(zip(outs, got))


def mm(l, r, dims=((1,), (0,))):
    return lax.dot_general(l, r, (dims, ((), ())), preferred_element_type=F32)


def final_body(yg, yu, yd, *refs):
    k = (len(refs) - 3) // 2
    for y, o in zip((yg, yu, yd), refs[k : k + 3]):
        rest = o.shape[1] - FH
        o[:, :FH] = y[0].astype(F32)
        o[:, FH:] = y[1, :, :rest].astype(F32)
    for i, o in zip(refs[:k], refs[k + 3 :]):
        o[...] = i[...]


def final(halves, others, ff):
    sd = jax.ShapeDtypeStruct
    return pl.pallas_call(
        final_body,
        out_shape=[sd((64, ff), F32)] * 3 + [sd(o.shape, o.dtype) for o in others],
        in_specs=[VM] * (3 + len(others)),
        out_specs=[VM] * (3 + len(others)),
        name="final",
    )(*halves, *others)


def per_device(
    tokens_in, cotangent, seq_ids, block_ids, positions, attn_gain, ffn_gain,
    w_query, w_key, w_value, w_out, w_gate, w_up, w_down,
):
    rows, d = tokens_in.shape
    n = seq_ids.shape[0]
    weights = (w_query, w_key, w_value, w_out.T, w_gate, w_up, w_down.T)
    g_a, g_f = attn_gain.reshape(1, -1), ffn_gain.reshape(1, -1)
    xf, mid, gains, xn, q, kv4, att, wqkv, wot, cos, sin, bias_t, cot, wg, wu, wdt = m1(
        tokens_in, cotangent, weights, g_a, g_f, seq_ids, block_ids, positions
    )
    cot = cot.reshape(2 * n, d)
    wg, wu, wdt = (w.reshape(d, FH) for w in (wg, wu, wdt))
    xf = xf.reshape(2 * n, d)
    gate = mm(xf, wg)
    up = mm(xf, wu)
    sig = jax.nn.sigmoid(gate)
    silu = gate * sig
    hid = (silu * up).astype(BF)
    gh = mm(cot, wdt)
    dgate = (gh * up * (sig * (1.0 + gate * (1.0 - sig)))).astype(BF)
    dup = (gh * silu).astype(BF)
    fback = (mm(dgate, wg, NT) + mm(dup, wu, NT)).astype(BF).reshape(2, 4, rows, d)
    fout = mm(hid, wdt, NT).astype(BF).reshape(2, 4, rows, d)
    out = m3(
        dict(fback=fback, fout=fout, xf=xf, call=cot),
        dict(
            hid=hid, dgate=dgate, dup=dup, mid=mid, cot=cotangent, tok=tokens_in, gains=gains, xn=xn, q=q, kv4=kv4,
            att=att, wq=wqkv, wo=wot, cos=cos, sin=sin, bias=bias_t,
            w_q=w_query, w_k=w_key, w_v=w_value, w_g=w_gate, w_u=w_up, g_a=g_a, g_f=g_f,
        ),
        (rows, d),
    )
    keep = ("res", "gtok", "dg1", "dg2", "oq", "ok", "ov", "oo")
    og, ou, od, res, gtok, dg1, dg2, oq, ok, ov, oo = final(
        [out[k] for k in ("yg", "yu", "yd")], [out[k] for k in keep], w_gate.shape[1]
    )
    return (res, gtok, dg1.reshape(-1), dg2.reshape(-1), oq, ok, ov, oo.T, og, ou, od.T)


def solution(mesh):
    both, dp, cols, rows = P(("dp", "tensor"), None), P("dp"), P("dp", "tensor"), P("tensor", "dp")
    return jax.shard_map(
        per_device,
        mesh=mesh,
        in_specs=(both, both, dp, dp, dp, dp, dp, cols, cols, cols, rows, cols, cols, rows),
        out_specs=(both, both, dp, dp, cols, cols, cols, rows, cols, cols, rows),
        check_vma=False,
    )
```
